256 devices in a mesh: gx: 8 (over y, z_hi), gy: 8 (over z_lo, core), gz: 4 (over x).
Axes of the slice: x: 4, y: 4, z: 8 (z_hi: 2, z_lo: 4; z = z_hi * 4 + z_lo), core: 2. Of those that a mesh axis runs over, the one named last changes fastest.
Arguments:
- right_side: float32 [3, 64, 64, 512], P(None, 'gx', 'gy', 'gz'), may hold values from -17 to 17
- phase_labels: int32 [32, 32, 256], P('gx', 'gy', 'gz'), may hold values from 0 to 7
- phase_moduli: float32 [8], replicated, may hold values from 0.03 to 0.3
- coarse_nodes: int32 [64, 64, 512], P('gx', 'gy', 'gz'), may hold values from 0 to 5
- coarse_inverse: float32 [9216, 9216], P(('gx', 'gy', 'gz')), as said below
Outputs:
- solution_field: float32 [3, 64, 64, 512], P(None, 'gx', 'gy', 'gz')
- residual: float32 [3, 64, 64, 512], P(None, 'gx', 'gy', 'gz')
The draws below stay inside these ranges and needn't reach their ends.
Inputs may be any that keep to these rules, and one draw needn't show every extreme that they name: `coarse_inverse`: symmetric.
All inputs are finite; a program needn't handle non-finite values.
Results may differ from the reference program's by a relative error of at most 0.0003.
Values sent between devices are 32-bit elements; how exact they have to be, the bound alone decides.
A program may use at most 64 MiB of HBM per device.

```python
import math
import jax
import jax.numpy as jnp
from jax import lax

CX = 8
CY = 8
CZ = 128
NPHASE = 8
NAGG = 6
SWEEPS = 4
ITERS = 2
NC = 9216
NX = 64
NY = 64
NZ = 512
N_GX = 8
N_GY = 8
N_GZ = 4


def draw_right_side(key, part):
    across_x = (jnp.arange(NX, dtype=jnp.float32) + 0.5) / NX
    ramp = (1.0 + 2.0 * across_x)[None, :, None, None]
    return jax.random.truncated_normal(key, -4.0, 4.0, (3, NX, NY, NZ), jnp.float32) * ramp


def draw_coarse_inverse(key, part):
    order = NC
    base = 0.3 * math.sqrt(NAGG / (CX * CY * CZ))
    spread = base / (4.0 * math.sqrt(order / 6.0))
    first_key, second_key = jax.random.split(key)
    noise = jax.random.uniform(first_key, (order, order), jnp.float32, -1.0, 1.0)
    symmetric = 0.5 * (noise + noise.T) * spread
    lifted = base * jax.random.uniform(second_key, (order,), jnp.float32, 1.0, 1.5)
    rows = jnp.arange(order)[:, None]
    cols = jnp.arange(order)[None, :]
    return jnp.where(rows == cols, lifted[:, None], symmetric)


def place_ends(result, stream_key, smallest, largest):
    longest = result.shape.index(max(result.shape))
    spots = []
    for shift in (0, 1):
        where = [jax.random.randint(jax.random.fold_in(stream_key, axis), (), 0, length) for axis, length in enumerate(result.shape)]
        where[longest] = (where[longest] + shift) % result.shape[longest]
        spots.append(tuple(where))
    return result.at[spots[0]].set(smallest).at[spots[1]].set(largest)


def setup_inputs(seed: int = 0) -> dict:
    splits = jax.random.split(jax.random.key(seed), 6)
    return {
        "right_side": draw_right_side(jax.random.fold_in(splits[5], 71), 0),
        "phase_labels": place_ends(jax.random.randint(splits[1], (NX // 2, NY // 2, NZ // 2), 0, NPHASE), jax.random.fold_in(splits[1], 1), 0, NPHASE - 1).astype(jnp.int32),
        "phase_moduli": jnp.clip(jnp.exp(jax.random.uniform(splits[2], (NPHASE,), jnp.float32, math.log(0.03), math.log(0.3))), 0.03, 0.3),
        "coarse_nodes": place_ends(jax.random.randint(splits[3], (NX, NY, NZ), 0, NAGG), jax.random.fold_in(splits[3], 1), 0, NAGG - 1).astype(jnp.int32),
        "coarse_inverse": draw_coarse_inverse(jax.random.fold_in(splits[5], 71), 0),
    }


bond_ratio = 0.5
relax = 0.6
highest = lax.Precision.HIGHEST
neighbour_offsets = tuple((shift_x, shift_y, shift_z) for shift_x in (-1, 0, 1) for shift_y in (-1, 0, 1) for shift_z in (-1, 0, 1) if shift_x * shift_x + shift_y * shift_y + shift_z * shift_z > 0)


def inner_view(array, shift_x, shift_y, shift_z):
    size_x, size_y, size_z = array.shape[-3:]
    return array[..., 1 + shift_x:size_x - 1 + shift_x, 1 + shift_y:size_y - 1 + shift_y, 1 + shift_z:size_z - 1 + shift_z]


def spring_force(field_pad, stiff_pad):
    centre = inner_view(field_pad, 0, 0, 0)
    stiff_centre = inner_view(stiff_pad, 0, 0, 0)
    parts = [jnp.zeros_like(centre[0]) for component in range(3)]
    for offset in neighbour_offsets:
        length = offset[0] * offset[0] + offset[1] * offset[1] + offset[2] * offset[2]
        spring = 0.5 * (stiff_centre + inner_view(stiff_pad, offset[0], offset[1], offset[2])) / length
        partner = inner_view(field_pad, offset[0], offset[1], offset[2])
        stretch = [centre[component] - partner[component] for component in range(3)]
        projected = jnp.zeros_like(stretch[0])
        for component in range(3):
            if offset[component] != 0:
                projected = projected + offset[component] * stretch[component]
        for component in range(3):
            summand = stretch[component]
            if offset[component] != 0:
                summand = summand + (bond_ratio * offset[component] / length) * projected
            parts[component] = parts[component] + spring * summand
    return jnp.stack(parts)


def diagonal(stiff_pad):
    stiff_centre = inner_view(stiff_pad, 0, 0, 0)
    parts = [jnp.zeros_like(stiff_centre) for component in range(3)]
    for offset in neighbour_offsets:
        length = offset[0] * offset[0] + offset[1] * offset[1] + offset[2] * offset[2]
        spring = 0.5 * (stiff_centre + inner_view(stiff_pad, offset[0], offset[1], offset[2])) / length
        for component in range(3):
            parts[component] = parts[component] + spring * (1.0 + bond_ratio * offset[component] * offset[component] / length)
    return jnp.stack(parts)


def local_solve(residual_ext, stiff_rim, diag_ext):
    widths = [(0, 0)] * (residual_ext.ndim - 3) + [(1, 1)] * 3
    solution = relax * residual_ext / diag_ext
    for sweep in range(SWEEPS - 1):
        solution = solution + relax * (residual_ext - spring_force(jnp.pad(solution, widths), stiff_rim)) / diag_ext
    return solution


def solve_members(members):
    return local_solve(members[0], members[1], members[2])


def cross(first, second):
    return jnp.stack([first[1] * second[2] - first[2] * second[1], first[2] * second[0] - first[0] * second[2], first[0] * second[1] - first[1] * second[0]])


def local_coords(size_x, size_y, size_z):
    along_x = ((2.0 * jnp.arange(size_x, dtype=jnp.float32) + 1.0) / size_x - 1.0).reshape(size_x, 1, 1)
    along_y = ((2.0 * jnp.arange(size_y, dtype=jnp.float32) + 1.0) / size_y - 1.0).reshape(1, size_y, 1)
    along_z = ((2.0 * jnp.arange(size_z, dtype=jnp.float32) + 1.0) / size_z - 1.0).reshape(1, 1, size_z)
    return (along_x, along_y, along_z)


def fold_blocks(extended, block_axis, local_axis):
    size = extended.shape[local_axis]
    count = size - 2
    blocks = extended.shape[block_axis]
    inner = lax.slice_in_dim(extended, 1, size - 1, axis=local_axis)
    lower = lax.slice_in_dim(extended, 0, 1, axis=local_axis)
    upper = lax.slice_in_dim(extended, size - 1, size, axis=local_axis)
    empty = jnp.zeros_like(lax.slice_in_dim(upper, 0, 1, axis=block_axis))
    from_below = jnp.concatenate([empty, lax.slice_in_dim(upper, 0, blocks - 1, axis=block_axis)], axis=block_axis)
    from_above = jnp.concatenate([lax.slice_in_dim(lower, 1, blocks, axis=block_axis), empty], axis=block_axis)
    head = lax.slice_in_dim(inner, 0, 1, axis=local_axis) + from_below
    tail = lax.slice_in_dim(inner, count - 1, count, axis=local_axis) + from_above
    middle = lax.slice_in_dim(inner, 1, count - 1, axis=local_axis)
    return jnp.concatenate([head, middle, tail], axis=local_axis)


def reference(right_side, phase_labels, phase_moduli, coarse_nodes, coarse_inverse):
    coarse_stiff = jnp.take(phase_moduli, phase_labels, axis=0)
    stiffness = jnp.repeat(jnp.repeat(jnp.repeat(coarse_stiff, 2, axis=0), 2, axis=1), 2, axis=2)

    def blocks(padded, width):
        lead = padded.ndim - 3
        index_x = jnp.arange(N_GX, dtype=jnp.int32)[:, None] * CX + jnp.arange(CX + 2 * width, dtype=jnp.int32)[None, :]
        index_y = jnp.arange(N_GY, dtype=jnp.int32)[:, None] * CY + jnp.arange(CY + 2 * width, dtype=jnp.int32)[None, :]
        index_z = jnp.arange(N_GZ, dtype=jnp.int32)[:, None] * CZ + jnp.arange(CZ + 2 * width, dtype=jnp.int32)[None, :]
        moved = jnp.take(padded, index_x, axis=lead)
        moved = jnp.take(moved, index_y, axis=lead + 2)
        moved = jnp.take(moved, index_z, axis=lead + 4)
        order = list(range(lead)) + [lead, lead + 2, lead + 4, lead + 1, lead + 3, lead + 5]
        return jnp.transpose(moved, order)

    block_count = N_GX * N_GY * N_GZ
    stiff_rim = blocks(jnp.pad(stiffness, 2), 2)
    stiff_flat = stiff_rim.reshape((block_count,) + stiff_rim.shape[3:])
    diag_flat = lax.map(diagonal, stiff_flat)
    stiff_pad = jnp.pad(stiffness, 1)
    node_blocks = coarse_nodes.reshape(N_GX, CX, N_GY, CY, N_GZ, CZ).transpose(0, 2, 4, 1, 3, 5)
    coords = local_coords(CX, CY, CZ)
    widths = ((0, 0), (1, 1), (1, 1), (1, 1))

    def precondition(residual):
        extended = blocks(jnp.pad(residual, widths), 1)
        ext_flat = jnp.moveaxis(extended.reshape((3, block_count) + extended.shape[4:]), 1, 0)
        solved_flat = lax.map(solve_members, (ext_flat, stiff_flat, diag_flat))
        solution = jnp.moveaxis(solved_flat, 0, 1).reshape(extended.shape)
        folded = fold_blocks(fold_blocks(fold_blocks(solution, 1, 4), 2, 5), 3, 6)
        pieces = residual.reshape(3, N_GX, CX, N_GY, CY, N_GZ, CZ).transpose(0, 1, 3, 5, 2, 4, 6)
        moments = jnp.concatenate([pieces, cross(coords, pieces)], axis=0)
        sums = jnp.stack([jnp.sum(jnp.where(node_blocks == node, moments, 0.0), axis=(4, 5, 6)) for node in range(NAGG)], axis=-1)
        coarse = jnp.transpose(sums, (1, 2, 3, 4, 0)).reshape(-1)
        solved = jnp.dot(coarse_inverse, coarse, precision=highest).reshape(N_GX, N_GY, N_GZ, NAGG, 6)
        solved_modes = jnp.transpose(solved, (4, 0, 1, 2, 3))
        per_cell = jnp.zeros_like(moments)
        for node in range(NAGG):
            per_cell = per_cell + jnp.where(node_blocks == node, solved_modes[..., node][..., None, None, None], 0.0)
        total = folded + per_cell[:3] + cross(per_cell[3:], coords)
        return total.transpose(0, 1, 4, 2, 5, 3, 6).reshape(3, N_GX * CX, N_GY * CY, N_GZ * CZ)

    def operate(vector):
        return spring_force(jnp.pad(vector, widths), stiff_pad)

    solution_field = jnp.zeros_like(right_side)
    residual = right_side
    search = precondition(residual)
    direction = search
    norm_now = jnp.sum(residual * search)
    for step in range(ITERS):
        image = operate(direction)
        step_size = norm_now / jnp.sum(direction * image)
        solution_field = solution_field + step_size * direction
        residual = residual - step_size * image
        if step + 1 < ITERS:
            search = precondition(residual)
            norm_next = jnp.sum(residual * search)
            direction = search + (norm_next / norm_now) * direction
            norm_now = norm_next
    return (solution_field, residual)
```

```python
import functools

import jax
import jax.numpy as jnp
import numpy as np
from jax import lax
from jax.experimental import pallas as pl
from jax.experimental.pallas import tpu as pltpu
from jax.sharding import PartitionSpec as P

MESH = pl.DeviceIdType.MESH
HIGH = lax.Precision.HIGHEST
F32 = jnp.float32

RELAX = 0.6
SWEEPS = 4
SIDE = 8
STRIDE = 11
LEAD = 8
ZH = 2
NODES = 6
MODES = 36


def bond(d):
    return d[0] * d[0] + d[1] * d[1] + d[2] * d[2]


def coef(m, k, d):
    n = bond(d)
    if n == 0:
        return 0.0
    return (1.0 / n if m == k else 0.0) + 0.5 * d[m] * d[k] / (n * n)


def plan(cz):
    rows = -(-(cz + 3) // 8) * 8
    srows = -(-(cz // 2 + 2) // 8) * 8
    total = -(-(3 * rows + srows) // 80) * 80
    return rows, srows, total


def tables(cz):
    rows, srows, total = plan(cz)
    place = np.zeros((64, 128), np.float32)
    for i in range(SIDE):
        for j in range(SIDE):
            place[i * SIDE + j, STRIDE * (i + 1) + j + 1] = 1.0
    spot = {-1: 0, 0: 1, 1: 2, 2: 3, 3: 8, 4: 9}
    place_blocks = np.zeros((16, 128), np.float32)
    for i in range(4):
        for j in range(4):
            place_blocks[i * 4 + j, STRIDE * spot[i] + spot[j]] = 1.0

    def lane_of(x, y):
        return STRIDE * spot[x // 2] + spot[y // 2]

    grow = np.zeros((3 * rows, srows), np.float32)
    for r in range(cz + 2):
        z = r - 1
        grow[r, z // 2 + 1] += 1.0
        for dz in (-1, 1):
            grow[rows + r, (z + dz) // 2 + 1] += 1.0
            grow[2 * rows + r, (z + dz) // 2 + 1] += dz
    pairs = ((0, 0), (1, 1), (2, 2), (0, 1), (0, 2), (1, 2))
    w0 = np.zeros((128, 5 * 128))
    ws = np.zeros((128, 4 * 128))
    wd = np.zeros((128, 2 * 128))
    for x in range(-1, 9):
        for y in range(-1, 9):
            out = STRIDE * (x + 1) + y + 1
            w0[lane_of(x, y), out] += 1.0
            for at, (m, k) in enumerate(pairs):
                if at < 3:
                    whole = sum(
                        coef(m, k, (a, b, c)) for a in (-1, 0, 1) for b in (-1, 0, 1) for c in (-1, 0, 1)
                    )
                    w0[lane_of(x, y), 128 * (at + 1) + out] += 0.5 * whole
                for a in (-1, 0, 1):
                    for b in (-1, 0, 1):
                        src = lane_of(x + a, y + b)
                        if at < 4:
                            w0[src, 128 * (at + 1) + out] += 0.5 * coef(m, k, (a, b, 0))
                            ws[src, 128 * at + out] += 0.5 * coef(m, k, (a, b, 1))
                        else:
                            wd[src, 128 * (at - 4) + out] += 0.5 * coef(m, k, (a, b, 1))
    lane = np.arange(128)
    ints = np.zeros((24, 128), np.int32)
    ints[0:8] = np.where(lane < 110, lane // STRIDE, 99)
    ints[8:16] = np.where(lane < 110, lane % STRIDE, 99)
    ints[16:24] = np.where(lane < 126, lane // 21, 99)
    floats = np.zeros((16, 128), np.float32)
    floats[0:8] = (2.0 * (lane // STRIDE - 1) + 1.0) / SIDE - 1.0
    floats[8:16] = (2.0 * (lane % STRIDE - 1) + 1.0) / SIDE - 1.0
    as32 = lambda a: jnp.asarray(a, F32)
    return (
        as32(place),
        as32(place_blocks),
        as32(grow),
        as32(w0),
        as32(ws),
        as32(wd),
        jnp.asarray(ints),
        as32(floats),
    )


def turn(x, shift):
    shift = shift % 128
    return x if shift == 0 else pltpu.roll(x, shift, 1)


def add_all(items):
    items = list(items)
    while len(items) > 1:
        items = [
            items[i] + items[i + 1] if i + 1 < len(items) else items[i] for i in range(0, len(items), 2)
        ]
    return items[0]


def kernel(
    sizes,
    cz,
    rhs,
    labels,
    moduli,
    nodes_in,
    inverse,
    place,
    place_blocks,
    grow,
    w0,
    ws,
    wd,
    ints,
    floats,
    sol_out,
    res_out,
    mat,
    field,
    zfield,
    qfield,
    rfield,
    pfield,
    vf,
    wf,
    syv,
    dyv,
    syw,
    dyw,
    dmat,
    stiff,
    cdiag,
    node,
    gridm,
    stage,
    rowm,
    ybuf,
    cvec,
    zsend,
    zrecv,
    ysend,
    yrecv,
    xsend,
    xrecv,
    gmsg,
    g1,
    g1c,
    g2,
    mat_sem,
    halo_ss,
    halo_rs,
    g1_ss,
    g1_rs,
    g2_ss,
    g2_rs,
):
    ngx, ngy, ngz = sizes
    rows, srows, total = plan(cz)
    tiles = rows // 8
    sbase = LEAD + 3 * rows
    gx, gy, gz = lax.axis_index("gx"), lax.axis_index("gy"), lax.axis_index("gz")
    zhi, yhi = lax.rem(gx, ZH), lax.div(gx, ZH)
    nline = ZH * ngy
    nplane = (ngx // ZH) * ngz
    slot1 = zhi * ngy + gy
    slot2 = yhi * ngz + gz

    def line_peer(step):
        other = lax.rem(slot1 + step, nline)
        return (yhi * ZH + lax.div(other, ngy), lax.rem(other, ngy), gz)

    def plane_peer(step):
        other = lax.rem(slot2 + step, nplane)
        return (lax.div(other, ngz) * ZH + zhi, gy, lax.rem(other, ngz))

    sides = (
        (gz > 0, (gx, gy, gz - 1)),
        (gz < ngz - 1, (gx, gy, gz + 1)),
        (gy > 0, (gx, gy - 1, gz)),
        (gy < ngy - 1, (gx, gy + 1, gz)),
        (gx > 0, (gx - 1, gy, gz)),
        (gx < ngx - 1, (gx + 1, gy, gz)),
    )

    barrier = pltpu.get_barrier_semaphore()
    for has, device in sides:

        @pl.when(has)
        def _(device=device):
            pl.semaphore_signal(barrier, inc=1, device_id=device, device_id_type=MESH)

    for step in range(1, nline):
        pl.semaphore_signal(barrier, inc=1, device_id=line_peer(step), device_id_type=MESH)
    for step in range(1, nplane):
        pl.semaphore_signal(barrier, inc=1, device_id=plane_peer(step), device_id_type=MESH)

    mat_copy = pltpu.make_async_copy(inverse, mat, mat_sem)
    mat_copy.start()

    lane_x, lane_y, lane_c = ints[0:8, :], ints[8:16, :], ints[16:24, :]
    lane = lax.broadcasted_iota(jnp.int32, (8, 128), 1)
    sub = lax.broadcasted_iota(jnp.int32, (8, 128), 0)
    xi_x, xi_y = floats[0:8, :], floats[8:16, :]

    def base_of(k, i):
        return pl.multiple_of(LEAD + k * rows + 8 * i, 8)

    def xi_z(i):
        along = (sub + (8 * i - 1)).astype(F32)
        return (2.0 * along + 1.0) / cz - 1.0

    for ref in (field, zfield, qfield, rfield, pfield):
        ref[...] = jnp.zeros(ref.shape, F32)
    for ref in (vf, wf, syv, dyv, syw, dyw):
        ref[0:LEAD, :] = jnp.zeros((LEAD, 128), F32)
        ref[LEAD + 3 * rows : LEAD + 3 * rows + 8, :] = jnp.zeros((8, 128), F32)
    node[...] = jnp.zeros(node.shape, F32)
    rowm[...] = jnp.zeros(rowm.shape, F32)
    zsend[...] = jnp.zeros(zsend.shape, F32)
    cvec[...] = jnp.zeros(cvec.shape, F32)
    stage[...] = jnp.zeros(stage.shape, F32)
    for side, (has, _) in enumerate(sides):

        @pl.when(jnp.logical_not(has))
        def _(side=side):
            ref = (zrecv, yrecv, xrecv)[side // 2]
            for t in range(4):
                ref[t, side % 2] = jnp.zeros(ref.shape[2:], F32)

    def across(a, b):
        return lax.dot_general(a, b, (((0,), (0,)), ((), ())), precision=HIGH, preferred_element_type=F32)

    def times(a, b):
        return lax.dot_general(a, b, (((1,), (0,)), ((), ())), precision=HIGH, preferred_element_type=F32)

    def times_t(a, b):
        return lax.dot_general(a, b, (((1,), (1,)), ((), ())), precision=HIGH, preferred_element_type=F32)

    for k in range(3):
        piece = across(rhs[64 * k : 64 * k + 64, :], place[...])
        first = LEAD + k * rows + 1
        field[first : first + cz, :] = piece
        rfield[first : first + cz, :] = piece
    node[1 : 1 + cz, :] = across(nodes_in[...].astype(F32) + 1.0, place[...])
    for i in range(4):
        lab = labels[i]
        value = jnp.zeros(lab.shape, F32)
        for phase in range(moduli.shape[0]):
            value = jnp.where(lab == phase, moduli[phase], value)
        stage[4 * i : 4 * i + 4, :] = value
    blocks = across(stage[...], place_blocks[...])
    field[sbase + 1 : sbase + 1 + cz // 2, :] = blocks

    bad_lane = (
        ((gx == 0) & (lane_x == 0))
        | ((gx == ngx - 1) & (lane_x == 9))
        | ((gy == 0) & (lane_y == 0))
        | ((gy == ngy - 1) & (lane_y == 9))
        | (lane_x > 9)
        | (lane_y > 9)
    )
    low = jnp.where(gz == 0, 1, 0)
    high = jnp.where(gz == ngz - 1, cz + 1, cz + 2)

    def grid_tile(i, carry):
        r = sub + 8 * i
        gridm[pl.ds(pl.multiple_of(8 * i, 8), 8), :] = jnp.where(bad_lane | (r < low) | (r >= high), 0.0, 1.0)
        return carry

    lax.fori_loop(0, tiles, grid_tile, 0)

    def halo(which, side, ref_s, ref_r):
        return pltpu.make_async_remote_copy(
            src_ref=ref_s.at[which, side % 2],
            dst_ref=ref_r.at[which, 1 - side % 2],
            send_sem=halo_ss.at[which, side],
            recv_sem=halo_rs.at[which, side + 1 - 2 * (side % 2)],
            device_id=sides[side][1],
            device_id_type=MESH,
        )

    def start(which, axis, ref_s, ref_r):
        for side in (2 * axis, 2 * axis + 1):

            @pl.when(sides[side][0])
            def _(side=side):
                halo(which, side, ref_s, ref_r).start()

    def arrive(which, axis, ref_s, ref_r):
        for side in (2 * axis, 2 * axis + 1):

            @pl.when(sides[side][0])
            def _(side=side):
                pltpu.make_async_remote_copy(
                    src_ref=ref_s.at[which, side % 2],
                    dst_ref=ref_r.at[which, side % 2],
                    send_sem=halo_ss.at[which, side],
                    recv_sem=halo_rs.at[which, side],
                    device_id=sides[side][1],
                    device_id_type=MESH,
                ).wait_recv()

    def left(which, axis, ref_s, ref_r):
        for side in (2 * axis, 2 * axis + 1):

            @pl.when(sides[side][0])
            def _(side=side):
                halo(which, side, ref_s, ref_r).wait_send()

    def z_rows(width):
        if width == 1:
            got = [(LEAD + k * rows, cz, k) for k in range(3)] + [(sbase, cz // 2, 3)]
            return [(r + n, r + 1, r, r + n + 1, at) for r, n, at in got]
        out = []
        for k in range(3):
            for layer in range(2):
                r = LEAD + k * rows + layer
                out.append((r + cz, r, r, r + cz, 2 * k + layer))
        return out

    def pack_z(ref, which, width):
        for up_from, down_from, _, _, at in z_rows(width):
            zsend[which, 0, at : at + 1, :] = ref[down_from : down_from + 1, :]
            zsend[which, 1, at : at + 1, :] = ref[up_from : up_from + 1, :]

    def unpack_z(ref, which, width):
        for _, _, low_to, high_to, at in z_rows(width):
            ref[low_to : low_to + 1, :] += zrecv[which, 0, at : at + 1, :]
            ref[high_to : high_to + 1, :] += zrecv[which, 1, at : at + 1, :]

    def scheme(axis, width):
        if width == 1:
            if axis == 1:
                return 10, total // 80, lambda k: lane_y == k, lambda k: (k - 1, k - 8), (lane_y == 0, lane_y == 9), lambda k: (-k, 9 - k)
            return (
                10,
                total // 80,
                lambda k: lane_x == k,
                lambda k: (STRIDE * (k - 1), STRIDE * (k - 8)),
                (lane_x == 0, lane_x == 9),
                lambda k: (-STRIDE * k, STRIDE * (9 - k)),
            )
        if axis == 1:
            return (
                5,
                -(-3 * rows // 40),
                lambda k: (lane_y == 2 * k) | (lane_y == 2 * k + 1),
                lambda k: (2 * k, 2 * k - 8),
                (lane_y < 2, (lane_y == 8) | (lane_y == 9)),
                lambda k: (-2 * k, 8 - 2 * k),
            )
        return (
            6,
            -(-3 * rows // 48),
            lambda k: lane_c == k,
            lambda k: (21 * k, 21 * k - 88),
            (lane < 21, (lane >= 88) & (lane < 109)),
            lambda k: (-21 * k, 88 - 21 * k),
        )

    def pack(ref, which, axis, width, buf):
        chunks, deep, mask, shift, _, _ = scheme(axis, width)
        masks = [mask(k) for k in range(chunks)]

        def one(t, carry):
            down, up = jnp.zeros((8, 128), F32), jnp.zeros((8, 128), F32)
            for k in range(chunks):
                tile = ref[pl.ds(pl.multiple_of(LEAD + 8 * (k * deep + t), 8), 8), :]
                down = jnp.where(masks[k], turn(tile, shift(k)[0]), down)
                up = jnp.where(masks[k], turn(tile, shift(k)[1]), up)
            at = pl.ds(pl.multiple_of(8 * t, 8), 8)
            buf[which, 0, at, :] = down
            buf[which, 1, at, :] = up
            return carry

        lax.fori_loop(0, deep, one, 0)

    def unpack(ref, which, axis, width, buf):
        chunks, deep, _, _, ends, shift = scheme(axis, width)

        def one(t, carry):
            at = pl.ds(pl.multiple_of(8 * t, 8), 8)
            from_low, from_high = buf[which, 0, at, :], buf[which, 1, at, :]
            for k in range(chunks):
                rows_k = pl.ds(pl.multiple_of(LEAD + 8 * (k * deep + t), 8), 8)
                tile = ref[rows_k, :]
                tile = tile + jnp.where(ends[0], turn(from_low, shift(k)[0]), 0.0)
                tile = tile + jnp.where(ends[1], turn(from_high, shift(k)[1]), 0.0)
                ref[rows_k, :] = tile
            return carry

        lax.fori_loop(0, deep, one, 0)

    def cut(ref, axis, width):
        deep = 8 * scheme(axis, width)[1]
        return ref.at[:, :, 0:deep, :]

    def exchange(ref, which, width, between=None):
        pack_z(ref, which, width)
        start(which, 0, zsend, zrecv)
        arrive(which, 0, zsend, zrecv)
        unpack_z(ref, which, width)
        pack(ref, which, 1, width, ysend)
        start(which, 1, cut(ysend, 1, width), cut(yrecv, 1, width))
        arrive(which, 1, cut(ysend, 1, width), cut(yrecv, 1, width))
        unpack(ref, which, 1, width, yrecv)
        pack(ref, which, 2, width, xsend)
        start(which, 2, cut(xsend, 2, width), cut(xrecv, 2, width))
        if between is not None:
            between()
        arrive(which, 2, cut(xsend, 2, width), cut(xrecv, 2, width))
        unpack(ref, which, 2, width, xrecv)

    def line_copy(which, step):
        return pltpu.make_async_remote_copy(
            src_ref=gmsg.at[which, pl.ds(0, 1)],
            dst_ref=g1.at[which, pl.ds(slot1, 1)],
            send_sem=g1_ss.at[which, step],
            recv_sem=g1_rs.at[which, slot1],
            device_id=line_peer(step),
            device_id_type=MESH,
        )

    def line_start(which, message):
        gmsg[which] = message
        g1[which, pl.ds(slot1, 1), :] = message[0:1, :]
        for step in range(1, nline):
            line_copy(which, step).start()

    def line_arrive(which):
        for step in range(1, nline):
            other = lax.rem(slot1 + step, nline)
            pltpu.make_async_remote_copy(
                src_ref=gmsg.at[which, pl.ds(0, 1)],
                dst_ref=g1.at[which, pl.ds(other, 1)],
                send_sem=g1_ss.at[which, step],
                recv_sem=g1_rs.at[which, other],
                device_id=line_peer(step),
                device_id_type=MESH,
            ).wait_recv()

    def plane_copy(which, step):
        return pltpu.make_async_remote_copy(
            src_ref=g1c.at[which],
            dst_ref=g2.at[which, slot2],
            send_sem=g2_ss.at[which, step],
            recv_sem=g2_rs.at[which, slot2],
            device_id=plane_peer(step),
            device_id_type=MESH,
        )

    def plane_start(which, block):
        g1c[which] = block
        g2[which, pl.ds(slot2, 1)] = block[None]
        for step in range(1, nplane):
            plane_copy(which, step).start()

    def plane_arrive(which):
        for step in range(1, nplane):
            other = lax.rem(slot2 + step, nplane)
            pltpu.make_async_remote_copy(
                src_ref=g1c.at[which],
                dst_ref=g2.at[which, other],
                send_sem=g2_ss.at[which, step],
                recv_sem=g2_rs.at[which, other],
                device_id=plane_peer(step),
                device_id_type=MESH,
            ).wait_recv()

    def moments(ref):
        def one(i, acc):
            r = [ref[pl.ds(base_of(k, i), 8), :] for k in range(3)]
            own = node[pl.ds(pl.multiple_of(8 * i, 8), 8), :]
            z = xi_z(i)
            parts = r + [xi_y * r[2] - z * r[1], z * r[0] - xi_x * r[2], xi_x * r[1] - xi_y * r[0]]
            out = []
            for g in range(NODES):
                here = own == float(g + 1)
                for m in range(6):
                    out.append(acc[6 * g + m] + jnp.where(here, parts[m], 0.0))
            return tuple(out)

        acc = lax.fori_loop(0, tiles, one, tuple(jnp.zeros((8, 128), F32) for _ in range(MODES)))
        for at in range(MODES):
            rowm[at : at + 1, :] = jnp.sum(acc[at], axis=0, keepdims=True)

    def row_to_lanes():
        return times_t(jnp.ones((8, 128), F32), rowm[...])

    turned = lax.rem((gy * ngz + gz) * MODES, 128)

    def own_range(c):
        begin = (sub * ngz + c) * MODES - 128 * sub
        ahead = begin < 128
        first = (lane >= begin) & (lane < begin + MODES)
        second = (lane + 128 >= begin) & (lane + 128 < begin + MODES)
        return first, second

    def coarse_solve(which):
        ranges = [own_range(c) for c in range(ngz)]
        acc = [jnp.zeros((8, 128), F32) for _ in range(5)]
        for y in range(ngx // ZH):
            for h in range(ZH):
                a = y * ZH + h
                got = [g2[which, y * ngz + c, 8 * h : 8 * h + 8, :] for c in range(ngz)]
                main = add_all([jnp.where(ranges[c][0], got[c], 0.0) for c in range(ngz)])
                nxt = add_all([jnp.where(ranges[c][1], got[c], 0.0) for c in range(ngz)])
                cvec[16 * a + 8 : 16 * a + 9, :] = jnp.zeros((1, 128), F32)
                cvec[16 * a : 16 * a + 8, :] = main
                cvec[16 * a + 1 : 16 * a + 9, :] += nxt
        for a in range(ngx):
            for j in range(9):
                row = jnp.broadcast_to(cvec[16 * a + j : 16 * a + j + 1, :], (8, 128))
                col = 128 * (9 * a + j)
                for t in range(4):
                    acc[t] = acc[t] + mat[8 * t : 8 * t + 8, col : col + 128] * row
                acc[4] = acc[4] + jnp.concatenate([mat[32:36, col : col + 128]] * 2, axis=0) * row
        for t in range(5):
            ybuf[8 * t : 8 * t + 8, :] = jnp.broadcast_to(jnp.sum(acc[t], axis=1, keepdims=True), (8, 128))

    def lane_sum(which, at):
        parts = []
        for c in range(ngz):
            pos = lax.rem((sub * ngz + c) * MODES + at, 128)
            here = lane == pos
            for y in range(ngx // ZH):
                for h in range(ZH):
                    parts.append(jnp.where(here, g2[which, y * ngz + c, 8 * h : 8 * h + 8, :], 0.0))
        whole = jnp.sum(add_all(parts), axis=0, keepdims=True)
        return jnp.sum(whole, axis=1, keepdims=True)

    def with_coarse(src, dst):
        def one(i, carry):
            own = node[pl.ds(pl.multiple_of(8 * i, 8), 8), :]
            grid = gridm[pl.ds(pl.multiple_of(8 * i, 8), 8), :]
            z = xi_z(i)
            modes = [jnp.zeros((8, 128), F32) for _ in range(6)]
            for g in range(NODES):
                here = own == float(g + 1)
                for m in range(6):
                    at = 6 * g + m
                    modes[m] = jnp.where(here, jnp.broadcast_to(ybuf[at : at + 1, :], (8, 128)), modes[m])
            t, w = modes[:3], modes[3:]
            add = [
                t[0] + (w[1] * z - w[2] * xi_y),
                t[1] + (w[2] * xi_x - w[0] * z),
                t[2] + (w[0] * xi_y - w[1] * xi_x),
            ]
            for k in range(3):
                at = pl.ds(base_of(k, i), 8)
                dst[at, :] = src[at, :] * grid + add[k]
            return carry

        lax.fori_loop(0, tiles, one, 0)

    def spread(ref):
        def one(i, carry):
            s = stiff[pl.ds(pl.multiple_of(8 * i, 8), 8), :]
            for k in range(3):
                at = pl.ds(base_of(k, i), 8)
                v = ref[at, :]
                w = s * v
                vf[at, :] = v
                wf[at, :] = w
                for x, sy, dy in ((v, syv, dyv), (w, syw, dyw)):
                    ahead, behind = turn(x, -1), turn(x, 1)
                    sy[at, :] = ahead + behind
                    dy[at, :] = ahead - behind
            return carry

        lax.fori_loop(0, tiles, one, 0)

    def couple(u_ref, sy_ref, dy_ref, i):
        def at(ref, k, dz):
            return ref[pl.ds(base_of(k, i) + dz, 8), :]

        up = [at(u_ref, k, 1) for k in range(3)]
        um = [at(u_ref, k, -1) for k in range(3)]
        u = [at(u_ref, k, 0) for k in range(3)]
        s = [up[k] + um[k] for k in range(3)]
        yp = [at(sy_ref, k, 1) for k in range(3)]
        ym = [at(sy_ref, k, -1) for k in range(3)]
        sy = [at(sy_ref, k, 0) for k in range(3)]
        sys = [yp[k] + ym[k] for k in range(3)]
        t_x, t_z = up[0] - um[0], up[2] - um[2]
        ty_x, ty_z = yp[0] - ym[0], yp[2] - ym[2]
        dp = [at(dy_ref, k, 1) for k in range(3)]
        dm = [at(dy_ref, k, -1) for k in range(3)]
        dys_x, dys_y = dp[0] + dm[0], dp[1] + dm[1]
        dyt_y, dyt_z = dp[1] - dm[1], dp[2] - dm[2]
        dy_x, dy_y = at(dy_ref, 0, 0), at(dy_ref, 1, 0)
        e, th, c7 = 0.125, 1.0 / 18.0, 7.0 / 18.0
        still = [
            sy[0] + s[0] + 0.5 * sys[0],
            1.5 * sy[1] + s[1] + 0.625 * sys[1] + e * dyt_z,
            sy[2] + 1.5 * s[2] + 0.625 * sys[2] + e * dyt_y,
        ]
        even = [
            1.5 * u[0] + 0.625 * (sy[0] + s[0]) + c7 * sys[0],
            u[1] + 0.625 * sy[1] + 0.5 * s[1] + c7 * sys[1] + th * dyt_z,
            u[2] + 0.5 * sy[2] + 0.625 * s[2] + c7 * sys[2] + th * dyt_y,
        ]
        odd = [
            e * (dy_y + t_z) + th * (dys_y + ty_z),
            e * dy_x + th * dys_x,
            e * t_x + th * ty_x,
        ]
        return [
            still[k] + (turn(even[k] + odd[k], -STRIDE) + turn(even[k] - odd[k], STRIDE)) for k in range(3)
        ], u

    def image_tile(i):
        here = pl.ds(pl.multiple_of(8 * i, 8), 8)
        lv, v = couple(vf, syv, dyv, i)
        lw, _ = couple(wf, syw, dyw, i)
        s = stiff[here, :]
        d = [dmat[pl.ds(pl.multiple_of(rows * f + 8 * i, 8), 8), :] for f in range(6)]
        full = ((0, 3, 4), (3, 1, 5), (4, 5, 2))
        out = []
        for m in range(3):
            diag = d[full[m][0]] * v[0] + d[full[m][1]] * v[1] + d[full[m][2]] * v[2]
            out.append(diag - 0.5 * (s * lv[m] + lw[m]))
        return out, v

    def local_solve(ref, out):
        def first(i, carry):
            for k in range(3):
                at = pl.ds(base_of(k, i), 8)
                out[at, :] = cdiag[pl.ds(pl.multiple_of(rows * k + 8 * i, 8), 8), :] * ref[at, :]
            return carry

        lax.fori_loop(0, tiles, first, 0)

        def sweep(n, carry):
            spread(out)

            def one(i, inner):
                image, v = image_tile(i)
                for k in range(3):
                    at = pl.ds(base_of(k, i), 8)
                    c = cdiag[pl.ds(pl.multiple_of(rows * k + 8 * i, 8), 8), :]
                    out[at, :] = v[k] + c * (ref[at, :] - image[k])
                return inner

            lax.fori_loop(0, tiles, one, 0)
            return carry

        lax.fori_loop(0, SWEEPS - 1, sweep, 0)

    def setup_stiffness():
        blocks_all = field[sbase : sbase + srows, :]
        fine = times(grow[...], blocks_all)
        flat, both, tilt = fine[0:rows], fine[rows : 2 * rows], fine[2 * rows : 3 * rows]
        for f in range(7):
            total_f = None
            if f < 5:
                total_f = times(flat, w0[:, 128 * f : 128 * f + 128])
            if 1 <= f < 5:
                total_f = total_f + times(both, ws[:, 128 * (f - 1) : 128 * f])
            if f >= 5:
                total_f = times(tilt, wd[:, 128 * (f - 5) : 128 * (f - 4)])
            if f == 0:
                stiff[...] = total_f
            else:
                dmat[rows * (f - 1) : rows * f, :] = total_f
        r = lax.broadcasted_iota(jnp.int32, (rows, 128), 0)
        for k in range(3):
            d = dmat[rows * k : rows * k + rows, :]
            live = (r < cz + 2) & (d > 0.0)
            cdiag[rows * k : rows * k + rows, :] = jnp.where(live, RELAX / jnp.where(live, d, 1.0), 0.0)

    moments(field)
    first_row = turn_by(row_to_lanes(), turned)
    greeters = nline - 1 + nplane - 1
    for has, _ in sides:
        greeters = greeters + jnp.where(has, 1, 0)
    pl.semaphore_wait(barrier, greeters)

    def forward(which):
        def run():
            line_arrive(which)
            plane_start(which, g1[which])

        return run

    line_start(0, first_row)
    exchange(field, 0, 1, forward(0))
    setup_stiffness()
    local_solve(field, pfield)
    mat_copy.wait()
    plane_arrive(0)
    coarse_solve(0)
    with_coarse(pfield, zfield)
    exchange(zfield, 1, 2)

    spread(zfield)

    def image_and_sums(dst, first, second):
        def one(i, acc):
            image, v = image_tile(i)
            own = node[pl.ds(pl.multiple_of(8 * i, 8), 8), :] > 0.0
            acc = list(acc)
            for k in range(3):
                at = pl.ds(base_of(k, i), 8)
                mine = jnp.where(own, image[k], 0.0)
                dst[at, :] = mine
                acc[0] = acc[0] + first[at, :] * v[k]
                acc[1] = acc[1] + v[k] * mine
                if second is not None:
                    acc[2] = acc[2] + second[at, :] * v[k]
            return tuple(acc)

        count = 2 if second is None else 3
        acc = lax.fori_loop(0, tiles, one, tuple(jnp.zeros((8, 128), F32) for _ in range(count)))
        return [jnp.sum(a, axis=0, keepdims=True) for a in acc]

    sums = image_and_sums(qfield, rfield, None)
    moments(qfield)
    rowm[MODES : MODES + 1, :] = sums[0]
    rowm[MODES + 1 : MODES + 2, :] = sums[1]
    second_row = turn_by(row_to_lanes(), turned)

    line_start(1, second_row)
    for k in range(3):
        field[LEAD + rows * k : LEAD + rows * (k + 1), :] = qfield[LEAD + rows * k : LEAD + rows * (k + 1), :]
    exchange(field, 2, 1, forward(1))
    local_solve(field, pfield)
    plane_arrive(1)
    coarse_solve(1)
    rho0 = lane_sum(1, MODES)
    curve0 = lane_sum(1, MODES + 1)
    alpha0 = rho0 / curve0
    with_coarse(pfield, field)
    exchange(field, 3, 2)

    def renew(i, carry):
        for k in range(3):
            at = pl.ds(base_of(k, i), 8)
            field[at, :] = zfield[at, :] - alpha0 * field[at, :]
            rfield[at, :] = rfield[at, :] - alpha0 * qfield[at, :]
        return carry

    lax.fori_loop(0, tiles, renew, 0)
    spread(field)

    sums = image_and_sums(pfield, rfield, qfield)
    rowm[0:MODES, :] = jnp.zeros((MODES, 128), F32)
    for at in range(3):
        rowm[MODES + at : MODES + at + 1, :] = sums[at]
    line_start(2, turn_by(row_to_lanes(), turned))
    line_arrive(2)
    plane_start(2, g1[2])
    plane_arrive(2)
    rho1 = lane_sum(2, MODES)
    zaz = lane_sum(2, MODES + 1)
    zq = lane_sum(2, MODES + 2)
    beta = rho1 / rho0
    alpha1 = rho1 / (zaz + 2.0 * beta * zq + beta * beta * curve0)

    for k in range(3):
        at = slice(LEAD + k * rows + 1, LEAD + k * rows + 1 + cz)
        z0, z1 = zfield[at, :], field[at, :]
        sol_out[64 * k : 64 * k + 64, :] = times_t(place[...], alpha0 * z0 + alpha1 * (z1 + beta * z0))
        res_out[64 * k : 64 * k + 64, :] = times_t(
            place[...], rfield[at, :] - alpha1 * (pfield[at, :] + beta * qfield[at, :])
        )

    for which in range(4):
        width = 1 + which % 2
        left(which, 0, zsend, zrecv)
        left(which, 1, cut(ysend, 1, width), cut(yrecv, 1, width))
        left(which, 2, cut(xsend, 2, width), cut(xrecv, 2, width))
    for which in range(3):
        for step in range(1, nline):
            line_copy(which, step).wait_send()
        for step in range(1, nplane):
            plane_copy(which, step).wait_send()


def turn_by(x, shift):
    return pltpu.roll(x, shift, 1)


def solution(mesh):
    sizes = (mesh.shape["gx"], mesh.shape["gy"], mesh.shape["gz"])
    nline = ZH * sizes[1]
    nplane = (sizes[0] // ZH) * sizes[2]

    def body(right_side, phase_labels, phase_moduli, coarse_nodes, coarse_inverse):
        cz = right_side.shape[3]
        rows, srows, total = plan(cz)
        tall = pltpu.VMEM((LEAD + total, 128), F32)
        ydeep = max(total // 10, 8 * -(-3 * rows // 40))
        xdeep = max(total // 10, 8 * -(-3 * rows // 48))
        vmem = pl.BlockSpec(memory_space=pltpu.VMEM)
        consts = tables(cz)
        sol, res = pl.pallas_call(
            functools.partial(kernel, sizes, cz),
            out_shape=(jax.ShapeDtypeStruct((192, cz), F32),) * 2,
            in_specs=[
                vmem,
                vmem,
                pl.BlockSpec(memory_space=pltpu.SMEM),
                vmem,
                pl.BlockSpec(memory_space=pl.ANY),
            ]
            + [vmem] * len(consts),
            out_specs=(vmem, vmem),
            scratch_shapes=[
                pltpu.VMEM(coarse_inverse.shape, F32),
                tall,
                tall,
                tall,
                tall,
                tall,
                tall,
                tall,
                tall,
                tall,
                tall,
                tall,
                pltpu.VMEM((6 * rows, 128), F32),
                pltpu.VMEM((rows, 128), F32),
                pltpu.VMEM((3 * rows, 128), F32),
                pltpu.VMEM((rows, 128), F32),
                pltpu.VMEM((rows, 128), F32),
                pltpu.VMEM((16, cz // 2), F32),
                pltpu.VMEM((128, 128), F32),
                pltpu.VMEM((40, 128), F32),
                pltpu.VMEM((16 * sizes[0], 128), F32),
                pltpu.VMEM((4, 2, 8, 128), F32),
                pltpu.VMEM((4, 2, 8, 128), F32),
                pltpu.VMEM((4, 2, ydeep, 128), F32),
                pltpu.VMEM((4, 2, ydeep, 128), F32),
                pltpu.VMEM((4, 2, xdeep, 128), F32),
                pltpu.VMEM((4, 2, xdeep, 128), F32),
                pltpu.VMEM((3, 8, 128), F32),
                pltpu.VMEM((3, nline, 128), F32),
                pltpu.VMEM((3, nline, 128), F32),
                pltpu.VMEM((3, nplane, nline, 128), F32),
                pltpu.SemaphoreType.DMA,
                pltpu.SemaphoreType.DMA((4, 6)),
                pltpu.SemaphoreType.DMA((4, 6)),
                pltpu.SemaphoreType.DMA((3, nline)),
                pltpu.SemaphoreType.DMA((3, nline)),
                pltpu.SemaphoreType.DMA((3, nplane)),
                pltpu.SemaphoreType.DMA((3, nplane)),
            ],
            compiler_params=pltpu.CompilerParams(
                collective_id=0, has_side_effects=True, vmem_limit_bytes=48 * 1024 * 1024
            ),
            name="schwarz_cg",
        )(
            right_side.reshape(192, cz),
            phase_labels,
            phase_moduli,
            coarse_nodes.reshape(64, cz),
            coarse_inverse,
            *consts,
        )
        return sol.reshape(right_side.shape), res.reshape(right_side.shape)

    spec = P(None, "gx", "gy", "gz")
    cells = P("gx", "gy", "gz")
    return jax.shard_map(
        body,
        mesh=mesh,
        in_specs=(spec, cells, P(), cells, P(("gx", "gy", "gz"), None)),
        out_specs=(spec, spec),
        check_vma=False,
    )
```

```python
import functools

import jax
import jax.numpy as jnp
import numpy as np
from jax import lax
from jax.experimental import pallas as pl
from jax.experimental.pallas import tpu as pltpu
from jax.sharding import PartitionSpec as P

MESH = pl.DeviceIdType.MESH
HIGH = lax.Precision.HIGHEST
F32 = jnp.float32

RELAX = 0.6
SWEEPS = 4
SIDE = 8
STRIDE = 11
LEAD = 8
ZH = 2
NODES = 6
MODES = 36


def bond(d):
    return d[0] * d[0] + d[1] * d[1] + d[2] * d[2]


def coef(m, k, d):
    n = bond(d)
    if n == 0:
        return 0.0
    return (1.0 / n if m == k else 0.0) + 0.5 * d[m] * d[k] / (n * n)


def plan(cz):
    rows = -(-(cz + 3) // 8) * 8
    srows = -(-(cz // 2 + 2) // 8) * 8
    total = -(-(3 * rows + srows) // 80) * 80
    return rows, srows, total


def tables(cz):
    rows, srows, total = plan(cz)
    place = np.zeros((64, 128), np.float32)
    for i in range(SIDE):
        for j in range(SIDE):
            place[i * SIDE + j, STRIDE * (i + 1) + j + 1] = 1.0
    spot = {-1: 0, 0: 1, 1: 2, 2: 3, 3: 8, 4: 9}
    place_blocks = np.zeros((16, 128), np.float32)
    for i in range(4):
        for j in range(4):
            place_blocks[i * 4 + j, STRIDE * spot[i] + spot[j]] = 1.0

    def lane_of(x, y):
        return STRIDE * spot[x // 2] + spot[y // 2]

    pairs = ((0, 0), (1, 1), (2, 2), (0, 1), (0, 2), (1, 2))
    mix = np.zeros((128, 11 * 128))
    for x in range(-1, 9):
        for y in range(-1, 9):
            out = STRIDE * (x + 1) + y + 1
            mix[lane_of(x, y), out] += 1.0
            for at, (m, k) in enumerate(pairs):
                for a in (-1, 0, 1):
                    for b in (-1, 0, 1):
                        src = lane_of(x + a, y + b)
                        if at < 4:
                            mix[src, 128 * (1 + at) + out] += 72.0 * coef(m, k, (a, b, 0))
                        mix[src, 128 * (5 + at) + out] += 72.0 * coef(m, k, (a, b, 1))
    mix = np.round(mix)
    lane = np.arange(128)
    ints = np.zeros((24, 128), np.int32)
    ints[0:8] = np.where(lane < 110, lane // STRIDE, 99)
    ints[8:16] = np.where(lane < 110, lane % STRIDE, 99)
    ints[16:24] = np.where(lane < 126, lane // 21, 99)
    floats = np.zeros((16, 128), np.float32)
    floats[0:8] = (2.0 * (lane // STRIDE - 1) + 1.0) / SIDE - 1.0
    floats[8:16] = (2.0 * (lane % STRIDE - 1) + 1.0) / SIDE - 1.0
    half = lambda a: jnp.asarray(a, jnp.bfloat16)
    return half(place), half(place_blocks), half(mix), jnp.asarray(ints), jnp.asarray(floats)


WHOLE = sum(coef(0, 0, (a, b, c)) for a in (-1, 0, 1) for b in (-1, 0, 1) for c in (-1, 0, 1))


def thirds(x):
    high = x.astype(jnp.bfloat16)
    rest = x - high.astype(F32)
    middle = rest.astype(jnp.bfloat16)
    return high, middle, (rest - middle.astype(F32)).astype(jnp.bfloat16)


def turn(x, shift):
    shift = shift % 128
    return x if shift == 0 else pltpu.roll(x, shift, 1)


def add_all(items):
    items = list(items)
    while len(items) > 1:
        items = [
            items[i] + items[i + 1] if i + 1 < len(items) else items[i] for i in range(0, len(items), 2)
        ]
    return items[0]


def kernel(
    sizes,
    cz,
    rhs_hbm,
    labels_hbm,
    moduli,
    nodes_hbm,
    inverse,
    place_hbm,
    place_blocks_hbm,
    mix_hbm,
    ints_hbm,
    floats_hbm,
    sol_out,
    res_out,
    mat,
    rhs,
    labels,
    nodes_in,
    place,
    place_blocks,
    mix,
    ints,
    floats,
    mixed,
    field,
    zfield,
    qfield,
    rfield,
    pfield,
    vf,
    wf,
    syv,
    dyv,
    syw,
    dyw,
    dmat,
    stiff,
    cdiag,
    node,
    gridm,
    stage,
    rowm,
    ybuf,
    cvec,
    zsend,
    zrecv,
    ysend,
    yrecv,
    xsend,
    xrecv,
    gmsg,
    g1,
    g1c,
    g2,
    load_sem,
    halo_ss,
    halo_rs,
    g1_ss,
    g1_rs,
    g2_ss,
    g2_rs,
):
    ngx, ngy, ngz = sizes
    rows, srows, total = plan(cz)
    tiles = rows // 8
    sbase = LEAD + 3 * rows
    gx, gy, gz = lax.axis_index("gx"), lax.axis_index("gy"), lax.axis_index("gz")
    zhi, yhi = lax.rem(gx, ZH), lax.div(gx, ZH)
    nline = ZH * ngy
    nplane = (ngx // ZH) * ngz
    slot1 = zhi * ngy + gy
    slot2 = yhi * ngz + gz

    def line_peer(step):
        other = lax.rem(slot1 + step, nline)
        return (yhi * ZH + lax.div(other, ngy), lax.rem(other, ngy), gz)

    def plane_peer(step):
        other = lax.rem(slot2 + step, nplane)
        return (lax.div(other, ngz) * ZH + zhi, gy, lax.rem(other, ngz))

    sides = (
        (gz > 0, (gx, gy, gz - 1)),
        (gz < ngz - 1, (gx, gy, gz + 1)),
        (gy > 0, (gx, gy - 1, gz)),
        (gy < ngy - 1, (gx, gy + 1, gz)),
        (gx > 0, (gx - 1, gy, gz)),
        (gx < ngx - 1, (gx + 1, gy, gz)),
    )

    barrier = pltpu.get_barrier_semaphore()
    for has, device in sides:

        @pl.when(has)
        def _(device=device):
            pl.semaphore_signal(barrier, inc=1, device_id=device, device_id_type=MESH)

    for step in range(1, nline):
        pl.semaphore_signal(barrier, inc=1, device_id=line_peer(step), device_id_type=MESH)
    for step in range(1, nplane):
        pl.semaphore_signal(barrier, inc=1, device_id=plane_peer(step), device_id_type=MESH)

    loads = [
        pltpu.make_async_copy(src, dst, load_sem.at[at])
        for at, (src, dst) in enumerate(
            (
                (rhs_hbm, rhs),
                (nodes_hbm, nodes_in),
                (labels_hbm, labels),
                (place_hbm, place),
                (place_blocks_hbm, place_blocks),
                (ints_hbm, ints),
                (floats_hbm, floats),
                (mix_hbm, mix),
                (inverse, mat),
            )
        )
    ]
    for load in loads:
        load.start()
    mat_copy, mix_copy = loads[-1], loads[-2]

    lane = lax.broadcasted_iota(jnp.int32, (8, 128), 1)
    sub = lax.broadcasted_iota(jnp.int32, (8, 128), 0)

    def base_of(k, i):
        return tile_at(LEAD + k * rows, i)

    def tile_at(first, i):
        return first + 8 * i if isinstance(i, int) else pl.multiple_of(first + 8 * i, 8)

    def each_tile(one, unroll=4):
        whole = tiles // unroll

        def some(n, carry):
            for j in range(unroll):
                one(n * unroll + j)
            return carry

        lax.fori_loop(0, whole, some, 0)
        for i in range(whole * unroll, tiles):
            one(i)

    def xi_z(i):
        along = (sub + (8 * i - 1)).astype(F32)
        return (2.0 * along + 1.0) / cz - 1.0

    for f in range(6):
        dmat[rows * f + cz + 2 : rows * (f + 1), :] = jnp.zeros((rows - cz - 2, 128), F32)
    stiff[cz + 2 : rows, :] = jnp.zeros((rows - cz - 2, 128), F32)
    for ref in (field, zfield, qfield, rfield, pfield):
        ref[...] = jnp.zeros(ref.shape, F32)
    for ref in (vf, wf, syv, dyv, syw, dyw):
        ref[0:LEAD, :] = jnp.zeros((LEAD, 128), F32)
        ref[LEAD + 3 * rows : LEAD + 3 * rows + 8, :] = jnp.zeros((8, 128), F32)
    node[...] = jnp.zeros(node.shape, F32)
    rowm[...] = jnp.zeros(rowm.shape, F32)
    zsend[...] = jnp.zeros(zsend.shape, F32)
    cvec[...] = jnp.zeros(cvec.shape, F32)
    stage[...] = jnp.zeros(stage.shape, F32)
    for side, (has, _) in enumerate(sides):

        @pl.when(jnp.logical_not(has))
        def _(side=side):
            ref = (zrecv, yrecv, xrecv)[side // 2]
            for t in range(4):
                ref[t, side % 2] = jnp.zeros(ref.shape[2:], F32)

    for load in loads[:-2]:
        load.wait()
    lane_x, lane_y, lane_c = ints[0:8, :], ints[8:16, :], ints[16:24, :]
    xi_x, xi_y = floats[0:8, :], floats[8:16, :]

    def dot(a, b, dims):
        return lax.dot_general(a, b, ((dims[:1], dims[1:]), ((), ())), preferred_element_type=F32)

    def spread_in(x):
        return add_all([dot(part, place[...], (0, 0)) for part in thirds(x)[::-1]])

    def gather_out(select, x):
        return add_all([dot(select, part, (1, 1)) for part in thirds(x)[::-1]])

    for k in range(3):
        piece = spread_in(rhs[64 * k : 64 * k + 64, :])
        first = LEAD + k * rows + 1
        field[first : first + cz, :] = piece
        rfield[first : first + cz, :] = piece
    node[1 : 1 + cz, :] = dot((nodes_in[...].astype(F32) + 1.0).astype(jnp.bfloat16), place[...], (0, 0))
    for i in range(4):
        stage[4 * i : 4 * i + 4, :] = labels[i].astype(F32) + 1.0
    phases = dot(stage[...].astype(jnp.bfloat16), place_blocks[...], (0, 0))
    blocks = jnp.zeros(phases.shape, F32)
    for phase in range(moduli.shape[0]):
        blocks = jnp.where(phases == float(phase + 1), moduli[phase], blocks)
    field[sbase + 1 : sbase + 1 + cz // 2, :] = blocks

    bad_lane = (
        ((gx == 0) & (lane_x == 0))
        | ((gx == ngx - 1) & (lane_x == 9))
        | ((gy == 0) & (lane_y == 0))
        | ((gy == ngy - 1) & (lane_y == 9))
        | (lane_x > 9)
        | (lane_y > 9)
    )
    low = jnp.where(gz == 0, 1, 0)
    high = jnp.where(gz == ngz - 1, cz + 1, cz + 2)

    def grid_tile(i):
        r = sub + 8 * i
        gridm[pl.ds(tile_at(0, i), 8), :] = jnp.where(bad_lane | (r < low) | (r >= high), 0.0, 1.0)

    each_tile(grid_tile)

    def halo(which, side, ref_s, ref_r):
        return pltpu.make_async_remote_copy(
            src_ref=ref_s.at[which, side % 2],
            dst_ref=ref_r.at[which, 1 - side % 2],
            send_sem=halo_ss.at[which, side],
            recv_sem=halo_rs.at[which, side + 1 - 2 * (side % 2)],
            device_id=sides[side][1],
            device_id_type=MESH,
        )

    def start(which, axis, ref_s, ref_r):
        for side in (2 * axis, 2 * axis + 1):

            @pl.when(sides[side][0])
            def _(side=side):
                halo(which, side, ref_s, ref_r).start()

    def arrive(which, axis, ref_s, ref_r):
        for side in (2 * axis, 2 * axis + 1):

            @pl.when(sides[side][0])
            def _(side=side):
                pltpu.make_async_remote_copy(
                    src_ref=ref_s.at[which, side % 2],
                    dst_ref=ref_r.at[which, side % 2],
                    send_sem=halo_ss.at[which, side],
                    recv_sem=halo_rs.at[which, side],
                    device_id=sides[side][1],
                    device_id_type=MESH,
                ).wait_recv()

    def left(which, axis, ref_s, ref_r):
        for side in (2 * axis, 2 * axis + 1):

            @pl.when(sides[side][0])
            def _(side=side):
                halo(which, side, ref_s, ref_r).wait_send()

    def z_rows(width):
        if width == 1:
            got = [(LEAD + k * rows, cz, k) for k in range(3)] + [(sbase, cz // 2, 3)]
            return [(r + n, r + 1, r, r + n + 1, at) for r, n, at in got]
        out = []
        for k in range(3):
            for layer in range(2):
                r = LEAD + k * rows + layer
                out.append((r + cz, r, r, r + cz, 2 * k + layer))
        return out

    def pack_z(ref, which, width):
        for up_from, down_from, _, _, at in z_rows(width):
            zsend[which, 0, at : at + 1, :] = ref[down_from : down_from + 1, :]
            zsend[which, 1, at : at + 1, :] = ref[up_from : up_from + 1, :]

    def unpack_z(ref, which, width):
        for _, _, low_to, high_to, at in z_rows(width):
            ref[low_to : low_to + 1, :] += zrecv[which, 0, at : at + 1, :]
            ref[high_to : high_to + 1, :] += zrecv[which, 1, at : at + 1, :]

    def scheme(axis, width):
        if width == 1:
            if axis == 1:
                return 10, total // 80, lambda k: lane_y == k, lambda k: (k - 1, k - 8), (lane_y == 0, lane_y == 9), lambda k: (-k, 9 - k)
            return (
                10,
                total // 80,
                lambda k: lane_x == k,
                lambda k: (STRIDE * (k - 1), STRIDE * (k - 8)),
                (lane_x == 0, lane_x == 9),
                lambda k: (-STRIDE * k, STRIDE * (9 - k)),
            )
        if axis == 1:
            return (
                5,
                -(-3 * rows // 40),
                lambda k: (lane_y == 2 * k) | (lane_y == 2 * k + 1),
                lambda k: (2 * k, 2 * k - 8),
                (lane_y < 2, (lane_y == 8) | (lane_y == 9)),
                lambda k: (-2 * k, 8 - 2 * k),
            )
        return (
            6,
            -(-3 * rows // 48),
            lambda k: lane_c == k,
            lambda k: (21 * k, 21 * k - 88),
            (lane < 21, (lane >= 88) & (lane < 109)),
            lambda k: (-21 * k, 88 - 21 * k),
        )

    def pack(ref, which, axis, width, buf):
        chunks, deep, mask, shift, _, _ = scheme(axis, width)
        masks = [mask(k) for k in range(chunks)]

        def one(t, carry):
            down, up = jnp.zeros((8, 128), F32), jnp.zeros((8, 128), F32)
            for k in range(chunks):
                tile = ref[pl.ds(pl.multiple_of(LEAD + 8 * (k * deep + t), 8), 8), :]
                down = jnp.where(masks[k], turn(tile, shift(k)[0]), down)
                up = jnp.where(masks[k], turn(tile, shift(k)[1]), up)
            at = pl.ds(pl.multiple_of(8 * t, 8), 8)
            buf[which, 0, at, :] = down
            buf[which, 1, at, :] = up
            return carry

        lax.fori_loop(0, deep, one, 0)

    def unpack(ref, which, axis, width, buf):
        chunks, deep, _, _, ends, shift = scheme(axis, width)

        def one(t, carry):
            at = pl.ds(pl.multiple_of(8 * t, 8), 8)
            from_low, from_high = buf[which, 0, at, :], buf[which, 1, at, :]
            for k in range(chunks):
                rows_k = pl.ds(pl.multiple_of(LEAD + 8 * (k * deep + t), 8), 8)
                tile = ref[rows_k, :]
                tile = tile + jnp.where(ends[0], turn(from_low, shift(k)[0]), 0.0)
                tile = tile + jnp.where(ends[1], turn(from_high, shift(k)[1]), 0.0)
                ref[rows_k, :] = tile
            return carry

        lax.fori_loop(0, deep, one, 0)

    def cut(ref, axis, width):
        deep = 8 * scheme(axis, width)[1]
        return ref.at[:, :, 0:deep, :]

    def exchange(ref, which, width, between=None):
        pack_z(ref, which, width)
        start(which, 0, zsend, zrecv)
        arrive(which, 0, zsend, zrecv)
        unpack_z(ref, which, width)
        pack(ref, which, 1, width, ysend)
        start(which, 1, cut(ysend, 1, width), cut(yrecv, 1, width))
        arrive(which, 1, cut(ysend, 1, width), cut(yrecv, 1, width))
        unpack(ref, which, 1, width, yrecv)
        pack(ref, which, 2, width, xsend)
        start(which, 2, cut(xsend, 2, width), cut(xrecv, 2, width))
        if between is not None:
            between()
        arrive(which, 2, cut(xsend, 2, width), cut(xrecv, 2, width))
        unpack(ref, which, 2, width, xrecv)

    def line_copy(which, step):
        return pltpu.make_async_remote_copy(
            src_ref=gmsg.at[which, pl.ds(0, 1)],
            dst_ref=g1.at[which, pl.ds(slot1, 1)],
            send_sem=g1_ss.at[which, step],
            recv_sem=g1_rs.at[which, slot1],
            device_id=line_peer(step),
            device_id_type=MESH,
        )

    def line_start(which, message):
        gmsg[which] = message
        g1[which, pl.ds(slot1, 1), :] = message[0:1, :]
        for step in range(1, nline):
            line_copy(which, step).start()

    def line_arrive(which):
        for step in range(1, nline):
            other = lax.rem(slot1 + step, nline)
            pltpu.make_async_remote_copy(
                src_ref=gmsg.at[which, pl.ds(0, 1)],
                dst_ref=g1.at[which, pl.ds(other, 1)],
                send_sem=g1_ss.at[which, step],
                recv_sem=g1_rs.at[which, other],
                device_id=line_peer(step),
                device_id_type=MESH,
            ).wait_recv()

    def plane_copy(which, step):
        return pltpu.make_async_remote_copy(
            src_ref=g1c.at[which],
            dst_ref=g2.at[which, slot2],
            send_sem=g2_ss.at[which, step],
            recv_sem=g2_rs.at[which, slot2],
            device_id=plane_peer(step),
            device_id_type=MESH,
        )

    def plane_start(which, block):
        g1c[which] = block
        g2[which, pl.ds(slot2, 1)] = block[None]
        for step in range(1, nplane):
            plane_copy(which, step).start()

    def plane_arrive(which):
        for step in range(1, nplane):
            other = lax.rem(slot2 + step, nplane)
            pltpu.make_async_remote_copy(
                src_ref=g1c.at[which],
                dst_ref=g2.at[which, other],
                send_sem=g2_ss.at[which, step],
                recv_sem=g2_rs.at[which, other],
                device_id=plane_peer(step),
                device_id_type=MESH,
            ).wait_recv()

    def moments(ref):
        def one(i, acc):
            r = [ref[pl.ds(base_of(k, i), 8), :] for k in range(3)]
            own = node[pl.ds(tile_at(0, i), 8), :]
            z = xi_z(i)
            parts = r + [xi_y * r[2] - z * r[1], z * r[0] - xi_x * r[2], xi_x * r[1] - xi_y * r[0]]
            out = []
            for g in range(NODES):
                here = own == float(g + 1)
                for m in range(6):
                    out.append(acc[6 * g + m] + jnp.where(here, parts[m], 0.0))
            return tuple(out)

        acc = lax.fori_loop(0, tiles, one, tuple(jnp.zeros((8, 128), F32) for _ in range(MODES)))
        for at in range(MODES):
            rowm[at : at + 1, :] = jnp.sum(acc[at], axis=0, keepdims=True)

    def row_to_lanes():
        return gather_out(jnp.ones((8, 128), jnp.bfloat16), rowm[...])

    turned = lax.rem((gy * ngz + gz) * MODES, 128)

    def own_range(c):
        begin = (sub * ngz + c) * MODES - 128 * sub
        ahead = begin < 128
        first = (lane >= begin) & (lane < begin + MODES)
        second = (lane + 128 >= begin) & (lane + 128 < begin + MODES)
        return first, second

    def coarse_solve(which):
        ranges = [own_range(c) for c in range(ngz)]
        acc = [jnp.zeros((8, 128), F32) for _ in range(5)]
        for y in range(ngx // ZH):
            for h in range(ZH):
                a = y * ZH + h
                got = [g2[which, y * ngz + c, 8 * h : 8 * h + 8, :] for c in range(ngz)]
                main = add_all([jnp.where(ranges[c][0], got[c], 0.0) for c in range(ngz)])
                nxt = add_all([jnp.where(ranges[c][1], got[c], 0.0) for c in range(ngz)])
                cvec[16 * a + 8 : 16 * a + 9, :] = jnp.zeros((1, 128), F32)
                cvec[16 * a : 16 * a + 8, :] = main
                cvec[16 * a + 1 : 16 * a + 9, :] += nxt
        for a in range(ngx):
            for j in range(9):
                row = jnp.broadcast_to(cvec[16 * a + j : 16 * a + j + 1, :], (8, 128))
                col = 128 * (9 * a + j)
                for t in range(4):
                    acc[t] = acc[t] + mat[8 * t : 8 * t + 8, col : col + 128] * row
                acc[4] = acc[4] + jnp.concatenate([mat[32:36, col : col + 128]] * 2, axis=0) * row
        for t in range(5):
            ybuf[8 * t : 8 * t + 8, :] = jnp.broadcast_to(jnp.sum(acc[t], axis=1, keepdims=True), (8, 128))

    def lane_sum(which, at):
        parts = []
        for c in range(ngz):
            pos = lax.rem((sub * ngz + c) * MODES + at, 128)
            here = lane == pos
            for y in range(ngx // ZH):
                for h in range(ZH):
                    parts.append(jnp.where(here, g2[which, y * ngz + c, 8 * h : 8 * h + 8, :], 0.0))
        whole = jnp.sum(add_all(parts), axis=0, keepdims=True)
        return jnp.sum(whole, axis=1, keepdims=True)

    def with_coarse(src, dst):
        def one(i):
            own = node[pl.ds(tile_at(0, i), 8), :]
            grid = gridm[pl.ds(tile_at(0, i), 8), :]
            z = xi_z(i)
            modes = [jnp.zeros((8, 128), F32) for _ in range(6)]
            for g in range(NODES):
                here = own == float(g + 1)
                for m in range(6):
                    at = 6 * g + m
                    modes[m] = jnp.where(here, jnp.broadcast_to(ybuf[at : at + 1, :], (8, 128)), modes[m])
            t, w = modes[:3], modes[3:]
            add = [
                t[0] + (w[1] * z - w[2] * xi_y),
                t[1] + (w[2] * xi_x - w[0] * z),
                t[2] + (w[0] * xi_y - w[1] * xi_x),
            ]
            for k in range(3):
                at = pl.ds(base_of(k, i), 8)
                dst[at, :] = src[at, :] * grid + add[k]

        each_tile(one)

    def spread(ref):
        def one(i):
            s = stiff[pl.ds(tile_at(0, i), 8), :]
            for k in range(3):
                at = pl.ds(base_of(k, i), 8)
                v = ref[at, :]
                w = s * v
                vf[at, :] = v
                wf[at, :] = w
                for x, sy, dy in ((v, syv, dyv), (w, syw, dyw)):
                    ahead, behind = turn(x, -1), turn(x, 1)
                    sy[at, :] = ahead + behind
                    dy[at, :] = ahead - behind

        each_tile(one)

    def couple(u_ref, sy_ref, dy_ref, i):
        def at(ref, k, dz):
            return ref[pl.ds(base_of(k, i) + dz, 8), :]

        up = [at(u_ref, k, 1) for k in range(3)]
        um = [at(u_ref, k, -1) for k in range(3)]
        u = [at(u_ref, k, 0) for k in range(3)]
        s = [up[k] + um[k] for k in range(3)]
        yp = [at(sy_ref, k, 1) for k in range(3)]
        ym = [at(sy_ref, k, -1) for k in range(3)]
        sy = [at(sy_ref, k, 0) for k in range(3)]
        sys = [yp[k] + ym[k] for k in range(3)]
        t_x, t_z = up[0] - um[0], up[2] - um[2]
        ty_x, ty_z = yp[0] - ym[0], yp[2] - ym[2]
        dp = [at(dy_ref, k, 1) for k in range(3)]
        dm = [at(dy_ref, k, -1) for k in range(3)]
        dys_x, dys_y = dp[0] + dm[0], dp[1] + dm[1]
        dyt_y, dyt_z = dp[1] - dm[1], dp[2] - dm[2]
        dy_x, dy_y = at(dy_ref, 0, 0), at(dy_ref, 1, 0)
        e, th, c7 = 0.125, 1.0 / 18.0, 7.0 / 18.0
        still = [
            sy[0] + s[0] + 0.5 * sys[0],
            1.5 * sy[1] + s[1] + 0.625 * sys[1] + e * dyt_z,
            sy[2] + 1.5 * s[2] + 0.625 * sys[2] + e * dyt_y,
        ]
        even = [
            1.5 * u[0] + 0.625 * (sy[0] + s[0]) + c7 * sys[0],
            u[1] + 0.625 * sy[1] + 0.5 * s[1] + c7 * sys[1] + th * dyt_z,
            u[2] + 0.5 * sy[2] + 0.625 * s[2] + c7 * sys[2] + th * dyt_y,
        ]
        odd = [
            e * (dy_y + t_z) + th * (dys_y + ty_z),
            e * dy_x + th * dys_x,
            e * t_x + th * ty_x,
        ]
        return [
            still[k] + (turn(even[k] + odd[k], -STRIDE) + turn(even[k] - odd[k], STRIDE)) for k in range(3)
        ], u

    def image_tile(i):
        here = pl.ds(tile_at(0, i), 8)
        lv, v = couple(vf, syv, dyv, i)
        lw, _ = couple(wf, syw, dyw, i)
        s = stiff[here, :]
        d = [dmat[pl.ds(tile_at(rows * f, i), 8), :] for f in range(6)]
        full = ((0, 3, 4), (3, 1, 5), (4, 5, 2))
        out = []
        for m in range(3):
            diag = d[full[m][0]] * v[0] + d[full[m][1]] * v[1] + d[full[m][2]] * v[2]
            out.append(diag - 0.5 * (s * lv[m] + lw[m]))
        return out, v

    def local_solve(ref, out):
        def first(i):
            for k in range(3):
                at = pl.ds(base_of(k, i), 8)
                out[at, :] = cdiag[pl.ds(tile_at(rows * k, i), 8), :] * ref[at, :]

        each_tile(first)

        def sweep(n, carry):
            spread(out)

            def one(i):
                image, v = image_tile(i)
                for k in range(3):
                    at = pl.ds(base_of(k, i), 8)
                    c = cdiag[pl.ds(tile_at(rows * k, i), 8), :]
                    out[at, :] = v[k] + c * (ref[at, :] - image[k])

            each_tile(one)
            return carry

        lax.fori_loop(0, SWEEPS - 1, sweep, 0)

    def setup_stiffness():
        mix_copy.wait()
        parts = thirds(field[sbase : sbase + srows, :])[::-1]
        for f in range(0, 11, 2):
            wide = 128 * min(2, 11 - f)
            got = add_all([dot(part, mix[:, 128 * f : 128 * f + wide], (1, 0)) for part in parts])
            for g in range(wide // 128):
                mixed[srows * (f + g) : srows * (f + g + 1), :] = got[:, 128 * g : 128 * g + 128]
        count = cz // 2 + 1

        def at(f, shift):
            return mixed[srows * f + shift : srows * f + shift + count, :]

        for parity in range(2):
            here = lambda f: at(f, parity)
            beyond = lambda f: at(f, 1 - parity)
            s_here = here(0)
            stiff[pl.ds(parity, count, stride=2), :] = s_here
            for m in range(6):
                if m < 4:
                    value = (here(1 + m) + here(5 + m) + beyond(5 + m)) * (1.0 / 144.0)
                    if m < 3:
                        value = value + (0.5 * WHOLE) * s_here
                else:
                    tilt = here(5 + m) - beyond(5 + m)
                    value = (tilt if parity == 1 else -tilt) * (1.0 / 144.0)
                dmat[pl.ds(rows * m + parity, count, stride=2), :] = value

        def one(i):
            for k in range(3):
                part = pl.ds(tile_at(rows * k, i), 8)
                d = dmat[part, :]
                live = d > 0.0
                cdiag[part, :] = jnp.where(live, RELAX / jnp.where(live, d, 1.0), 0.0)

        each_tile(one)

    moments(field)
    first_row = turn_by(row_to_lanes(), turned)
    greeters = nline - 1 + nplane - 1
    for has, _ in sides:
        greeters = greeters + jnp.where(has, 1, 0)
    pl.semaphore_wait(barrier, greeters)

    def forward(which):
        def run():
            line_arrive(which)
            plane_start(which, g1[which])

        return run

    line_start(0, first_row)
    exchange(field, 0, 1, forward(0))
    setup_stiffness()
    local_solve(field, pfield)
    mat_copy.wait()
    plane_arrive(0)
    coarse_solve(0)
    with_coarse(pfield, zfield)
    exchange(zfield, 1, 2)

    spread(zfield)

    def image_and_sums(dst, first, second):
        def one(i, acc):
            image, v = image_tile(i)
            own = node[pl.ds(tile_at(0, i), 8), :] > 0.0
            acc = list(acc)
            for k in range(3):
                at = pl.ds(base_of(k, i), 8)
                mine = jnp.where(own, image[k], 0.0)
                dst[at, :] = mine
                acc[0] = acc[0] + first[at, :] * v[k]
                acc[1] = acc[1] + v[k] * mine
                if second is not None:
                    acc[2] = acc[2] + second[at, :] * v[k]
            return tuple(acc)

        count = 2 if second is None else 3
        acc = lax.fori_loop(0, tiles, one, tuple(jnp.zeros((8, 128), F32) for _ in range(count)))
        return [jnp.sum(a, axis=0, keepdims=True) for a in acc]

    sums = image_and_sums(qfield, rfield, None)
    moments(qfield)
    rowm[MODES : MODES + 1, :] = sums[0]
    rowm[MODES + 1 : MODES + 2, :] = sums[1]
    second_row = turn_by(row_to_lanes(), turned)

    line_start(1, second_row)
    for k in range(3):
        field[LEAD + rows * k : LEAD + rows * (k + 1), :] = qfield[LEAD + rows * k : LEAD + rows * (k + 1), :]
    exchange(field, 2, 1, forward(1))
    local_solve(field, pfield)
    plane_arrive(1)
    coarse_solve(1)
    rho0 = lane_sum(1, MODES)
    curve0 = lane_sum(1, MODES + 1)
    alpha0 = rho0 / curve0
    with_coarse(pfield, field)
    exchange(field, 3, 2)

    def renew(i):
        for k in range(3):
            at = pl.ds(base_of(k, i), 8)
            field[at, :] = zfield[at, :] - alpha0 * field[at, :]
            rfield[at, :] = rfield[at, :] - alpha0 * qfield[at, :]

    each_tile(renew)
    spread(field)

    sums = image_and_sums(pfield, rfield, qfield)
    rowm[0:MODES, :] = jnp.zeros((MODES, 128), F32)
    for at in range(3):
        rowm[MODES + at : MODES + at + 1, :] = sums[at]
    line_start(2, turn_by(row_to_lanes(), turned))
    line_arrive(2)
    plane_start(2, g1[2])
    plane_arrive(2)
    rho1 = lane_sum(2, MODES)
    zaz = lane_sum(2, MODES + 1)
    zq = lane_sum(2, MODES + 2)
    beta = rho1 / rho0
    alpha1 = rho1 / (zaz + 2.0 * beta * zq + beta * beta * curve0)

    for k in range(3):
        at = slice(LEAD + k * rows + 1, LEAD + k * rows + 1 + cz)
        z0, z1 = zfield[at, :], field[at, :]
        sol_out[64 * k : 64 * k + 64, :] = gather_out(place[...], alpha0 * z0 + alpha1 * (z1 + beta * z0))
        res_out[64 * k : 64 * k + 64, :] = gather_out(
            place[...], rfield[at, :] - alpha1 * (pfield[at, :] + beta * qfield[at, :])
        )

    for which in range(4):
        width = 1 + which % 2
        left(which, 0, zsend, zrecv)
        left(which, 1, cut(ysend, 1, width), cut(yrecv, 1, width))
        left(which, 2, cut(xsend, 2, width), cut(xrecv, 2, width))
    for which in range(3):
        for step in range(1, nline):
            line_copy(which, step).wait_send()
        for step in range(1, nplane):
            plane_copy(which, step).wait_send()


def turn_by(x, shift):
    return pltpu.roll(x, shift, 1)


def solution(mesh):
    sizes = (mesh.shape["gx"], mesh.shape["gy"], mesh.shape["gz"])
    nline = ZH * sizes[1]
    nplane = (sizes[0] // ZH) * sizes[2]

    def body(right_side, phase_labels, phase_moduli, coarse_nodes, coarse_inverse):
        cz = right_side.shape[3]
        rows, srows, total = plan(cz)
        tall = pltpu.VMEM((LEAD + total, 128), F32)
        ydeep = max(total // 10, 8 * -(-3 * rows // 40))
        xdeep = max(total // 10, 8 * -(-3 * rows // 48))
        vmem = pl.BlockSpec(memory_space=pltpu.VMEM)
        away = pl.BlockSpec(memory_space=pl.ANY)
        consts = tables(cz)
        sol, res = pl.pallas_call(
            functools.partial(kernel, sizes, cz),
            out_shape=(jax.ShapeDtypeStruct((192, cz), F32),) * 2,
            in_specs=[
                away,
                away,
                pl.BlockSpec(memory_space=pltpu.SMEM),
                away,
                away,
            ]
            + [away] * len(consts),
            out_specs=(vmem, vmem),
            scratch_shapes=[
                pltpu.VMEM(coarse_inverse.shape, F32),
                pltpu.VMEM((192, cz), F32),
                pltpu.VMEM(phase_labels.shape, jnp.int32),
                pltpu.VMEM((64, cz), jnp.int32),
            ]
            + [pltpu.VMEM(c.shape, c.dtype) for c in consts]
            + [
                pltpu.VMEM((11 * srows + 8, 128), F32),
                tall,
                tall,
                tall,
                tall,
                tall,
                tall,
                tall,
                tall,
                tall,
                tall,
                tall,
                pltpu.VMEM((6 * rows, 128), F32),
                pltpu.VMEM((rows, 128), F32),
                pltpu.VMEM((3 * rows, 128), F32),
                pltpu.VMEM((rows, 128), F32),
                pltpu.VMEM((rows, 128), F32),
                pltpu.VMEM((16, cz // 2), F32),
                pltpu.VMEM((128, 128), F32),
                pltpu.VMEM((40, 128), F32),
                pltpu.VMEM((16 * sizes[0], 128), F32),
                pltpu.VMEM((4, 2, 8, 128), F32),
                pltpu.VMEM((4, 2, 8, 128), F32),
                pltpu.VMEM((4, 2, ydeep, 128), F32),
                pltpu.VMEM((4, 2, ydeep, 128), F32),
                pltpu.VMEM((4, 2, xdeep, 128), F32),
                pltpu.VMEM((4, 2, xdeep, 128), F32),
                pltpu.VMEM((3, 8, 128), F32),
                pltpu.VMEM((3, nline, 128), F32),
                pltpu.VMEM((3, nline, 128), F32),
                pltpu.VMEM((3, nplane, nline, 128), F32),
                pltpu.SemaphoreType.DMA((9,)),
                pltpu.SemaphoreType.DMA((4, 6)),
                pltpu.SemaphoreType.DMA((4, 6)),
                pltpu.SemaphoreType.DMA((3, nline)),
                pltpu.SemaphoreType.DMA((3, nline)),
                pltpu.SemaphoreType.DMA((3, nplane)),
                pltpu.SemaphoreType.DMA((3, nplane)),
            ],
            compiler_params=pltpu.CompilerParams(
                collective_id=0, has_side_effects=True, vmem_limit_bytes=67_000_000
            ),
            name="schwarz_cg",
        )(
            right_side.reshape(192, cz),
            phase_labels,
            phase_moduli,
            coarse_nodes.reshape(64, cz),
            coarse_inverse,
            *consts,
        )
        return sol.reshape(right_side.shape), res.reshape(right_side.shape)

    spec = P(None, "gx", "gy", "gz")
    cells = P("gx", "gy", "gz")
    return jax.shard_map(
        body,
        mesh=mesh,
        in_specs=(spec, cells, P(), cells, P(("gx", "gy", "gz"), None)),
        out_specs=(spec, spec),
        check_vma=False,
    )
```

```python
import functools

import jax
import jax.numpy as jnp
import numpy as np
from jax import lax
from jax.experimental import pallas as pl
from jax.experimental.pallas import tpu as pltpu
from jax.sharding import PartitionSpec as P

MESH = pl.DeviceIdType.MESH
HIGH = lax.Precision.HIGHEST
F32 = jnp.float32

RELAX = 0.6
SWEEPS = 4
SIDE = 8
STRIDE = 11
LEAD = 8
ZH = 2
NODES = 6
NEIGHBOURS = [(x, y, z) for x in (-1, 0, 1) for y in (-1, 0, 1) for z in (-1, 0, 1) if (x, y, z) != (0, 0, 0)]
MODES = 36


def bond(d):
    return d[0] * d[0] + d[1] * d[1] + d[2] * d[2]


def coef(m, k, d):
    n = bond(d)
    if n == 0:
        return 0.0
    return (1.0 / n if m == k else 0.0) + 0.5 * d[m] * d[k] / (n * n)


def plan(cz):
    rows = -(-(cz + 3) // 8) * 8
    srows = -(-(cz // 2 + 2) // 8) * 8
    total = -(-(3 * rows + srows) // 80) * 80
    return rows, srows, total


def tables(cz):
    rows, srows, total = plan(cz)
    place = np.zeros((64, 128), np.float32)
    for i in range(SIDE):
        for j in range(SIDE):
            place[i * SIDE + j, STRIDE * (i + 1) + j + 1] = 1.0
    spot = {-1: 0, 0: 1, 1: 2, 2: 3, 3: 8, 4: 9}
    place_blocks = np.zeros((16, 128), np.float32)
    for i in range(4):
        for j in range(4):
            place_blocks[i * 4 + j, STRIDE * spot[i] + spot[j]] = 1.0

    def lane_of(x, y):
        return STRIDE * spot[x // 2] + spot[y // 2]

    pairs = ((0, 0), (1, 1), (2, 2), (0, 1), (0, 2), (1, 2))
    mix = np.zeros((128, 11 * 128))
    for x in range(-1, 9):
        for y in range(-1, 9):
            out = STRIDE * (x + 1) + y + 1
            mix[lane_of(x, y), out] += 1.0
            for at, (m, k) in enumerate(pairs):
                for a in (-1, 0, 1):
                    for b in (-1, 0, 1):
                        src = lane_of(x + a, y + b)
                        if at < 4:
                            mix[src, 128 * (1 + at) + out] += 72.0 * coef(m, k, (a, b, 0))
                        mix[src, 128 * (5 + at) + out] += 72.0 * coef(m, k, (a, b, 1))
    mix = np.round(mix)
    lane = np.arange(128)
    ints = np.zeros((24, 128), np.int32)
    ints[0:8] = np.where(lane < 110, lane // STRIDE, 99)
    ints[8:16] = np.where(lane < 110, lane % STRIDE, 99)
    ints[16:24] = np.where(lane < 126, lane // 21, 99)
    floats = np.zeros((16, 128), np.float32)
    floats[0:8] = (2.0 * (lane // STRIDE - 1) + 1.0) / SIDE - 1.0
    floats[8:16] = (2.0 * (lane % STRIDE - 1) + 1.0) / SIDE - 1.0
    half = lambda a: jnp.asarray(a, jnp.bfloat16)
    return half(place), half(place_blocks), half(mix), jnp.asarray(ints), jnp.asarray(floats)


WHOLE = sum(coef(0, 0, (a, b, c)) for a in (-1, 0, 1) for b in (-1, 0, 1) for c in (-1, 0, 1))


def thirds(x):
    high = x.astype(jnp.bfloat16)
    rest = x - high.astype(F32)
    middle = rest.astype(jnp.bfloat16)
    return high, middle, (rest - middle.astype(F32)).astype(jnp.bfloat16)


def turn(x, shift):
    shift = shift % 128
    return x if shift == 0 else pltpu.roll(x, shift, 1)


def add_all(items):
    items = list(items)
    while len(items) > 1:
        items = [
            items[i] + items[i + 1] if i + 1 < len(items) else items[i] for i in range(0, len(items), 2)
        ]
    return items[0]


def kernel(
    sizes,
    cz,
    rhs_hbm,
    labels_hbm,
    moduli,
    nodes_hbm,
    inverse,
    place_hbm,
    place_blocks_hbm,
    mix_hbm,
    ints_hbm,
    floats_hbm,
    sol_out,
    res_out,
    mat,
    rhs,
    labels,
    nodes_in,
    place,
    place_blocks,
    mix,
    ints,
    floats,
    mixed,
    field,
    zfield,
    qfield,
    rfield,
    pfield,
    vf,
    wf,
    syv,
    dyv,
    syw,
    dyw,
    dmat,
    stiff,
    cdiag,
    node,
    gridm,
    stage,
    rowm,
    ybuf,
    cvec,
    zsend,
    zrecv,
    ysend,
    yrecv,
    xsend,
    xrecv,
    csend,
    crecv,
    rsend,
    rrecv,
    zsum,
    gmsg,
    g1,
    g1c,
    g2,
    load_sem,
    halo_ss,
    halo_rs,
    g1_ss,
    g1_rs,
    g2_ss,
    g2_rs,
):
    ngx, ngy, ngz = sizes
    rows, srows, total = plan(cz)
    tiles = rows // 8
    sbase = LEAD + 3 * rows
    gx, gy, gz = lax.axis_index("gx"), lax.axis_index("gy"), lax.axis_index("gz")
    zhi, yhi = lax.rem(gx, ZH), lax.div(gx, ZH)
    nline = ZH * ngy
    nplane = (ngx // ZH) * ngz
    slot1 = zhi * ngy + gy
    slot2 = yhi * ngz + gz

    def line_peer(step):
        other = lax.rem(slot1 + step, nline)
        return (yhi * ZH + lax.div(other, ngy), lax.rem(other, ngy), gz)

    def plane_peer(step):
        other = lax.rem(slot2 + step, nplane)
        return (lax.div(other, ngz) * ZH + zhi, gy, lax.rem(other, ngz))

    sides = {}
    for d in NEIGHBOURS:
        has = None
        for way, at, count in zip(d, (gx, gy, gz), sizes):
            if way != 0:
                one = at > 0 if way < 0 else at < count - 1
                has = one if has is None else has & one
        sides[d] = (has, (gx + d[0], gy + d[1], gz + d[2]))

    barrier = pltpu.get_barrier_semaphore()
    for has, device in sides.values():

        @pl.when(has)
        def _(device=device):
            pl.semaphore_signal(barrier, inc=1, device_id=device, device_id_type=MESH)

    for step in range(1, nline):
        pl.semaphore_signal(barrier, inc=1, device_id=line_peer(step), device_id_type=MESH)
    for step in range(1, nplane):
        pl.semaphore_signal(barrier, inc=1, device_id=plane_peer(step), device_id_type=MESH)

    loads = [
        pltpu.make_async_copy(src, dst, load_sem.at[at])
        for at, (src, dst) in enumerate(
            (
                (rhs_hbm, rhs),
                (nodes_hbm, nodes_in),
                (labels_hbm, labels),
                (place_hbm, place),
                (place_blocks_hbm, place_blocks),
                (ints_hbm, ints),
                (floats_hbm, floats),
                (mix_hbm, mix),
                (inverse, mat),
            )
        )
    ]
    for load in loads:
        load.start()
    mat_copy, mix_copy = loads[-1], loads[-2]

    lane = lax.broadcasted_iota(jnp.int32, (8, 128), 1)
    sub = lax.broadcasted_iota(jnp.int32, (8, 128), 0)

    def base_of(k, i):
        return tile_at(LEAD + k * rows, i)

    def tile_at(first, i):
        return first + 8 * i if isinstance(i, int) else pl.multiple_of(first + 8 * i, 8)

    def each_tile(one, unroll=4):
        whole = tiles // unroll

        def some(n, carry):
            for j in range(unroll):
                one(n * unroll + j)
            return carry

        lax.fori_loop(0, whole, some, 0)
        for i in range(whole * unroll, tiles):
            one(i)

    def xi_z(i):
        along = (sub + (8 * i - 1)).astype(F32)
        return (2.0 * along + 1.0) / cz - 1.0

    def deep(axis, width):
        if width == 1:
            return total // 10
        return 8 * -(-3 * rows // (40 if axis == 1 else 48))

    def edge_deep(width):
        return 8 * -(-deep(1, width) // 48)

    def inbox(which, d):
        x, y, z = d
        width = 1 + which % 2
        if z != 0:
            if x == 0:
                return zrecv.at[which, 3 * (z > 0) + y + 1]
            at = 6 * (x > 0) + 3 * (z > 0) + y + 1
            return rrecv.at[which, at : at + 1]
        if x != 0 and y != 0:
            return crecv.at[which, 2 * (x > 0) + (y > 0), 0 : edge_deep(width)]
        if y != 0:
            return yrecv.at[which, int(y > 0), 0 : deep(1, width)]
        return xrecv.at[which, int(x > 0), 0 : deep(2, width)]

    def outbox(which, d):
        x, y, z = d
        width = 1 + which % 2
        if z != 0:
            if x == 0:
                return zsend.at[which, int(z > 0)]
            at = 2 * (x > 0) + (z > 0)
            return rsend.at[which, at, 0:1]
        if x != 0 and y != 0:
            return csend.at[which, 2 * (x > 0) + (y > 0), 0 : edge_deep(width)]
        if y != 0:
            return ysend.at[which, int(y > 0), 0 : deep(1, width)]
        return xsend.at[which, int(x > 0), 0 : deep(2, width)]

    for f in range(6):
        dmat[rows * f + cz + 2 : rows * (f + 1), :] = jnp.zeros((rows - cz - 2, 128), F32)
    stiff[cz + 2 : rows, :] = jnp.zeros((rows - cz - 2, 128), F32)
    for ref in (field, zfield, qfield, rfield, pfield):
        ref[...] = jnp.zeros(ref.shape, F32)
    for ref in (vf, wf, syv, dyv, syw, dyw):
        ref[0:LEAD, :] = jnp.zeros((LEAD, 128), F32)
        ref[LEAD + 3 * rows : LEAD + 3 * rows + 8, :] = jnp.zeros((8, 128), F32)
    node[...] = jnp.zeros(node.shape, F32)
    rowm[...] = jnp.zeros(rowm.shape, F32)
    for ref in (zsend, ysend):
        ref[...] = jnp.zeros(ref.shape, F32)
    tail = deep(1, 1)
    if tail < yrecv.shape[2]:
        for t in range(4):
            for e in range(2):
                end = deep(1, 1 + t % 2)
                yrecv[t, e, end:, :] = jnp.zeros((yrecv.shape[2] - end, 128), F32)
    cvec[...] = jnp.zeros(cvec.shape, F32)
    stage[...] = jnp.zeros(stage.shape, F32)
    for d in NEIGHBOURS:

        @pl.when(jnp.logical_not(sides[d][0]))
        def _(d=d):
            for t in range(4):
                ref = inbox(t, d)
                ref[...] = jnp.zeros(ref.shape, F32)

    for load in loads[:-2]:
        load.wait()
    lane_x, lane_y, lane_c = ints[0:8, :], ints[8:16, :], ints[16:24, :]
    xi_x, xi_y = floats[0:8, :], floats[8:16, :]

    def dot(a, b, dims):
        return lax.dot_general(a, b, ((dims[:1], dims[1:]), ((), ())), preferred_element_type=F32)

    def spread_in(x):
        return add_all([dot(part, place[...], (0, 0)) for part in thirds(x)[::-1]])

    def gather_out(select, x):
        return add_all([dot(select, part, (1, 1)) for part in thirds(x)[::-1]])

    for k in range(3):
        piece = spread_in(rhs[64 * k : 64 * k + 64, :])
        first = LEAD + k * rows + 1
        field[first : first + cz, :] = piece
        rfield[first : first + cz, :] = piece
    node[1 : 1 + cz, :] = dot((nodes_in[...].astype(F32) + 1.0).astype(jnp.bfloat16), place[...], (0, 0))
    for i in range(4):
        stage[4 * i : 4 * i + 4, :] = labels[i].astype(F32) + 1.0
    phases = dot(stage[...].astype(jnp.bfloat16), place_blocks[...], (0, 0))
    blocks = jnp.zeros(phases.shape, F32)
    for phase in range(moduli.shape[0]):
        blocks = jnp.where(phases == float(phase + 1), moduli[phase], blocks)
    field[sbase + 1 : sbase + 1 + cz // 2, :] = blocks

    bad_lane = (
        ((gx == 0) & (lane_x == 0))
        | ((gx == ngx - 1) & (lane_x == 9))
        | ((gy == 0) & (lane_y == 0))
        | ((gy == ngy - 1) & (lane_y == 9))
        | (lane_x > 9)
        | (lane_y > 9)
    )
    low = jnp.where(gz == 0, 1, 0)
    high = jnp.where(gz == ngz - 1, cz + 1, cz + 2)

    def grid_tile(i):
        r = sub + 8 * i
        gridm[pl.ds(tile_at(0, i), 8), :] = jnp.where(bad_lane | (r < low) | (r >= high), 0.0, 1.0)

    each_tile(grid_tile)

    def number(d):
        return 9 * (d[0] + 1) + 3 * (d[1] + 1) + d[2] + 1

    def opposite(d):
        return (-d[0], -d[1], -d[2])

    def halo(which, d):
        return pltpu.make_async_remote_copy(
            src_ref=outbox(which, d),
            dst_ref=inbox(which, opposite(d)),
            send_sem=halo_ss.at[which, number(d)],
            recv_sem=halo_rs.at[which, number(opposite(d))],
            device_id=sides[d][1],
            device_id_type=MESH,
        )

    def send(which, group):
        for d in group:

            @pl.when(sides[d][0])
            def _(d=d):
                halo(which, d).start()

    def arrive(which, group):
        for d in group:

            @pl.when(sides[d][0])
            def _(d=d):
                pltpu.make_async_remote_copy(
                    src_ref=outbox(which, d),
                    dst_ref=inbox(which, d),
                    send_sem=halo_ss.at[which, number(d)],
                    recv_sem=halo_rs.at[which, number(d)],
                    device_id=sides[d][1],
                    device_id_type=MESH,
                ).wait_recv()

    def left(which):
        for d in NEIGHBOURS:

            @pl.when(sides[d][0])
            def _(d=d):
                halo(which, d).wait_send()

    def z_rows(width):
        if width == 1:
            got = [(LEAD + k * rows, cz, k) for k in range(3)] + [(sbase, cz // 2, 3)]
            return [(r + n, r + 1, r, r + n + 1, at) for r, n, at in got]
        out = []
        for k in range(3):
            for layer in range(2):
                r = LEAD + k * rows + layer
                out.append((r + cz, r, r, r + cz, 2 * k + layer))
        return out

    def groups(axis, width):
        if axis == 1:
            if width == 1:
                return 10, [lane_y == k for k in range(10)]
            return 5, [(lane_y == 2 * k) | (lane_y == 2 * k + 1) for k in range(5)]
        if width == 1:
            return 10, [lane_x == k for k in range(10)]
        return 6, [lane_c == k for k in range(6)]

    def move(axis, width):
        if axis == 1:
            if width == 1:
                return 1, (1, 8), (0, 9), (lane_y == 0, lane_y == 9)
            return 2, (0, 8), (0, 8), (lane_y < 2, (lane_y == 8) | (lane_y == 9))
        if width == 1:
            return STRIDE, (STRIDE, 8 * STRIDE), (0, 9 * STRIDE), (lane_x == 0, lane_x == 9)
        return 21, (0, 88), (0, 88), (lane < 21, (lane >= 88) & (lane < 109))

    def pack(src, first, dsts, axis, width, chunks, depth):
        gap, froms, _, _ = move(axis, width)
        masks = groups(axis, width)[1]

        def one(t, carry):
            low, high = jnp.zeros((8, 128), F32), jnp.zeros((8, 128), F32)
            for k in range(chunks):
                tile = src[pl.ds(pl.multiple_of(first + 8 * (k * depth + t), 8), 8), :]
                low = jnp.where(masks[k], turn(tile, gap * k - froms[0]), low)
                high = jnp.where(masks[k], turn(tile, gap * k - froms[1]), high)
            at = pl.ds(pl.multiple_of(8 * t, 8), 8)
            dsts[0][at, :] = low
            dsts[1][at, :] = high
            return carry

        lax.fori_loop(0, depth, one, 0)

    def unpack(dst, first, srcs, axis, width, chunks, depth):
        gap, _, tos, ends = move(axis, width)

        def one(t, carry):
            at = pl.ds(pl.multiple_of(8 * t, 8), 8)
            low, high = srcs[0][at, :], srcs[1][at, :]
            for k in range(chunks):
                part = pl.ds(pl.multiple_of(first + 8 * (k * depth + t), 8), 8)
                tile = dst[part, :]
                tile = tile + jnp.where(ends[0], turn(low, tos[0] - gap * k), 0.0)
                tile = tile + jnp.where(ends[1], turn(high, tos[1] - gap * k), 0.0)
                dst[part, :] = tile
            return carry

        lax.fori_loop(0, depth, one, 0)

    def exchange(ref, which, width, between=None):
        chunks = [None, groups(1, width)[0], groups(2, width)[0]]
        depth = [None, deep(1, width) // 8, deep(2, width) // 8]
        edge = edge_deep(width) // 8
        gap, froms, tos, ends = move(2, width)
        pack(ref, LEAD, [xsend.at[which, e] for e in range(2)], 2, width, chunks[2], depth[2])
        send(which, [(-1, 0, 0), (1, 0, 0)])
        for up_from, down_from, _, _, at in z_rows(width):
            zsend[which, 0, at : at + 1, :] = ref[down_from : down_from + 1, :]
            zsend[which, 1, at : at + 1, :] = ref[up_from : up_from + 1, :]
        layers = 4 if width == 1 else 6
        mine = [(sub == r) & (lane >= gap * r) & (lane < gap * r + gap) for r in range(layers)]
        for z in range(2):
            tile = zsend[which, z]
            for x in range(2):
                row = jnp.zeros((8, 128), F32)
                for r in range(layers):
                    row = jnp.where(mine[r], turn(tile, gap * r - froms[x]), row)
                rsend[which, 2 * x + z, 0:1, :] = jnp.sum(row, axis=0, keepdims=True)
        send(which, [(x, y, z) for x in (-1, 1) for z in (-1, 1) for y in (-1, 0, 1)])
        pack(ref, LEAD, [ysend.at[which, e] for e in range(2)], 1, width, chunks[1], depth[1])
        for y in range(2):
            pack(ysend.at[which, y], 0, [csend.at[which, 2 * x + y] for x in range(2)], 2, width, 6, edge)
        send(which, [(x, y, 0) for x in (-1, 1) for y in (-1, 1)])
        send(which, [(0, -1, 0), (0, 1, 0)])
        send(which, [(0, y, z) for z in (-1, 1) for y in (-1, 0, 1)])
        if between is not None:
            between()
        arrive(which, [(0, y, z) for z in (-1, 1) for y in (-1, 0, 1)])
        arrive(which, [(0, -1, 0), (0, 1, 0)])
        arrive(which, [(x, y, z) for x in (-1, 1) for z in (-1, 1) for y in (-1, 0, 1)])
        yends = move(1, width)[3]
        for z in range(2):
            tiles_y = []
            for y in range(3):
                tile = zrecv[which, 3 * z + y]
                for x in range(2):
                    at = 6 * x + 3 * z + y
                    row = jnp.broadcast_to(rrecv[which, at : at + 1, :], (8, 128))
                    for r in range(layers):
                        here = (sub == r) & ends[x]
                        tile = tile + jnp.where(here, turn(row, tos[x] - gap * r), 0.0)
                tiles_y.append(tile)
            zsum[z] = (
                tiles_y[1]
                + jnp.where(yends[0], turn(tiles_y[0], -8), 0.0)
                + jnp.where(yends[1], turn(tiles_y[2], 8), 0.0)
            )
        arrive(which, [(x, y, 0) for x in (-1, 1) for y in (-1, 1)])
        for y in range(2):
            unpack(yrecv.at[which, y], 0, [crecv.at[which, 2 * x + y] for x in range(2)], 2, width, 6, edge)
        unpack(ref, LEAD, [yrecv.at[which, e] for e in range(2)], 1, width, chunks[1], depth[1])
        arrive(which, [(-1, 0, 0), (1, 0, 0)])
        unpack(ref, LEAD, [xrecv.at[which, e] for e in range(2)], 2, width, chunks[2], depth[2])
        for _, _, low_to, high_to, at in z_rows(width):
            ref[low_to : low_to + 1, :] += zsum[0, at : at + 1, :]
            ref[high_to : high_to + 1, :] += zsum[1, at : at + 1, :]

    def line_copy(which, step):
        return pltpu.make_async_remote_copy(
            src_ref=gmsg.at[which, pl.ds(0, 1)],
            dst_ref=g1.at[which, pl.ds(slot1, 1)],
            send_sem=g1_ss.at[which, step],
            recv_sem=g1_rs.at[which, slot1],
            device_id=line_peer(step),
            device_id_type=MESH,
        )

    def line_start(which, message):
        gmsg[which] = message
        g1[which, pl.ds(slot1, 1), :] = message[0:1, :]
        for step in range(1, nline):
            line_copy(which, step).start()

    def line_arrive(which):
        for step in range(1, nline):
            other = lax.rem(slot1 + step, nline)
            pltpu.make_async_remote_copy(
                src_ref=gmsg.at[which, pl.ds(0, 1)],
                dst_ref=g1.at[which, pl.ds(other, 1)],
                send_sem=g1_ss.at[which, step],
                recv_sem=g1_rs.at[which, other],
                device_id=line_peer(step),
                device_id_type=MESH,
            ).wait_recv()

    def plane_copy(which, step):
        return pltpu.make_async_remote_copy(
            src_ref=g1c.at[which],
            dst_ref=g2.at[which, slot2],
            send_sem=g2_ss.at[which, step],
            recv_sem=g2_rs.at[which, slot2],
            device_id=plane_peer(step),
            device_id_type=MESH,
        )

    def plane_start(which, block):
        g1c[which] = block
        g2[which, pl.ds(slot2, 1)] = block[None]
        for step in range(1, nplane):
            plane_copy(which, step).start()

    def plane_arrive(which):
        for step in range(1, nplane):
            other = lax.rem(slot2 + step, nplane)
            pltpu.make_async_remote_copy(
                src_ref=g1c.at[which],
                dst_ref=g2.at[which, other],
                send_sem=g2_ss.at[which, step],
                recv_sem=g2_rs.at[which, other],
                device_id=plane_peer(step),
                device_id_type=MESH,
            ).wait_recv()

    def moments(ref):
        def one(i, acc):
            r = [ref[pl.ds(base_of(k, i), 8), :] for k in range(3)]
            own = node[pl.ds(tile_at(0, i), 8), :]
            z = xi_z(i)
            parts = r + [xi_y * r[2] - z * r[1], z * r[0] - xi_x * r[2], xi_x * r[1] - xi_y * r[0]]
            out = []
            for g in range(NODES):
                here = own == float(g + 1)
                for m in range(6):
                    out.append(acc[6 * g + m] + jnp.where(here, parts[m], 0.0))
            return tuple(out)

        acc = lax.fori_loop(0, tiles, one, tuple(jnp.zeros((8, 128), F32) for _ in range(MODES)))
        for at in range(MODES):
            rowm[at : at + 1, :] = jnp.sum(acc[at], axis=0, keepdims=True)

    def row_to_lanes():
        return gather_out(jnp.ones((8, 128), jnp.bfloat16), rowm[...])

    turned = lax.rem((gy * ngz + gz) * MODES, 128)

    def own_range(c):
        begin = (sub * ngz + c) * MODES - 128 * sub
        ahead = begin < 128
        first = (lane >= begin) & (lane < begin + MODES)
        second = (lane + 128 >= begin) & (lane + 128 < begin + MODES)
        return first, second

    def coarse_solve(which):
        ranges = [own_range(c) for c in range(ngz)]
        acc = [jnp.zeros((8, 128), F32) for _ in range(5)]
        for y in range(ngx // ZH):
            for h in range(ZH):
                a = y * ZH + h
                got = [g2[which, y * ngz + c, 8 * h : 8 * h + 8, :] for c in range(ngz)]
                main = add_all([jnp.where(ranges[c][0], got[c], 0.0) for c in range(ngz)])
                nxt = add_all([jnp.where(ranges[c][1], got[c], 0.0) for c in range(ngz)])
                cvec[16 * a + 8 : 16 * a + 9, :] = jnp.zeros((1, 128), F32)
                cvec[16 * a : 16 * a + 8, :] = main
                cvec[16 * a + 1 : 16 * a + 9, :] += nxt
        for a in range(ngx):
            for j in range(9):
                row = jnp.broadcast_to(cvec[16 * a + j : 16 * a + j + 1, :], (8, 128))
                col = 128 * (9 * a + j)
                for t in range(4):
                    acc[t] = acc[t] + mat[8 * t : 8 * t + 8, col : col + 128] * row
                acc[4] = acc[4] + jnp.concatenate([mat[32:36, col : col + 128]] * 2, axis=0) * row
        for t in range(5):
            ybuf[8 * t : 8 * t + 8, :] = jnp.broadcast_to(jnp.sum(acc[t], axis=1, keepdims=True), (8, 128))

    def lane_sum(which, at):
        parts = []
        for c in range(ngz):
            pos = lax.rem((sub * ngz + c) * MODES + at, 128)
            here = lane == pos
            for y in range(ngx // ZH):
                for h in range(ZH):
                    parts.append(jnp.where(here, g2[which, y * ngz + c, 8 * h : 8 * h + 8, :], 0.0))
        whole = jnp.sum(add_all(parts), axis=0, keepdims=True)
        return jnp.sum(whole, axis=1, keepdims=True)

    def with_coarse(src, dst):
        def one(i):
            own = node[pl.ds(tile_at(0, i), 8), :]
            grid = gridm[pl.ds(tile_at(0, i), 8), :]
            z = xi_z(i)
            modes = [jnp.zeros((8, 128), F32) for _ in range(6)]
            for g in range(NODES):
                here = own == float(g + 1)
                for m in range(6):
                    at = 6 * g + m
                    modes[m] = jnp.where(here, jnp.broadcast_to(ybuf[at : at + 1, :], (8, 128)), modes[m])
            t, w = modes[:3], modes[3:]
            add = [
                t[0] + (w[1] * z - w[2] * xi_y),
                t[1] + (w[2] * xi_x - w[0] * z),
                t[2] + (w[0] * xi_y - w[1] * xi_x),
            ]
            for k in range(3):
                at = pl.ds(base_of(k, i), 8)
                dst[at, :] = src[at, :] * grid + add[k]

        each_tile(one)

    def spread(ref):
        def one(i):
            s = stiff[pl.ds(tile_at(0, i), 8), :]
            for k in range(3):
                at = pl.ds(base_of(k, i), 8)
                v = ref[at, :]
                w = s * v
                vf[at, :] = v
                wf[at, :] = w
                for x, sy, dy in ((v, syv, dyv), (w, syw, dyw)):
                    ahead, behind = turn(x, -1), turn(x, 1)
                    sy[at, :] = ahead + behind
                    dy[at, :] = ahead - behind

        each_tile(one)

    def couple(u_ref, sy_ref, dy_ref, i):
        def at(ref, k, dz):
            return ref[pl.ds(base_of(k, i) + dz, 8), :]

        up = [at(u_ref, k, 1) for k in range(3)]
        um = [at(u_ref, k, -1) for k in range(3)]
        u = [at(u_ref, k, 0) for k in range(3)]
        s = [up[k] + um[k] for k in range(3)]
        yp = [at(sy_ref, k, 1) for k in range(3)]
        ym = [at(sy_ref, k, -1) for k in range(3)]
        sy = [at(sy_ref, k, 0) for k in range(3)]
        sys = [yp[k] + ym[k] for k in range(3)]
        t_x, t_z = up[0] - um[0], up[2] - um[2]
        ty_x, ty_z = yp[0] - ym[0], yp[2] - ym[2]
        dp = [at(dy_ref, k, 1) for k in range(3)]
        dm = [at(dy_ref, k, -1) for k in range(3)]
        dys_x, dys_y = dp[0] + dm[0], dp[1] + dm[1]
        dyt_y, dyt_z = dp[1] - dm[1], dp[2] - dm[2]
        dy_x, dy_y = at(dy_ref, 0, 0), at(dy_ref, 1, 0)
        e, th, c7 = 0.125, 1.0 / 18.0, 7.0 / 18.0
        still = [
            sy[0] + s[0] + 0.5 * sys[0],
            1.5 * sy[1] + s[1] + 0.625 * sys[1] + e * dyt_z,
            sy[2] + 1.5 * s[2] + 0.625 * sys[2] + e * dyt_y,
        ]
        even = [
            1.5 * u[0] + 0.625 * (sy[0] + s[0]) + c7 * sys[0],
            u[1] + 0.625 * sy[1] + 0.5 * s[1] + c7 * sys[1] + th * dyt_z,
            u[2] + 0.5 * sy[2] + 0.625 * s[2] + c7 * sys[2] + th * dyt_y,
        ]
        odd = [
            e * (dy_y + t_z) + th * (dys_y + ty_z),
            e * dy_x + th * dys_x,
            e * t_x + th * ty_x,
        ]
        return [
            still[k] + (turn(even[k] + odd[k], -STRIDE) + turn(even[k] - odd[k], STRIDE)) for k in range(3)
        ], u

    def image_tile(i):
        here = pl.ds(tile_at(0, i), 8)
        lv, v = couple(vf, syv, dyv, i)
        lw, _ = couple(wf, syw, dyw, i)
        s = stiff[here, :]
        d = [dmat[pl.ds(tile_at(rows * f, i), 8), :] for f in range(6)]
        full = ((0, 3, 4), (3, 1, 5), (4, 5, 2))
        out = []
        for m in range(3):
            diag = d[full[m][0]] * v[0] + d[full[m][1]] * v[1] + d[full[m][2]] * v[2]
            out.append(diag - 0.5 * (s * lv[m] + lw[m]))
        return out, v

    def local_solve(ref, out):
        def first(i):
            for k in range(3):
                at = pl.ds(base_of(k, i), 8)
                out[at, :] = cdiag[pl.ds(tile_at(rows * k, i), 8), :] * ref[at, :]

        each_tile(first)

        def sweep(n, carry):
            spread(out)

            def one(i):
                image, v = image_tile(i)
                for k in range(3):
                    at = pl.ds(base_of(k, i), 8)
                    c = cdiag[pl.ds(tile_at(rows * k, i), 8), :]
                    out[at, :] = v[k] + c * (ref[at, :] - image[k])

            each_tile(one)
            return carry

        lax.fori_loop(0, SWEEPS - 1, sweep, 0)

    def setup_stiffness():
        mix_copy.wait()
        parts = thirds(field[sbase : sbase + srows, :])[::-1]
        for f in range(0, 11, 2):
            wide = 128 * min(2, 11 - f)
            got = add_all([dot(part, mix[:, 128 * f : 128 * f + wide], (1, 0)) for part in parts])
            for g in range(wide // 128):
                mixed[srows * (f + g) : srows * (f + g + 1), :] = got[:, 128 * g : 128 * g + 128]
        count = cz // 2 + 1

        def at(f, shift):
            return mixed[srows * f + shift : srows * f + shift + count, :]

        for parity in range(2):
            here = lambda f: at(f, parity)
            beyond = lambda f: at(f, 1 - parity)
            s_here = here(0)
            stiff[pl.ds(parity, count, stride=2), :] = s_here
            for m in range(6):
                if m < 4:
                    value = (here(1 + m) + here(5 + m) + beyond(5 + m)) * (1.0 / 144.0)
                    if m < 3:
                        value = value + (0.5 * WHOLE) * s_here
                else:
                    tilt = here(5 + m) - beyond(5 + m)
                    value = (tilt if parity == 1 else -tilt) * (1.0 / 144.0)
                dmat[pl.ds(rows * m + parity, count, stride=2), :] = value

        def one(i):
            for k in range(3):
                part = pl.ds(tile_at(rows * k, i), 8)
                d = dmat[part, :]
                live = d > 0.0
                cdiag[part, :] = jnp.where(live, RELAX / jnp.where(live, d, 1.0), 0.0)

        each_tile(one)

    moments(field)
    first_row = turn_by(row_to_lanes(), turned)
    greeters = nline - 1 + nplane - 1
    for has, _ in sides.values():
        greeters = greeters + jnp.where(has, 1, 0)
    pl.semaphore_wait(barrier, greeters)

    def forward(which, row):
        def run():
            line_start(which, row)
            line_arrive(which)
            plane_start(which, g1[which])

        return run

    exchange(field, 0, 1, forward(0, first_row))
    setup_stiffness()
    local_solve(field, pfield)
    mat_copy.wait()
    plane_arrive(0)
    coarse_solve(0)
    with_coarse(pfield, zfield)
    exchange(zfield, 1, 2)

    spread(zfield)

    def image_and_sums(dst, first, second):
        def one(i, acc):
            image, v = image_tile(i)
            own = node[pl.ds(tile_at(0, i), 8), :] > 0.0
            acc = list(acc)
            for k in range(3):
                at = pl.ds(base_of(k, i), 8)
                mine = jnp.where(own, image[k], 0.0)
                dst[at, :] = mine
                acc[0] = acc[0] + first[at, :] * v[k]
                acc[1] = acc[1] + v[k] * mine
                if second is not None:
                    acc[2] = acc[2] + second[at, :] * v[k]
            return tuple(acc)

        count = 2 if second is None else 3
        acc = lax.fori_loop(0, tiles, one, tuple(jnp.zeros((8, 128), F32) for _ in range(count)))
        return [jnp.sum(a, axis=0, keepdims=True) for a in acc]

    sums = image_and_sums(qfield, rfield, None)
    moments(qfield)
    rowm[MODES : MODES + 1, :] = sums[0]
    rowm[MODES + 1 : MODES + 2, :] = sums[1]
    second_row = turn_by(row_to_lanes(), turned)

    for k in range(3):
        field[LEAD + rows * k : LEAD + rows * (k + 1), :] = qfield[LEAD + rows * k : LEAD + rows * (k + 1), :]
    exchange(field, 2, 1, forward(1, second_row))
    local_solve(field, pfield)
    plane_arrive(1)
    coarse_solve(1)
    rho0 = lane_sum(1, MODES)
    curve0 = lane_sum(1, MODES + 1)
    alpha0 = rho0 / curve0
    with_coarse(pfield, field)
    exchange(field, 3, 2)

    def renew(i):
        for k in range(3):
            at = pl.ds(base_of(k, i), 8)
            field[at, :] = zfield[at, :] - alpha0 * field[at, :]
            rfield[at, :] = rfield[at, :] - alpha0 * qfield[at, :]

    each_tile(renew)
    spread(field)

    sums = image_and_sums(pfield, rfield, qfield)
    rowm[0:MODES, :] = jnp.zeros((MODES, 128), F32)
    for at in range(3):
        rowm[MODES + at : MODES + at + 1, :] = sums[at]
    line_start(2, turn_by(row_to_lanes(), turned))
    line_arrive(2)
    plane_start(2, g1[2])
    plane_arrive(2)
    rho1 = lane_sum(2, MODES)
    zaz = lane_sum(2, MODES + 1)
    zq = lane_sum(2, MODES + 2)
    beta = rho1 / rho0
    alpha1 = rho1 / (zaz + 2.0 * beta * zq + beta * beta * curve0)

    for k in range(3):
        at = slice(LEAD + k * rows + 1, LEAD + k * rows + 1 + cz)
        z0, z1 = zfield[at, :], field[at, :]
        sol_out[64 * k : 64 * k + 64, :] = gather_out(place[...], alpha0 * z0 + alpha1 * (z1 + beta * z0))
        res_out[64 * k : 64 * k + 64, :] = gather_out(
            place[...], rfield[at, :] - alpha1 * (pfield[at, :] + beta * qfield[at, :])
        )

    for which in range(4):
        left(which)
    for which in range(3):
        for step in range(1, nline):
            line_copy(which, step).wait_send()
        for step in range(1, nplane):
            plane_copy(which, step).wait_send()


def turn_by(x, shift):
    return pltpu.roll(x, shift, 1)


def solution(mesh):
    sizes = (mesh.shape["gx"], mesh.shape["gy"], mesh.shape["gz"])
    nline = ZH * sizes[1]
    nplane = (sizes[0] // ZH) * sizes[2]

    def body(right_side, phase_labels, phase_moduli, coarse_nodes, coarse_inverse):
        cz = right_side.shape[3]
        rows, srows, total = plan(cz)
        tall = pltpu.VMEM((LEAD + total, 128), F32)
        ydeep = max(total // 10, 8 * -(-3 * rows // 40))
        cdeep = 8 * -(-ydeep // 48)
        ydeep = 6 * cdeep
        xdeep = max(total // 10, 8 * -(-3 * rows // 48))
        vmem = pl.BlockSpec(memory_space=pltpu.VMEM)
        away = pl.BlockSpec(memory_space=pl.ANY)
        consts = tables(cz)
        sol, res = pl.pallas_call(
            functools.partial(kernel, sizes, cz),
            out_shape=(jax.ShapeDtypeStruct((192, cz), F32),) * 2,
            in_specs=[
                away,
                away,
                pl.BlockSpec(memory_space=pltpu.SMEM),
                away,
                away,
            ]
            + [away] * len(consts),
            out_specs=(vmem, vmem),
            scratch_shapes=[
                pltpu.VMEM(coarse_inverse.shape, F32),
                pltpu.VMEM((192, cz), F32),
                pltpu.VMEM(phase_labels.shape, jnp.int32),
                pltpu.VMEM((64, cz), jnp.int32),
            ]
            + [pltpu.VMEM(c.shape, c.dtype) for c in consts]
            + [
                pltpu.VMEM((11 * srows + 8, 128), F32),
                tall,
                tall,
                tall,
                tall,
                tall,
                tall,
                tall,
                tall,
                tall,
                tall,
                tall,
                pltpu.VMEM((6 * rows, 128), F32),
                pltpu.VMEM((rows, 128), F32),
                pltpu.VMEM((3 * rows, 128), F32),
                pltpu.VMEM((rows, 128), F32),
                pltpu.VMEM((rows, 128), F32),
                pltpu.VMEM((16, cz // 2), F32),
                pltpu.VMEM((128, 128), F32),
                pltpu.VMEM((40, 128), F32),
                pltpu.VMEM((16 * sizes[0], 128), F32),
                pltpu.VMEM((4, 2, 8, 128), F32),
                pltpu.VMEM((4, 6, 8, 128), F32),
                pltpu.VMEM((4, 2, ydeep, 128), F32),
                pltpu.VMEM((4, 2, ydeep, 128), F32),
                pltpu.VMEM((4, 2, xdeep, 128), F32),
                pltpu.VMEM((4, 2, xdeep, 128), F32),
                pltpu.VMEM((4, 4, cdeep, 128), F32),
                pltpu.VMEM((4, 4, cdeep, 128), F32),
                pltpu.VMEM((4, 4, 8, 128), F32),
                pltpu.VMEM((4, 16, 128), F32),
                pltpu.VMEM((2, 8, 128), F32),
                pltpu.VMEM((3, 8, 128), F32),
                pltpu.VMEM((3, nline, 128), F32),
                pltpu.VMEM((3, nline, 128), F32),
                pltpu.VMEM((3, nplane, nline, 128), F32),
                pltpu.SemaphoreType.DMA((9,)),
                pltpu.SemaphoreType.DMA((4, 27)),
                pltpu.SemaphoreType.DMA((4, 27)),
                pltpu.SemaphoreType.DMA((3, nline)),
                pltpu.SemaphoreType.DMA((3, nline)),
                pltpu.SemaphoreType.DMA((3, nplane)),
                pltpu.SemaphoreType.DMA((3, nplane)),
            ],
            compiler_params=pltpu.CompilerParams(
                collective_id=0, has_side_effects=True, vmem_limit_bytes=67_000_000
            ),
            name="schwarz_cg",
        )(
            right_side.reshape(192, cz),
            phase_labels,
            phase_moduli,
            coarse_nodes.reshape(64, cz),
            coarse_inverse,
            *consts,
        )
        return sol.reshape(right_side.shape), res.reshape(right_side.shape)

    spec = P(None, "gx", "gy", "gz")
    cells = P("gx", "gy", "gz")
    return jax.shard_map(
        body,
        mesh=mesh,
        in_specs=(spec, cells, P(), cells, P(("gx", "gy", "gz"), None)),
        out_specs=(spec, spec),
        check_vma=False,
    )
```

```python
import functools

import jax
import jax.numpy as jnp
import numpy as np
from jax import lax
from jax.experimental import pallas as pl
from jax.experimental.pallas import tpu as pltpu
from jax.sharding import PartitionSpec as P

MESH = pl.DeviceIdType.MESH
HIGH = lax.Precision.HIGHEST
F32 = jnp.float32

RELAX = 0.6
UNROLL = 4
SWEEPS = 4
SIDE = 8
STRIDE = 11
LEAD = 8
ZH = 2
NODES = 6
NEIGHBOURS = [(x, y, z) for x in (-1, 0, 1) for y in (-1, 0, 1) for z in (-1, 0, 1) if (x, y, z) != (0, 0, 0)]
MODES = 36


def bond(d):
    return d[0] * d[0] + d[1] * d[1] + d[2] * d[2]


def coef(m, k, d):
    n = bond(d)
    if n == 0:
        return 0.0
    return (1.0 / n if m == k else 0.0) + 0.5 * d[m] * d[k] / (n * n)


def plan(cz):
    rows = -(-(cz + 3) // 8) * 8
    srows = -(-(cz // 2 + 2) // 8) * 8
    total = -(-(3 * rows + srows) // 80) * 80
    return rows, srows, total


def tables(cz):
    rows, srows, total = plan(cz)
    place = np.zeros((64, 128), np.float32)
    for i in range(SIDE):
        for j in range(SIDE):
            place[i * SIDE + j, STRIDE * (i + 1) + j + 1] = 1.0
    spot = {-1: 0, 0: 1, 1: 2, 2: 3, 3: 8, 4: 9}
    place_blocks = np.zeros((16, 128), np.float32)
    for i in range(4):
        for j in range(4):
            place_blocks[i * 4 + j, STRIDE * spot[i] + spot[j]] = 1.0

    def lane_of(x, y):
        return STRIDE * spot[x // 2] + spot[y // 2]

    pairs = ((0, 0), (1, 1), (2, 2), (0, 1), (0, 2), (1, 2))
    mix = np.zeros((128, 11 * 128))
    for x in range(-1, 9):
        for y in range(-1, 9):
            out = STRIDE * (x + 1) + y + 1
            mix[lane_of(x, y), out] += 1.0
            for at, (m, k) in enumerate(pairs):
                for a in (-1, 0, 1):
                    for b in (-1, 0, 1):
                        src = lane_of(x + a, y + b)
                        if at < 4:
                            mix[src, 128 * (1 + at) + out] += 72.0 * coef(m, k, (a, b, 0))
                        mix[src, 128 * (5 + at) + out] += 72.0 * coef(m, k, (a, b, 1))
    mix = np.round(mix)
    lane = np.arange(128)
    ints = np.zeros((32, 128), np.int32)
    ints[0:8] = np.where(lane < 110, lane // STRIDE, 99)
    ints[8:16] = np.where(lane < 110, lane % STRIDE, 99)
    ints[16:24] = np.where(lane < 126, lane // 21, 99)
    ints[24:32] = np.where(lane < 126, lane % 21 % STRIDE, 99)
    floats = np.zeros((16, 128), np.float32)
    floats[0:8] = (2.0 * (lane // STRIDE - 1) + 1.0) / SIDE - 1.0
    floats[8:16] = (2.0 * (lane % STRIDE - 1) + 1.0) / SIDE - 1.0
    half = lambda a: jnp.asarray(a, jnp.bfloat16)
    return half(place), half(place_blocks), half(mix), jnp.asarray(ints), jnp.asarray(floats)


WHOLE = sum(coef(0, 0, (a, b, c)) for a in (-1, 0, 1) for b in (-1, 0, 1) for c in (-1, 0, 1))


def thirds(x):
    high = x.astype(jnp.bfloat16)
    rest = x - high.astype(F32)
    middle = rest.astype(jnp.bfloat16)
    return high, middle, (rest - middle.astype(F32)).astype(jnp.bfloat16)


def turn(x, shift):
    shift = shift % 128
    return x if shift == 0 else pltpu.roll(x, shift, 1)


def add_all(items):
    items = list(items)
    while len(items) > 1:
        items = [
            items[i] + items[i + 1] if i + 1 < len(items) else items[i] for i in range(0, len(items), 2)
        ]
    return items[0]


def kernel(
    sizes,
    cz,
    rhs_hbm,
    labels_hbm,
    moduli,
    nodes_hbm,
    inverse,
    place_hbm,
    place_blocks_hbm,
    mix_hbm,
    ints_hbm,
    floats_hbm,
    sol_out,
    res_out,
    mat,
    rhs,
    labels,
    nodes_in,
    place,
    place_blocks,
    mix,
    ints,
    floats,
    mixed,
    field,
    zfield,
    qfield,
    rfield,
    pfield,
    set_a,
    set_b,
    dmat,
    stiff,
    cdiag,
    node,
    gridm,
    stage,
    rowm,
    ybuf,
    cvec,
    zsend,
    zrecv,
    ysend,
    yrecv,
    xsend,
    xrecv,
    csend,
    crecv,
    rsend,
    rrecv,
    zsum,
    outs,
    gmsg,
    g1,
    g1c,
    g2,
    load_sem,
    halo_ss,
    halo_rs,
    g1_ss,
    g1_rs,
    g2_ss,
    g2_rs,
):
    ngx, ngy, ngz = sizes
    rows, srows, total = plan(cz)
    tiles = rows // 8
    sbase = LEAD + 3 * rows
    gx, gy, gz = lax.axis_index("gx"), lax.axis_index("gy"), lax.axis_index("gz")
    zhi, yhi = lax.rem(gx, ZH), lax.div(gx, ZH)
    nline = ZH * ngy
    nplane = (ngx // ZH) * ngz
    slot1 = zhi * ngy + gy
    slot2 = yhi * ngz + gz

    def line_peer(step):
        other = lax.rem(slot1 + step, nline)
        return (yhi * ZH + lax.div(other, ngy), lax.rem(other, ngy), gz)

    def plane_peer(step):
        other = lax.rem(slot2 + step, nplane)
        return (lax.div(other, ngz) * ZH + zhi, gy, lax.rem(other, ngz))

    sides = {}
    for d in NEIGHBOURS:
        has = None
        for way, at, count in zip(d, (gx, gy, gz), sizes):
            if way != 0:
                one = at > 0 if way < 0 else at < count - 1
                has = one if has is None else has & one
        sides[d] = (has, (gx + d[0], gy + d[1], gz + d[2]))

    loads = [
        pltpu.make_async_copy(src, dst, load_sem.at[at])
        for at, (src, dst) in enumerate(
            (
                (rhs_hbm, rhs),
                (nodes_hbm, nodes_in),
                (labels_hbm, labels),
                (place_hbm, place),
                (place_blocks_hbm, place_blocks),
                (ints_hbm, ints),
                (floats_hbm, floats),
                (mix_hbm, mix),
                (inverse, mat),
            )
        )
    ]
    for load in loads:
        load.start()
    mat_copy, mix_copy = loads[-1], loads[-2]

    barrier = pltpu.get_barrier_semaphore()
    for has, device in [sides[d] for d in sorted(NEIGHBOURS, key=lambda d: -abs(d[0]))]:

        @pl.when(has)
        def _(device=device):
            pl.semaphore_signal(barrier, inc=1, device_id=device, device_id_type=MESH)

    for step in range(1, nline):
        pl.semaphore_signal(barrier, inc=1, device_id=line_peer(step), device_id_type=MESH)
    for step in range(1, nplane):
        pl.semaphore_signal(barrier, inc=1, device_id=plane_peer(step), device_id_type=MESH)


    lane = lax.broadcasted_iota(jnp.int32, (8, 128), 1)
    sub = lax.broadcasted_iota(jnp.int32, (8, 128), 0)

    def base_of(k, i):
        return tile_at(LEAD + k * rows, i)

    def tile_at(first, i):
        return first + 8 * i if isinstance(i, int) else pl.multiple_of(first + 8 * i, 8)

    def each_tile(one, unroll=4):
        whole = tiles // unroll

        def some(n, carry):
            for j in range(unroll):
                one(n * unroll + j)
            return carry

        lax.fori_loop(0, whole, some, 0)
        for i in range(whole * unroll, tiles):
            one(i)

    def xi_z(i):
        along = (sub + (8 * i - 1)).astype(F32)
        return (2.0 * along + 1.0) / cz - 1.0

    def deep(axis, width):
        if width == 1:
            return total // 10
        return 8 * -(-3 * rows // (40 if axis == 1 else 48))

    def edge_chunks(width):
        return 6 if width == 1 else 5

    def edge_deep(width):
        return 8 * -(-deep(2, width) // (8 * edge_chunks(width)))

    def inbox(which, d):
        x, y, z = d
        width = 1 + which % 2
        if z != 0:
            if x == 0:
                return zrecv.at[which, 3 * (z > 0) + y + 1]
            at = 6 * (x > 0) + 3 * (z > 0) + y + 1
            return rrecv.at[which, at : at + 1]
        if x != 0 and y != 0:
            return crecv.at[which, 2 * (x > 0) + (y > 0), 0 : edge_deep(width)]
        if y != 0:
            return yrecv.at[which, int(y > 0), 0 : deep(1, width)]
        return xrecv.at[which, int(x > 0), 0 : deep(2, width)]

    def outbox(which, d):
        x, y, z = d
        width = 1 + which % 2
        if z != 0:
            if x == 0:
                return zsend.at[which, int(z > 0)]
            at = 2 * (x > 0) + (z > 0)
            return rsend.at[which, at, 0:1]
        if x != 0 and y != 0:
            return csend.at[which, 2 * (x > 0) + (y > 0), 0 : edge_deep(width)]
        if y != 0:
            return ysend.at[which, int(y > 0), 0 : deep(1, width)]
        return xsend.at[which, int(x > 0), 0 : deep(2, width)]

    for f in range(6):
        dmat[rows * f + cz + 2 : rows * (f + 1), :] = jnp.zeros((rows - cz - 2, 128), F32)
    stiff[cz + 2 : rows, :] = jnp.zeros((rows - cz - 2, 128), F32)
    for ref in (field, rfield):
        ref[...] = jnp.zeros(ref.shape, F32)
    zfield[sbase:, :] = jnp.zeros((LEAD + total - sbase, 128), F32)
    for ref in set_a + set_b:
        ref[0:LEAD, :] = jnp.zeros((LEAD, 128), F32)
        ref[LEAD + 3 * rows : LEAD + 3 * rows + 8, :] = jnp.zeros((8, 128), F32)
    node[...] = jnp.zeros(node.shape, F32)
    rowm[...] = jnp.zeros(rowm.shape, F32)
    for ref in (zsend, xsend):
        ref[...] = jnp.zeros(ref.shape, F32)
    for t in range(4):
        for e in range(2):
            end = deep(2, 1 + t % 2)
            xrecv[t, e, end:, :] = jnp.zeros((xrecv.shape[2] - end, 128), F32)
    cvec[...] = jnp.zeros(cvec.shape, F32)
    stage[...] = jnp.zeros(stage.shape, F32)
    for d in NEIGHBOURS:

        @pl.when(jnp.logical_not(sides[d][0]))
        def _(d=d):
            for t in range(4):
                ref = inbox(t, d)
                ref[...] = jnp.zeros(ref.shape, F32)

    for load in loads[:-2]:
        load.wait()
    lane_x, lane_y, lane_c = ints[0:8, :], ints[8:16, :], ints[16:24, :]
    lane_e = ints[24:32, :]
    xi_x, xi_y = floats[0:8, :], floats[8:16, :]

    def dot(a, b, dims):
        return lax.dot_general(a, b, ((dims[:1], dims[1:]), ((), ())), preferred_element_type=F32)

    def spread_in(x):
        return add_all([dot(part, place[...], (0, 0)) for part in thirds(x)[::-1]])

    def gather_out(select, x):
        return add_all([dot(select, part, (1, 1)) for part in thirds(x)[::-1]])

    for k in range(3):
        piece = spread_in(rhs[64 * k : 64 * k + 64, :])
        first = LEAD + k * rows + 1
        field[first : first + cz, :] = piece
        rfield[first : first + cz, :] = piece
    node[1 : 1 + cz, :] = dot((nodes_in[...].astype(F32) + 1.0).astype(jnp.bfloat16), place[...], (0, 0))
    for i in range(4):
        stage[4 * i : 4 * i + 4, :] = labels[i].astype(F32) + 1.0
    phases = dot(stage[...].astype(jnp.bfloat16), place_blocks[...], (0, 0))
    blocks = jnp.zeros(phases.shape, F32)
    for phase in range(moduli.shape[0]):
        blocks = jnp.where(phases == float(phase + 1), moduli[phase], blocks)
    field[sbase + 1 : sbase + 1 + cz // 2, :] = blocks

    bad_lane = (
        ((gx == 0) & (lane_x == 0))
        | ((gx == ngx - 1) & (lane_x == 9))
        | ((gy == 0) & (lane_y == 0))
        | ((gy == ngy - 1) & (lane_y == 9))
        | (lane_x > 9)
        | (lane_y > 9)
    )
    low = jnp.where(gz == 0, 1, 0)
    high = jnp.where(gz == ngz - 1, cz + 1, cz + 2)

    def grid_tile(i):
        r = sub + 8 * i
        gridm[pl.ds(tile_at(0, i), 8), :] = jnp.where(bad_lane | (r < low) | (r >= high), 0.0, 1.0)

    each_tile(grid_tile)

    def number(d):
        return 9 * (d[0] + 1) + 3 * (d[1] + 1) + d[2] + 1

    def opposite(d):
        return (-d[0], -d[1], -d[2])

    def halo(which, d):
        return pltpu.make_async_remote_copy(
            src_ref=outbox(which, d),
            dst_ref=inbox(which, opposite(d)),
            send_sem=halo_ss.at[which, number(d)],
            recv_sem=halo_rs.at[which, number(opposite(d))],
            device_id=sides[d][1],
            device_id_type=MESH,
        )

    def send(which, group):
        for d in group:

            @pl.when(sides[d][0])
            def _(d=d):
                halo(which, d).start()

    def arrive(which, group):
        for d in group:

            @pl.when(sides[d][0])
            def _(d=d):
                pltpu.make_async_remote_copy(
                    src_ref=outbox(which, d),
                    dst_ref=inbox(which, d),
                    send_sem=halo_ss.at[which, number(d)],
                    recv_sem=halo_rs.at[which, number(d)],
                    device_id=sides[d][1],
                    device_id_type=MESH,
                ).wait_recv()

    def left(which):
        for d in NEIGHBOURS:

            @pl.when(sides[d][0])
            def _(d=d):
                halo(which, d).wait_send()

    def z_rows(width):
        if width == 1:
            got = [(LEAD + k * rows, cz, k) for k in range(3)] + [(sbase, cz // 2, 3)]
            return [(r + n, r + 1, r, r + n + 1, at) for r, n, at in got]
        out = []
        for k in range(3):
            for layer in range(2):
                r = LEAD + k * rows + layer
                out.append((r + cz, r, r, r + cz, 2 * k + layer))
        return out

    def groups(axis, width, along=None):
        if axis == 1:
            along = lane_y if along is None else along
            if width == 1:
                return 10, [along == k for k in range(10)]
            return 5, [(along == 2 * k) | (along == 2 * k + 1) for k in range(5)]
        if width == 1:
            return 10, [lane_x == k for k in range(10)]
        return 6, [lane_c == k for k in range(6)]

    def move(axis, width, along=None):
        if axis == 1:
            along = lane_y if along is None else along
            if width == 1:
                return 1, (1, 8), (0, 9), (along == 0, along == 9)
            return 2, (0, 8), (0, 8), (along < 2, (along == 8) | (along == 9))
        if width == 1:
            return STRIDE, (STRIDE, 8 * STRIDE), (0, 9 * STRIDE), (lane_x == 0, lane_x == 9)
        return 21, (0, 88), (0, 88), (lane < 21, (lane >= 88) & (lane < 109))

    def pack(src, first, dsts, axis, width, chunks, depth, along=None):
        gap, froms, _, _ = move(axis, width)
        masks = groups(axis, width, along)[1]

        def one(t, carry):
            low, high = jnp.zeros((8, 128), F32), jnp.zeros((8, 128), F32)
            for k in range(chunks):
                tile = src[pl.ds(pl.multiple_of(first + 8 * (k * depth + t), 8), 8), :]
                low = jnp.where(masks[k], turn(tile, gap * k - froms[0]), low)
                high = jnp.where(masks[k], turn(tile, gap * k - froms[1]), high)
            at = pl.ds(pl.multiple_of(8 * t, 8), 8)
            dsts[0][at, :] = low
            dsts[1][at, :] = high
            return carry

        lax.fori_loop(0, depth, one, 0)

    def unpack(dst, first, srcs, axis, width, chunks, depth, along=None):
        gap, _, tos, ends = move(axis, width, along)

        def one(t, carry):
            at = pl.ds(pl.multiple_of(8 * t, 8), 8)
            low, high = srcs[0][at, :], srcs[1][at, :]
            for k in range(chunks):
                part = pl.ds(pl.multiple_of(first + 8 * (k * depth + t), 8), 8)
                tile = dst[part, :]
                tile = tile + jnp.where(ends[0], turn(low, tos[0] - gap * k), 0.0)
                tile = tile + jnp.where(ends[1], turn(high, tos[1] - gap * k), 0.0)
                dst[part, :] = tile
            return carry

        lax.fori_loop(0, depth, one, 0)

    far_rows = [(x, y, z) for x in (-1, 1) for z in (-1, 1) for y in (-1, 0, 1)]
    near_layers = [(0, y, z) for z in (-1, 1) for y in (-1, 0, 1)]
    edges = [(x, y, 0) for x in (-1, 1) for y in (-1, 1)]

    def exchange(ref, which, width, early=None, late=None):
        chunks = [None, groups(1, width)[0], groups(2, width)[0]]
        depth = [None, deep(1, width) // 8, deep(2, width) // 8]
        edge, edge_parts = edge_deep(width) // 8, edge_chunks(width)
        along = lane_y if width == 1 else lane_e
        gap, froms, tos, ends = move(2, width)
        layers = 4 if width == 1 else 6
        pack(ref, LEAD, [xsend.at[which, e] for e in range(2)], 2, width, chunks[2], depth[2])
        send(which, [(-1, 0, 0), (1, 0, 0)])
        for x in range(2):
            pack(
                xsend.at[which, x],
                0,
                [csend.at[which, 2 * x + y] for y in range(2)],
                1,
                width,
                edge_parts,
                edge,
                along,
            )
        send(which, edges)
        for up_from, down_from, _, _, at in z_rows(width):
            zsend[which, 0, at : at + 1, :] = ref[down_from : down_from + 1, :]
            zsend[which, 1, at : at + 1, :] = ref[up_from : up_from + 1, :]
        mine = [(sub == r) & (lane >= gap * r) & (lane < gap * r + gap) for r in range(layers)]
        for z in range(2):
            tile = zsend[which, z]
            for x in range(2):
                row = jnp.zeros((8, 128), F32)
                for r in range(layers):
                    row = jnp.where(mine[r], turn(tile, gap * r - froms[x]), row)
                rsend[which, 2 * x + z, 0:1, :] = jnp.sum(row, axis=0, keepdims=True)
        send(which, far_rows)
        pack(ref, LEAD, [ysend.at[which, e] for e in range(2)], 1, width, chunks[1], depth[1])
        send(which, [(0, -1, 0), (0, 1, 0)])
        send(which, near_layers)
        if early is not None:
            early()
        arrive(which, [(0, -1, 0), (0, 1, 0)])
        unpack(ref, LEAD, [yrecv.at[which, e] for e in range(2)], 1, width, chunks[1], depth[1])
        if late is not None:
            late()
        arrive(which, near_layers)
        arrive(which, far_rows)
        yends = move(1, width)[3]
        for z in range(2):
            tiles_y = []
            for y in range(3):
                tile = zrecv[which, 3 * z + y]
                for x in range(2):
                    at = 6 * x + 3 * z + y
                    row = jnp.broadcast_to(rrecv[which, at : at + 1, :], (8, 128))
                    for r in range(layers):
                        here = (sub == r) & ends[x]
                        tile = tile + jnp.where(here, turn(row, tos[x] - gap * r), 0.0)
                tiles_y.append(tile)
            zsum[z] = (
                tiles_y[1]
                + jnp.where(yends[0], turn(tiles_y[0], -8), 0.0)
                + jnp.where(yends[1], turn(tiles_y[2], 8), 0.0)
            )
        for _, _, low_to, high_to, at in z_rows(width):
            ref[low_to : low_to + 1, :] += zsum[0, at : at + 1, :]
            ref[high_to : high_to + 1, :] += zsum[1, at : at + 1, :]
        arrive(which, [(-1, 0, 0), (1, 0, 0)])
        arrive(which, edges)
        for x in range(2):
            unpack(
                xrecv.at[which, x],
                0,
                [crecv.at[which, 2 * x + y] for y in range(2)],
                1,
                width,
                edge_parts,
                edge,
                along,
            )
        unpack(ref, LEAD, [xrecv.at[which, e] for e in range(2)], 2, width, chunks[2], depth[2])

    def line_copy(which, step):
        return pltpu.make_async_remote_copy(
            src_ref=gmsg.at[which, pl.ds(0, 1)],
            dst_ref=g1.at[which, pl.ds(slot1, 1)],
            send_sem=g1_ss.at[which, step],
            recv_sem=g1_rs.at[which, slot1],
            device_id=line_peer(step),
            device_id_type=MESH,
        )

    def line_start(which, message):
        gmsg[which] = message
        g1[which, pl.ds(slot1, 1), :] = message[0:1, :]
        for step in range(1, nline):
            line_copy(which, step).start()

    def line_arrive(which):
        for step in range(1, nline):
            other = lax.rem(slot1 + step, nline)
            pltpu.make_async_remote_copy(
                src_ref=gmsg.at[which, pl.ds(0, 1)],
                dst_ref=g1.at[which, pl.ds(other, 1)],
                send_sem=g1_ss.at[which, step],
                recv_sem=g1_rs.at[which, other],
                device_id=line_peer(step),
                device_id_type=MESH,
            ).wait_recv()

    def plane_rows(which):
        return nline if which < 2 else 8

    def plane_copy(which, step):
        return pltpu.make_async_remote_copy(
            src_ref=g1c.at[which, 0 : plane_rows(which)],
            dst_ref=g2.at[which, slot2, 0 : plane_rows(which)],
            send_sem=g2_ss.at[which, step],
            recv_sem=g2_rs.at[which, slot2],
            device_id=plane_peer(step),
            device_id_type=MESH,
        )

    def plane_start(which, block):
        g1c[which] = block
        g2[which, pl.ds(slot2, 1)] = block[None]
        for step in range(1, nplane):
            plane_copy(which, step).start()

    def plane_arrive(which):
        for step in range(1, nplane):
            other = lax.rem(slot2 + step, nplane)
            pltpu.make_async_remote_copy(
                src_ref=g1c.at[which, 0 : plane_rows(which)],
                dst_ref=g2.at[which, other, 0 : plane_rows(which)],
                send_sem=g2_ss.at[which, step],
                recv_sem=g2_rs.at[which, other],
                device_id=plane_peer(step),
                device_id_type=MESH,
            ).wait_recv()

    def moments(ref):
        def one(i, acc):
            r = [ref[pl.ds(base_of(k, i), 8), :] for k in range(3)]
            own = node[pl.ds(tile_at(0, i), 8), :]
            z = xi_z(i)
            parts = r + [xi_y * r[2] - z * r[1], z * r[0] - xi_x * r[2], xi_x * r[1] - xi_y * r[0]]
            out = []
            for g in range(NODES):
                here = own == float(g + 1)
                for m in range(6):
                    out.append(acc[6 * g + m] + jnp.where(here, parts[m], 0.0))
            return tuple(out)

        acc = lax.fori_loop(0, tiles, one, tuple(jnp.zeros((8, 128), F32) for _ in range(MODES)))
        for at in range(MODES):
            rowm[at : at + 1, :] = jnp.sum(acc[at], axis=0, keepdims=True)

    def row_to_lanes():
        return gather_out(jnp.ones((8, 128), jnp.bfloat16), rowm[...])

    turned = lax.rem((gy * ngz + gz) * MODES, 128)

    def own_range(c):
        begin = (sub * ngz + c) * MODES - 128 * sub
        ahead = begin < 128
        first = (lane >= begin) & (lane < begin + MODES)
        second = (lane + 128 >= begin) & (lane + 128 < begin + MODES)
        return first, second

    def coarse_solve(which):
        ranges = [own_range(c) for c in range(ngz)]
        acc = [jnp.zeros((8, 128), F32) for _ in range(5)]
        for y in range(ngx // ZH):
            for h in range(ZH):
                a = y * ZH + h
                got = [g2[which, y * ngz + c, 8 * h : 8 * h + 8, :] for c in range(ngz)]
                main = add_all([jnp.where(ranges[c][0], got[c], 0.0) for c in range(ngz)])
                nxt = add_all([jnp.where(ranges[c][1], got[c], 0.0) for c in range(ngz)])
                cvec[16 * a + 8 : 16 * a + 9, :] = jnp.zeros((1, 128), F32)
                cvec[16 * a : 16 * a + 8, :] = main
                cvec[16 * a + 1 : 16 * a + 9, :] += nxt
        for a in range(ngx):
            for j in range(9):
                row = jnp.broadcast_to(cvec[16 * a + j : 16 * a + j + 1, :], (8, 128))
                col = 128 * (9 * a + j)
                for t in range(4):
                    acc[t] = acc[t] + mat[8 * t : 8 * t + 8, col : col + 128] * row
                acc[4] = acc[4] + jnp.concatenate([mat[32:36, col : col + 128]] * 2, axis=0) * row
        for t in range(5):
            ybuf[8 * t : 8 * t + 8, :] = jnp.broadcast_to(jnp.sum(acc[t], axis=1, keepdims=True), (8, 128))

    def lane_sum(which, at):
        parts = []
        for c in range(ngz):
            pos = lax.rem((sub * ngz + c) * MODES + at, 128)
            here = lane == pos
            for y in range(ngx // ZH):
                for h in range(ZH):
                    parts.append(jnp.where(here, g2[which, y * ngz + c, 8 * h : 8 * h + 8, :], 0.0))
        whole = jnp.sum(add_all(parts), axis=0, keepdims=True)
        return jnp.sum(whole, axis=1, keepdims=True)

    def with_coarse(src, dst):
        def one(i):
            own = node[pl.ds(tile_at(0, i), 8), :]
            grid = gridm[pl.ds(tile_at(0, i), 8), :]
            z = xi_z(i)
            modes = [jnp.zeros((8, 128), F32) for _ in range(6)]
            for g in range(NODES):
                here = own == float(g + 1)
                for m in range(6):
                    at = 6 * g + m
                    modes[m] = jnp.where(here, jnp.broadcast_to(ybuf[at : at + 1, :], (8, 128)), modes[m])
            t, w = modes[:3], modes[3:]
            add = [
                t[0] + (w[1] * z - w[2] * xi_y),
                t[1] + (w[2] * xi_x - w[0] * z),
                t[2] + (w[0] * xi_y - w[1] * xi_x),
            ]
            for k in range(3):
                at = pl.ds(base_of(k, i), 8)
                dst[at, :] = src[at, :] * grid + add[k]

        each_tile(one)

    def spread_tile(i, values, bufs):
        vf, wf, syv, dyv, syw, dyw = bufs
        s = stiff[pl.ds(tile_at(0, i), 8), :]
        for k in range(3):
            at = pl.ds(base_of(k, i), 8)
            v = values[k]
            w = s * v
            vf[at, :] = v
            wf[at, :] = w
            for x, sy, dy in ((v, syv, dyv), (w, syw, dyw)):
                ahead, behind = turn(x, -1), turn(x, 1)
                sy[at, :] = ahead + behind
                dy[at, :] = ahead - behind

    def spread(ref):
        each_tile(lambda i: spread_tile(i, [ref[pl.ds(base_of(k, i), 8), :] for k in range(3)], set_a))

    def couple(u_ref, sy_ref, dy_ref, i):
        def at(ref, k, dz):
            return ref[pl.ds(base_of(k, i) + dz, 8), :]

        up = [at(u_ref, k, 1) for k in range(3)]
        um = [at(u_ref, k, -1) for k in range(3)]
        u = [at(u_ref, k, 0) for k in range(3)]
        s = [up[k] + um[k] for k in range(3)]
        yp = [at(sy_ref, k, 1) for k in range(3)]
        ym = [at(sy_ref, k, -1) for k in range(3)]
        sy = [at(sy_ref, k, 0) for k in range(3)]
        sys = [yp[k] + ym[k] for k in range(3)]
        t_x, t_z = up[0] - um[0], up[2] - um[2]
        ty_x, ty_z = yp[0] - ym[0], yp[2] - ym[2]
        dp = [at(dy_ref, k, 1) for k in range(3)]
        dm = [at(dy_ref, k, -1) for k in range(3)]
        dys_x, dys_y = dp[0] + dm[0], dp[1] + dm[1]
        dyt_y, dyt_z = dp[1] - dm[1], dp[2] - dm[2]
        dy_x, dy_y = at(dy_ref, 0, 0), at(dy_ref, 1, 0)
        e, th, c7 = 0.125, 1.0 / 18.0, 7.0 / 18.0
        still = [
            sy[0] + s[0] + 0.5 * sys[0],
            1.5 * sy[1] + s[1] + 0.625 * sys[1] + e * dyt_z,
            sy[2] + 1.5 * s[2] + 0.625 * sys[2] + e * dyt_y,
        ]
        even = [
            1.5 * u[0] + 0.625 * (sy[0] + s[0]) + c7 * sys[0],
            u[1] + 0.625 * sy[1] + 0.5 * s[1] + c7 * sys[1] + th * dyt_z,
            u[2] + 0.5 * sy[2] + 0.625 * s[2] + c7 * sys[2] + th * dyt_y,
        ]
        odd = [
            e * (dy_y + t_z) + th * (dys_y + ty_z),
            e * dy_x + th * dys_x,
            e * t_x + th * ty_x,
        ]
        return [
            still[k] + (turn(even[k] + odd[k], -STRIDE) + turn(even[k] - odd[k], STRIDE)) for k in range(3)
        ], u

    def image_tile(i, bufs):
        vf, wf, syv, dyv, syw, dyw = bufs
        here = pl.ds(tile_at(0, i), 8)
        lv, v = couple(vf, syv, dyv, i)
        lw, _ = couple(wf, syw, dyw, i)
        s = stiff[here, :]
        d = [dmat[pl.ds(tile_at(rows * f, i), 8), :] for f in range(6)]
        full = ((0, 3, 4), (3, 1, 5), (4, 5, 2))
        out = []
        for m in range(3):
            diag = d[full[m][0]] * v[0] + d[full[m][1]] * v[1] + d[full[m][2]] * v[2]
            out.append(diag - 0.5 * (s * lv[m] + lw[m]))
        return out, v

    def local_solve(ref, out):
        def first(i):
            spread_tile(
                i,
                [cdiag[pl.ds(tile_at(rows * k, i), 8), :] * ref[pl.ds(base_of(k, i), 8), :] for k in range(3)],
                set_a,
            )

        each_tile(first)
        bufs = [set_a, set_b]
        for sweep in range(SWEEPS - 1):

            def one(i, sweep=sweep):
                image, v = image_tile(i, bufs[sweep % 2])
                new = []
                for k in range(3):
                    c = cdiag[pl.ds(tile_at(rows * k, i), 8), :]
                    new.append(v[k] + c * (ref[pl.ds(base_of(k, i), 8), :] - image[k]))
                if sweep < SWEEPS - 2:
                    spread_tile(i, new, bufs[(sweep + 1) % 2])
                else:
                    for k in range(3):
                        out[pl.ds(base_of(k, i), 8), :] = new[k]

            each_tile(one, UNROLL)

    def setup_stiffness():
        mix_copy.wait()
        parts = thirds(field[sbase : sbase + srows, :])[::-1]
        for f in range(0, 11, 2):
            wide = 128 * min(2, 11 - f)
            got = add_all([dot(part, mix[:, 128 * f : 128 * f + wide], (1, 0)) for part in parts])
            for g in range(wide // 128):
                mixed[srows * (f + g) : srows * (f + g + 1), :] = got[:, 128 * g : 128 * g + 128]
        count = cz // 2 + 1

        def at(f, shift):
            return mixed[srows * f + shift : srows * f + shift + count, :]

        for parity in range(2):
            here = lambda f: at(f, parity)
            beyond = lambda f: at(f, 1 - parity)
            s_here = here(0)
            stiff[pl.ds(parity, count, stride=2), :] = s_here
            for m in range(6):
                if m < 4:
                    value = (here(1 + m) + here(5 + m) + beyond(5 + m)) * (1.0 / 144.0)
                    if m < 3:
                        value = value + (0.5 * WHOLE) * s_here
                else:
                    tilt = here(5 + m) - beyond(5 + m)
                    value = (tilt if parity == 1 else -tilt) * (1.0 / 144.0)
                dmat[pl.ds(rows * m + parity, count, stride=2), :] = value

        def one(i):
            for k in range(3):
                part = pl.ds(tile_at(rows * k, i), 8)
                d = dmat[part, :]
                live = d > 0.0
                cdiag[part, :] = jnp.where(live, RELAX / jnp.where(live, d, 1.0), 0.0)

        each_tile(one)

    def first_row():
        moments(field)
        return turn_by(row_to_lanes(), turned)

    greeters = nline - 1 + nplane - 1
    for has, _ in sides.values():
        greeters = greeters + jnp.where(has, 1, 0)
    pl.semaphore_wait(barrier, greeters)

    def forward(which):
        line_arrive(which)
        plane_start(which, g1[which])

    exchange(field, 0, 1, lambda: line_start(0, first_row()), lambda: forward(0))
    setup_stiffness()
    local_solve(field, pfield)
    mat_copy.wait()
    plane_arrive(0)
    coarse_solve(0)
    with_coarse(pfield, zfield)
    exchange(zfield, 1, 2)

    spread(zfield)

    def image_and_sums(dsts, first, second):
        def one(i, acc):
            image, v = image_tile(i, set_a)
            own = node[pl.ds(tile_at(0, i), 8), :] > 0.0
            acc = list(acc)
            for k in range(3):
                at = pl.ds(base_of(k, i), 8)
                mine = jnp.where(own, image[k], 0.0)
                for dst in dsts:
                    dst[at, :] = mine
                acc[0] = acc[0] + first[at, :] * v[k]
                acc[1] = acc[1] + v[k] * mine
                if second is not None:
                    acc[2] = acc[2] + second[at, :] * v[k]
            return tuple(acc)

        count = 2 if second is None else 3
        acc = lax.fori_loop(0, tiles, one, tuple(jnp.zeros((8, 128), F32) for _ in range(count)))
        return [jnp.sum(a, axis=0, keepdims=True) for a in acc]

    sums = image_and_sums((qfield, field), rfield, None)
    def second_row():
        moments(qfield)
        rowm[MODES : MODES + 1, :] = sums[0]
        rowm[MODES + 1 : MODES + 2, :] = sums[1]
        return turn_by(row_to_lanes(), turned)

    exchange(field, 2, 1, lambda: line_start(1, second_row()), lambda: forward(1))
    local_solve(field, pfield)
    plane_arrive(1)
    coarse_solve(1)
    rho0 = lane_sum(1, MODES)
    curve0 = lane_sum(1, MODES + 1)
    alpha0 = rho0 / curve0
    with_coarse(pfield, field)
    exchange(field, 3, 2)

    def renew(i):
        for k in range(3):
            at = pl.ds(base_of(k, i), 8)
            field[at, :] = zfield[at, :] - alpha0 * field[at, :]
            rfield[at, :] = rfield[at, :] - alpha0 * qfield[at, :]

    each_tile(renew)
    spread(field)

    sums = image_and_sums((pfield,), rfield, qfield)
    rowm[0:MODES, :] = jnp.zeros((MODES, 128), F32)
    for at in range(3):
        rowm[MODES + at : MODES + at + 1, :] = sums[at]
    line_start(2, row_to_lanes())
    for at, ref in enumerate((zfield, field, rfield, pfield, qfield)):
        for k in range(3):
            first = LEAD + k * rows + 1
            outs[192 * at + 64 * k : 192 * at + 64 * k + 64, :] = gather_out(place[...], ref[first : first + cz, :])
    line_arrive(2)
    plane_start(2, jnp.broadcast_to(jnp.sum(g1[2], axis=0, keepdims=True), (nline, 128)))
    plane_arrive(2)
    last = add_all([g2[2, p, 0:8, :] for p in range(nplane)])[0:1, :]
    rho1, zaz, zq = [
        jnp.sum(jnp.where(lane[0:1, :] == MODES + at, last, 0.0), axis=1, keepdims=True) for at in range(3)
    ]
    beta = rho1 / rho0
    alpha1 = rho1 / (zaz + 2.0 * beta * zq + beta * beta * curve0)

    for i in range(24):
        z0, z1, r1, q1, q0 = [outs[192 * at + 8 * i : 192 * at + 8 * i + 8, :] for at in range(5)]
        sol_out[8 * i : 8 * i + 8, :] = alpha0 * z0 + alpha1 * (z1 + beta * z0)
        res_out[8 * i : 8 * i + 8, :] = r1 - alpha1 * (q1 + beta * q0)

    for which in range(4):
        left(which)
    for which in range(3):
        for step in range(1, nline):
            line_copy(which, step).wait_send()
        for step in range(1, nplane):
            plane_copy(which, step).wait_send()


def turn_by(x, shift):
    return pltpu.roll(x, shift, 1)


def solution(mesh):
    sizes = (mesh.shape["gx"], mesh.shape["gy"], mesh.shape["gz"])
    nline = ZH * sizes[1]
    nplane = (sizes[0] // ZH) * sizes[2]

    def body(right_side, phase_labels, phase_moduli, coarse_nodes, coarse_inverse):
        cz = right_side.shape[3]
        rows, srows, total = plan(cz)
        tall = pltpu.VMEM((LEAD + total, 128), F32)
        ydeep = max(total // 10, 8 * -(-3 * rows // 40))
        cdeep = 16
        xdeep = max(total // 10, 8 * -(-3 * rows // 48))
        xdeep = max(xdeep, 5 * cdeep)
        vmem = pl.BlockSpec(memory_space=pltpu.VMEM)
        away = pl.BlockSpec(memory_space=pl.ANY)
        consts = tables(cz)
        sol, res = pl.pallas_call(
            functools.partial(kernel, sizes, cz),
            out_shape=(jax.ShapeDtypeStruct((192, cz), F32),) * 2,
            in_specs=[
                away,
                away,
                pl.BlockSpec(memory_space=pltpu.SMEM),
                away,
                away,
            ]
            + [away] * len(consts),
            out_specs=(vmem, vmem),
            scratch_shapes=[
                pltpu.VMEM(coarse_inverse.shape, F32),
                pltpu.VMEM((192, cz), F32),
                pltpu.VMEM(phase_labels.shape, jnp.int32),
                pltpu.VMEM((64, cz), jnp.int32),
            ]
            + [pltpu.VMEM(c.shape, c.dtype) for c in consts]
            + [
                pltpu.VMEM((11 * srows + 8, 128), F32),
                tall,
                tall,
                tall,
                tall,
                tall,
                (tall,) * 6,
                (tall,) * 6,
                pltpu.VMEM((6 * rows, 128), F32),
                pltpu.VMEM((rows, 128), F32),
                pltpu.VMEM((3 * rows, 128), F32),
                pltpu.VMEM((rows, 128), F32),
                pltpu.VMEM((rows, 128), F32),
                pltpu.VMEM((16, cz // 2), F32),
                pltpu.VMEM((128, 128), F32),
                pltpu.VMEM((40, 128), F32),
                pltpu.VMEM((16 * sizes[0], 128), F32),
                pltpu.VMEM((4, 2, 8, 128), F32),
                pltpu.VMEM((4, 6, 8, 128), F32),
                pltpu.VMEM((4, 2, ydeep, 128), F32),
                pltpu.VMEM((4, 2, ydeep, 128), F32),
                pltpu.VMEM((4, 2, xdeep, 128), F32),
                pltpu.VMEM((4, 2, xdeep, 128), F32),
                pltpu.VMEM((4, 4, cdeep, 128), F32),
                pltpu.VMEM((4, 4, cdeep, 128), F32),
                pltpu.VMEM((4, 4, 8, 128), F32),
                pltpu.VMEM((4, 16, 128), F32),
                pltpu.VMEM((2, 8, 128), F32),
                pltpu.VMEM((5 * 192, cz), F32),
                pltpu.VMEM((3, 8, 128), F32),
                pltpu.VMEM((3, nline, 128), F32),
                pltpu.VMEM((3, nline, 128), F32),
                pltpu.VMEM((3, nplane, nline, 128), F32),
                pltpu.SemaphoreType.DMA((9,)),
                pltpu.SemaphoreType.DMA((4, 27)),
                pltpu.SemaphoreType.DMA((4, 27)),
                pltpu.SemaphoreType.DMA((3, nline)),
                pltpu.SemaphoreType.DMA((3, nline)),
                pltpu.SemaphoreType.DMA((3, nplane)),
                pltpu.SemaphoreType.DMA((3, nplane)),
            ],
            compiler_params=pltpu.CompilerParams(
                collective_id=0, has_side_effects=True, vmem_limit_bytes=67_000_000
            ),
            name="schwarz_cg",
        )(
            right_side.reshape(192, cz),
            phase_labels,
            phase_moduli,
            coarse_nodes.reshape(64, cz),
            coarse_inverse,
            *consts,
        )
        return sol.reshape(right_side.shape), res.reshape(right_side.shape)

    spec = P(None, "gx", "gy", "gz")
    cells = P("gx", "gy", "gz")
    return jax.shard_map(
        body,
        mesh=mesh,
        in_specs=(spec, cells, P(), cells, P(("gx", "gy", "gz"), None)),
        out_specs=(spec, spec),
        check_vma=False,
    )
```

```python
import functools

import jax
import jax.numpy as jnp
import numpy as np
from jax import lax
from jax.experimental import pallas as pl
from jax.experimental.pallas import tpu as pltpu
from jax.sharding import PartitionSpec as P

MESH = pl.DeviceIdType.MESH
HIGH = lax.Precision.HIGHEST
F32 = jnp.float32

RELAX = 0.6
UNROLL = 4
SWEEPS = 4
SIDE = 8
STRIDE = 11
LEAD = 8
ZH = 2
NODES = 6
NEIGHBOURS = [(x, y, z) for x in (-1, 0, 1) for y in (-1, 0, 1) for z in (-1, 0, 1) if (x, y, z) != (0, 0, 0)]
MODES = 36


def bond(d):
    return d[0] * d[0] + d[1] * d[1] + d[2] * d[2]


def coef(m, k, d):
    n = bond(d)
    if n == 0:
        return 0.0
    return (1.0 / n if m == k else 0.0) + 0.5 * d[m] * d[k] / (n * n)


def plan(cz):
    rows = -(-(cz + 3) // 8) * 8
    srows = -(-(cz // 2 + 2) // 8) * 8
    total = -(-(3 * rows + srows) // 80) * 80
    return rows, srows, total


def tables(cz):
    rows, srows, total = plan(cz)
    place = np.zeros((64, 128), np.float32)
    for i in range(SIDE):
        for j in range(SIDE):
            place[i * SIDE + j, STRIDE * (i + 1) + j + 1] = 1.0
    spot = {-1: 0, 0: 1, 1: 2, 2: 3, 3: 8, 4: 9}
    place_blocks = np.zeros((16, 128), np.float32)
    for i in range(4):
        for j in range(4):
            place_blocks[i * 4 + j, STRIDE * spot[i] + spot[j]] = 1.0

    def lane_of(x, y):
        return STRIDE * spot[x // 2] + spot[y // 2]

    pairs = ((0, 0), (1, 1), (2, 2), (0, 1), (0, 2), (1, 2))
    mix = np.zeros((128, 11 * 128))
    for x in range(-1, 9):
        for y in range(-1, 9):
            out = STRIDE * (x + 1) + y + 1
            mix[lane_of(x, y), out] += 1.0
            for at, (m, k) in enumerate(pairs):
                for a in (-1, 0, 1):
                    for b in (-1, 0, 1):
                        src = lane_of(x + a, y + b)
                        if at < 4:
                            mix[src, 128 * (1 + at) + out] += 72.0 * coef(m, k, (a, b, 0))
                        mix[src, 128 * (5 + at) + out] += 72.0 * coef(m, k, (a, b, 1))
    mix = np.round(mix)
    lane = np.arange(128)
    ints = np.zeros((32, 128), np.int32)
    ints[0:8] = np.where(lane < 110, lane // STRIDE, 99)
    ints[8:16] = np.where(lane < 110, lane % STRIDE, 99)
    ints[16:24] = np.where(lane < 126, lane // 21, 99)
    ints[24:32] = np.where(lane < 126, lane % 21 % STRIDE, 99)
    floats = np.zeros((16, 128), np.float32)
    floats[0:8] = (2.0 * (lane // STRIDE - 1) + 1.0) / SIDE - 1.0
    floats[8:16] = (2.0 * (lane % STRIDE - 1) + 1.0) / SIDE - 1.0
    half = lambda a: jnp.asarray(a, jnp.bfloat16)
    return half(place), half(place_blocks), half(mix), jnp.asarray(ints), jnp.asarray(floats)


WHOLE = sum(coef(0, 0, (a, b, c)) for a in (-1, 0, 1) for b in (-1, 0, 1) for c in (-1, 0, 1))


def thirds(x):
    high = x.astype(jnp.bfloat16)
    rest = x - high.astype(F32)
    middle = rest.astype(jnp.bfloat16)
    return high, middle, (rest - middle.astype(F32)).astype(jnp.bfloat16)


def turn(x, shift):
    shift = shift % 128
    return x if shift == 0 else pltpu.roll(x, shift, 1)


def add_all(items):
    items = list(items)
    while len(items) > 1:
        items = [
            items[i] + items[i + 1] if i + 1 < len(items) else items[i] for i in range(0, len(items), 2)
        ]
    return items[0]


def kernel(
    sizes,
    cz,
    rhs_hbm,
    labels_hbm,
    moduli,
    nodes_hbm,
    inverse,
    place_hbm,
    place_blocks_hbm,
    mix_hbm,
    ints_hbm,
    floats_hbm,
    sol_out,
    res_out,
    mat,
    rhs,
    labels,
    nodes_in,
    place,
    place_blocks,
    mix,
    ints,
    floats,
    mixed,
    field,
    zfield,
    qfield,
    rfield,
    pfield,
    set_a,
    set_b,
    dmat,
    stiff,
    cdiag,
    node,
    gridm,
    stage,
    rowm,
    ybuf,
    cvec,
    zsend,
    zrecv,
    ysend,
    yrecv,
    xsend,
    xrecv,
    csend,
    crecv,
    rsend,
    rrecv,
    zsum,
    outs,
    gmsg,
    g1,
    g1c,
    g2,
    load_sem,
    halo_ss,
    halo_rs,
    g1_ss,
    g1_rs,
    g2_ss,
    g2_rs,
):
    ngx, ngy, ngz = sizes
    rows, srows, total = plan(cz)
    tiles = rows // 8
    sbase = LEAD + 3 * rows
    gx, gy, gz = lax.axis_index("gx"), lax.axis_index("gy"), lax.axis_index("gz")
    zhi, yhi = lax.rem(gx, ZH), lax.div(gx, ZH)
    nline = ZH * ngy
    nplane = (ngx // ZH) * ngz
    slot1 = zhi * ngy + gy
    slot2 = yhi * ngz + gz

    def line_peer(step):
        other = lax.rem(slot1 + step, nline)
        return (yhi * ZH + lax.div(other, ngy), lax.rem(other, ngy), gz)

    def plane_peer(step):
        other = lax.rem(slot2 + step, nplane)
        return (lax.div(other, ngz) * ZH + zhi, gy, lax.rem(other, ngz))

    sides = {}
    for d in NEIGHBOURS:
        has = None
        for way, at, count in zip(d, (gx, gy, gz), sizes):
            if way != 0:
                one = at > 0 if way < 0 else at < count - 1
                has = one if has is None else has & one
        sides[d] = (has, (gx + d[0], gy + d[1], gz + d[2]))

    loads = [
        pltpu.make_async_copy(src, dst, load_sem.at[at])
        for at, (src, dst) in enumerate(
            (
                (rhs_hbm, rhs),
                (nodes_hbm, nodes_in),
                (labels_hbm, labels),
                (place_hbm, place),
                (place_blocks_hbm, place_blocks),
                (ints_hbm, ints),
                (floats_hbm, floats),
                (mix_hbm, mix),
                (inverse, mat),
            )
        )
    ]
    for load in loads:
        load.start()
    mat_copy, mix_copy = loads[-1], loads[-2]

    barrier = pltpu.get_barrier_semaphore()
    for has, device in [sides[d] for d in sorted(NEIGHBOURS, key=lambda d: -abs(d[0]))]:

        @pl.when(has)
        def _(device=device):
            pl.semaphore_signal(barrier, inc=1, device_id=device, device_id_type=MESH)

    for step in range(1, nline):
        pl.semaphore_signal(barrier, inc=1, device_id=line_peer(step), device_id_type=MESH)
    for step in range(1, nplane):
        pl.semaphore_signal(barrier, inc=1, device_id=plane_peer(step), device_id_type=MESH)


    lane = lax.broadcasted_iota(jnp.int32, (8, 128), 1)
    sub = lax.broadcasted_iota(jnp.int32, (8, 128), 0)

    def base_of(k, i):
        return tile_at(LEAD + k * rows, i)

    def tile_at(first, i):
        return first + 8 * i if isinstance(i, int) else pl.multiple_of(first + 8 * i, 8)

    def repeat(count, one, unroll):
        whole = count // unroll if count > 2 * unroll else 0

        def some(n, carry):
            for j in range(unroll):
                one(n * unroll + j)
            return carry

        if whole:
            lax.fori_loop(0, whole, some, 0)
        for i in range(whole * unroll, count):
            one(i)

    def each_tile(one, unroll=4):
        whole = tiles // unroll

        def some(n, carry):
            for j in range(unroll):
                one(n * unroll + j)
            return carry

        lax.fori_loop(0, whole, some, 0)
        for i in range(whole * unroll, tiles):
            one(i)

    def xi_z(i):
        along = (sub + (8 * i - 1)).astype(F32)
        return (2.0 * along + 1.0) / cz - 1.0

    def deep(axis, width):
        if width == 1:
            return total // 10
        return 8 * -(-3 * rows // (40 if axis == 1 else 48))

    def edge_chunks(width):
        return 6 if width == 1 else 5

    def edge_deep(width):
        return 8 * -(-deep(2, width) // (8 * edge_chunks(width)))

    def inbox(which, d):
        x, y, z = d
        width = 1 + which % 2
        if z != 0:
            if x == 0:
                return zrecv.at[which, 3 * (z > 0) + y + 1]
            at = 6 * (x > 0) + 3 * (z > 0) + y + 1
            return rrecv.at[which, at : at + 1]
        if x != 0 and y != 0:
            return crecv.at[which, 2 * (x > 0) + (y > 0), 0 : edge_deep(width)]
        if y != 0:
            return yrecv.at[which, int(y > 0), 0 : deep(1, width)]
        return xrecv.at[which, int(x > 0), 0 : deep(2, width)]

    def outbox(which, d):
        x, y, z = d
        width = 1 + which % 2
        if z != 0:
            if x == 0:
                return zsend.at[which, int(z > 0)]
            at = 2 * (x > 0) + (z > 0)
            return rsend.at[which, at, 0:1]
        if x != 0 and y != 0:
            return csend.at[which, 2 * (x > 0) + (y > 0), 0 : edge_deep(width)]
        if y != 0:
            return ysend.at[which, int(y > 0), 0 : deep(1, width)]
        return xsend.at[which, int(x > 0), 0 : deep(2, width)]

    for f in range(6):
        dmat[rows * f + cz + 2 : rows * (f + 1), :] = jnp.zeros((rows - cz - 2, 128), F32)
    stiff[cz + 2 : rows, :] = jnp.zeros((rows - cz - 2, 128), F32)
    for ref in (field, rfield):
        ref[...] = jnp.zeros(ref.shape, F32)
    zfield[sbase:, :] = jnp.zeros((LEAD + total - sbase, 128), F32)
    for ref in set_a + set_b:
        ref[0:LEAD, :] = jnp.zeros((LEAD, 128), F32)
        ref[LEAD + 3 * rows : LEAD + 3 * rows + 8, :] = jnp.zeros((8, 128), F32)
    node[...] = jnp.zeros(node.shape, F32)
    rowm[...] = jnp.zeros(rowm.shape, F32)
    for ref in (zsend, xsend):
        ref[...] = jnp.zeros(ref.shape, F32)
    for t in range(4):
        for e in range(2):
            end = deep(2, 1 + t % 2)
            xrecv[t, e, end:, :] = jnp.zeros((xrecv.shape[2] - end, 128), F32)
    cvec[...] = jnp.zeros(cvec.shape, F32)
    stage[...] = jnp.zeros(stage.shape, F32)
    for d in NEIGHBOURS:

        @pl.when(jnp.logical_not(sides[d][0]))
        def _(d=d):
            for t in range(4):
                ref = inbox(t, d)
                ref[...] = jnp.zeros(ref.shape, F32)

    for load in loads[:-2]:
        load.wait()
    lane_x, lane_y, lane_c = ints[0:8, :], ints[8:16, :], ints[16:24, :]
    lane_e = ints[24:32, :]
    xi_x, xi_y = floats[0:8, :], floats[8:16, :]

    def dot(a, b, dims):
        return lax.dot_general(a, b, ((dims[:1], dims[1:]), ((), ())), preferred_element_type=F32)

    def spread_in(x):
        return add_all([dot(part, place[...], (0, 0)) for part in thirds(x)[::-1]])

    def gather_out(select, x):
        return add_all([dot(select, part, (1, 1)) for part in thirds(x)[::-1]])

    for k in range(3):
        piece = spread_in(rhs[64 * k : 64 * k + 64, :])
        first = LEAD + k * rows + 1
        field[first : first + cz, :] = piece
        rfield[first : first + cz, :] = piece
    node[1 : 1 + cz, :] = dot((nodes_in[...].astype(F32) + 1.0).astype(jnp.bfloat16), place[...], (0, 0))
    for i in range(4):
        stage[4 * i : 4 * i + 4, :] = labels[i].astype(F32) + 1.0
    phases = dot(stage[...].astype(jnp.bfloat16), place_blocks[...], (0, 0))
    blocks = jnp.zeros(phases.shape, F32)
    for phase in range(moduli.shape[0]):
        blocks = jnp.where(phases == float(phase + 1), moduli[phase], blocks)
    field[sbase + 1 : sbase + 1 + cz // 2, :] = blocks

    bad_lane = (
        ((gx == 0) & (lane_x == 0))
        | ((gx == ngx - 1) & (lane_x == 9))
        | ((gy == 0) & (lane_y == 0))
        | ((gy == ngy - 1) & (lane_y == 9))
        | (lane_x > 9)
        | (lane_y > 9)
    )
    low = jnp.where(gz == 0, 1, 0)
    high = jnp.where(gz == ngz - 1, cz + 1, cz + 2)

    def grid_tile(i):
        r = sub + 8 * i
        gridm[pl.ds(tile_at(0, i), 8), :] = jnp.where(bad_lane | (r < low) | (r >= high), 0.0, 1.0)

    each_tile(grid_tile)

    def number(d):
        return 9 * (d[0] + 1) + 3 * (d[1] + 1) + d[2] + 1

    def opposite(d):
        return (-d[0], -d[1], -d[2])

    def halo(which, d):
        return pltpu.make_async_remote_copy(
            src_ref=outbox(which, d),
            dst_ref=inbox(which, opposite(d)),
            send_sem=halo_ss.at[which, number(d)],
            recv_sem=halo_rs.at[which, number(opposite(d))],
            device_id=sides[d][1],
            device_id_type=MESH,
        )

    def send(which, group):
        for d in group:

            @pl.when(sides[d][0])
            def _(d=d):
                halo(which, d).start()

    def arrive(which, group):
        for d in group:

            @pl.when(sides[d][0])
            def _(d=d):
                pltpu.make_async_remote_copy(
                    src_ref=outbox(which, d),
                    dst_ref=inbox(which, d),
                    send_sem=halo_ss.at[which, number(d)],
                    recv_sem=halo_rs.at[which, number(d)],
                    device_id=sides[d][1],
                    device_id_type=MESH,
                ).wait_recv()

    def left(which):
        for d in NEIGHBOURS:

            @pl.when(sides[d][0])
            def _(d=d):
                halo(which, d).wait_send()

    def z_rows(width):
        if width == 1:
            got = [(LEAD + k * rows, cz, k) for k in range(3)] + [(sbase, cz // 2, 3)]
            return [(r + n, r + 1, r, r + n + 1, at) for r, n, at in got]
        out = []
        for k in range(3):
            for layer in range(2):
                r = LEAD + k * rows + layer
                out.append((r + cz, r, r, r + cz, 2 * k + layer))
        return out

    def groups(axis, width, along=None):
        if axis == 1:
            along = lane_y if along is None else along
            if width == 1:
                return 10, [along == k for k in range(10)]
            return 5, [(along == 2 * k) | (along == 2 * k + 1) for k in range(5)]
        if width == 1:
            return 10, [lane_x == k for k in range(10)]
        return 6, [lane_c == k for k in range(6)]

    def move(axis, width, along=None):
        if axis == 1:
            along = lane_y if along is None else along
            if width == 1:
                return 1, (1, 8), (0, 9), (along == 0, along == 9)
            return 2, (0, 8), (0, 8), (along < 2, (along == 8) | (along == 9))
        if width == 1:
            return STRIDE, (STRIDE, 8 * STRIDE), (0, 9 * STRIDE), (lane_x == 0, lane_x == 9)
        return 21, (0, 88), (0, 88), (lane < 21, (lane >= 88) & (lane < 109))

    def pack(src, first, dsts, axis, width, chunks, depth, along=None):
        gap, froms, _, _ = move(axis, width)
        masks = groups(axis, width, along)[1]

        def one(t):
            low, high = jnp.zeros((8, 128), F32), jnp.zeros((8, 128), F32)
            for k in range(chunks):
                tile = src[pl.ds(tile_at(first + 8 * k * depth, t), 8), :]
                low = jnp.where(masks[k], turn(tile, gap * k - froms[0]), low)
                high = jnp.where(masks[k], turn(tile, gap * k - froms[1]), high)
            at = pl.ds(tile_at(0, t), 8)
            dsts[0][at, :] = low
            dsts[1][at, :] = high

        repeat(depth, one, 3)

    def unpack(dst, first, srcs, axis, width, chunks, depth, along=None):
        gap, _, tos, ends = move(axis, width, along)

        def one(t):
            at = pl.ds(tile_at(0, t), 8)
            low, high = srcs[0][at, :], srcs[1][at, :]
            for k in range(chunks):
                part = pl.ds(tile_at(first + 8 * k * depth, t), 8)
                tile = dst[part, :]
                tile = tile + jnp.where(ends[0], turn(low, tos[0] - gap * k), 0.0)
                tile = tile + jnp.where(ends[1], turn(high, tos[1] - gap * k), 0.0)
                dst[part, :] = tile

        repeat(depth, one, 3)

    far_rows = [(x, y, z) for x in (-1, 1) for z in (-1, 1) for y in (-1, 0, 1)]
    near_layers = [(0, y, z) for z in (-1, 1) for y in (-1, 0, 1)]
    edges = [(x, y, 0) for x in (-1, 1) for y in (-1, 1)]

    def exchange(ref, which, width, early=None, late=None):
        chunks = [None, groups(1, width)[0], groups(2, width)[0]]
        depth = [None, deep(1, width) // 8, deep(2, width) // 8]
        edge, edge_parts = edge_deep(width) // 8, edge_chunks(width)
        along = lane_y if width == 1 else lane_e
        gap, froms, tos, ends = move(2, width)
        layers = 4 if width == 1 else 6
        pack(ref, LEAD, [xsend.at[which, e] for e in range(2)], 2, width, chunks[2], depth[2])
        send(which, [(-1, 0, 0), (1, 0, 0)])
        for x in range(2):
            pack(
                xsend.at[which, x],
                0,
                [csend.at[which, 2 * x + y] for y in range(2)],
                1,
                width,
                edge_parts,
                edge,
                along,
            )
        send(which, edges)
        for up_from, down_from, _, _, at in z_rows(width):
            zsend[which, 0, at : at + 1, :] = ref[down_from : down_from + 1, :]
            zsend[which, 1, at : at + 1, :] = ref[up_from : up_from + 1, :]
        mine = [(sub == r) & (lane >= gap * r) & (lane < gap * r + gap) for r in range(layers)]
        for z in range(2):
            tile = zsend[which, z]
            for x in range(2):
                row = jnp.zeros((8, 128), F32)
                for r in range(layers):
                    row = jnp.where(mine[r], turn(tile, gap * r - froms[x]), row)
                rsend[which, 2 * x + z, 0:1, :] = jnp.sum(row, axis=0, keepdims=True)
        send(which, far_rows)
        pack(ref, LEAD, [ysend.at[which, e] for e in range(2)], 1, width, chunks[1], depth[1])
        send(which, [(0, -1, 0), (0, 1, 0)])
        send(which, near_layers)
        if early is not None:
            early()
        arrive(which, [(0, -1, 0), (0, 1, 0)])
        unpack(ref, LEAD, [yrecv.at[which, e] for e in range(2)], 1, width, chunks[1], depth[1])
        if late is not None:
            late()
        arrive(which, near_layers)
        arrive(which, far_rows)
        yends = move(1, width)[3]
        for z in range(2):
            tiles_y = []
            for y in range(3):
                tile = zrecv[which, 3 * z + y]
                for x in range(2):
                    at = 6 * x + 3 * z + y
                    row = jnp.broadcast_to(rrecv[which, at : at + 1, :], (8, 128))
                    for r in range(layers):
                        here = (sub == r) & ends[x]
                        tile = tile + jnp.where(here, turn(row, tos[x] - gap * r), 0.0)
                tiles_y.append(tile)
            zsum[z] = (
                tiles_y[1]
                + jnp.where(yends[0], turn(tiles_y[0], -8), 0.0)
                + jnp.where(yends[1], turn(tiles_y[2], 8), 0.0)
            )
        for _, _, low_to, high_to, at in z_rows(width):
            ref[low_to : low_to + 1, :] += zsum[0, at : at + 1, :]
            ref[high_to : high_to + 1, :] += zsum[1, at : at + 1, :]
        arrive(which, [(-1, 0, 0), (1, 0, 0)])
        arrive(which, edges)
        for x in range(2):
            unpack(
                xrecv.at[which, x],
                0,
                [crecv.at[which, 2 * x + y] for y in range(2)],
                1,
                width,
                edge_parts,
                edge,
                along,
            )
        unpack(ref, LEAD, [xrecv.at[which, e] for e in range(2)], 2, width, chunks[2], depth[2])

    def line_copy(which, step):
        return pltpu.make_async_remote_copy(
            src_ref=gmsg.at[which, pl.ds(0, 1)],
            dst_ref=g1.at[which, pl.ds(slot1, 1)],
            send_sem=g1_ss.at[which, step],
            recv_sem=g1_rs.at[which, slot1],
            device_id=line_peer(step),
            device_id_type=MESH,
        )

    def line_start(which, message):
        gmsg[which] = message
        g1[which, pl.ds(slot1, 1), :] = message[0:1, :]
        for step in range(1, nline):
            line_copy(which, step).start()

    def line_arrive(which):
        for step in range(1, nline):
            other = lax.rem(slot1 + step, nline)
            pltpu.make_async_remote_copy(
                src_ref=gmsg.at[which, pl.ds(0, 1)],
                dst_ref=g1.at[which, pl.ds(other, 1)],
                send_sem=g1_ss.at[which, step],
                recv_sem=g1_rs.at[which, other],
                device_id=line_peer(step),
                device_id_type=MESH,
            ).wait_recv()

    def plane_rows(which):
        return nline if which < 2 else 8

    def plane_copy(which, step):
        return pltpu.make_async_remote_copy(
            src_ref=g1c.at[which, 0 : plane_rows(which)],
            dst_ref=g2.at[which, slot2, 0 : plane_rows(which)],
            send_sem=g2_ss.at[which, step],
            recv_sem=g2_rs.at[which, slot2],
            device_id=plane_peer(step),
            device_id_type=MESH,
        )

    def plane_start(which, block):
        g1c[which] = block
        g2[which, pl.ds(slot2, 1)] = block[None]
        for step in range(1, nplane):
            plane_copy(which, step).start()

    def plane_arrive(which):
        for step in range(1, nplane):
            other = lax.rem(slot2 + step, nplane)
            pltpu.make_async_remote_copy(
                src_ref=g1c.at[which, 0 : plane_rows(which)],
                dst_ref=g2.at[which, other, 0 : plane_rows(which)],
                send_sem=g2_ss.at[which, step],
                recv_sem=g2_rs.at[which, other],
                device_id=plane_peer(step),
                device_id_type=MESH,
            ).wait_recv()

    def moments(ref):
        def one(i, acc):
            r = [ref[pl.ds(base_of(k, i), 8), :] for k in range(3)]
            own = node[pl.ds(tile_at(0, i), 8), :]
            z = xi_z(i)
            parts = r + [xi_y * r[2] - z * r[1], z * r[0] - xi_x * r[2], xi_x * r[1] - xi_y * r[0]]
            out = []
            for g in range(NODES):
                here = own == float(g + 1)
                for m in range(6):
                    out.append(acc[6 * g + m] + jnp.where(here, parts[m], 0.0))
            return tuple(out)

        acc = lax.fori_loop(0, tiles, one, tuple(jnp.zeros((8, 128), F32) for _ in range(MODES)))
        for at in range(MODES):
            rowm[at : at + 1, :] = jnp.sum(acc[at], axis=0, keepdims=True)

    def row_to_lanes():
        return gather_out(jnp.ones((8, 128), jnp.bfloat16), rowm[...])

    turned = lax.rem((gy * ngz + gz) * MODES, 128)

    def own_range(c):
        begin = (sub * ngz + c) * MODES - 128 * sub
        ahead = begin < 128
        first = (lane >= begin) & (lane < begin + MODES)
        second = (lane + 128 >= begin) & (lane + 128 < begin + MODES)
        return first, second

    def coarse_solve(which):
        ranges = [own_range(c) for c in range(ngz)]
        acc = [jnp.zeros((8, 128), F32) for _ in range(5)]
        for y in range(ngx // ZH):
            for h in range(ZH):
                a = y * ZH + h
                got = [g2[which, y * ngz + c, 8 * h : 8 * h + 8, :] for c in range(ngz)]
                main = add_all([jnp.where(ranges[c][0], got[c], 0.0) for c in range(ngz)])
                nxt = add_all([jnp.where(ranges[c][1], got[c], 0.0) for c in range(ngz)])
                cvec[16 * a + 8 : 16 * a + 9, :] = jnp.zeros((1, 128), F32)
                cvec[16 * a : 16 * a + 8, :] = main
                cvec[16 * a + 1 : 16 * a + 9, :] += nxt
        for a in range(ngx):
            for j in range(9):
                row = jnp.broadcast_to(cvec[16 * a + j : 16 * a + j + 1, :], (8, 128))
                col = 128 * (9 * a + j)
                for t in range(4):
                    acc[t] = acc[t] + mat[8 * t : 8 * t + 8, col : col + 128] * row
                acc[4] = acc[4] + jnp.concatenate([mat[32:36, col : col + 128]] * 2, axis=0) * row
        for t in range(5):
            ybuf[8 * t : 8 * t + 8, :] = jnp.broadcast_to(jnp.sum(acc[t], axis=1, keepdims=True), (8, 128))

    def lane_sum(which, at):
        parts = []
        for c in range(ngz):
            pos = lax.rem((sub * ngz + c) * MODES + at, 128)
            here = lane == pos
            for y in range(ngx // ZH):
                for h in range(ZH):
                    parts.append(jnp.where(here, g2[which, y * ngz + c, 8 * h : 8 * h + 8, :], 0.0))
        whole = jnp.sum(add_all(parts), axis=0, keepdims=True)
        return jnp.sum(whole, axis=1, keepdims=True)

    def with_coarse(src, dst):
        def one(i):
            own = node[pl.ds(tile_at(0, i), 8), :]
            grid = gridm[pl.ds(tile_at(0, i), 8), :]
            z = xi_z(i)
            modes = [jnp.zeros((8, 128), F32) for _ in range(6)]
            for g in range(NODES):
                here = own == float(g + 1)
                for m in range(6):
                    at = 6 * g + m
                    modes[m] = jnp.where(here, jnp.broadcast_to(ybuf[at : at + 1, :], (8, 128)), modes[m])
            t, w = modes[:3], modes[3:]
            add = [
                t[0] + (w[1] * z - w[2] * xi_y),
                t[1] + (w[2] * xi_x - w[0] * z),
                t[2] + (w[0] * xi_y - w[1] * xi_x),
            ]
            for k in range(3):
                at = pl.ds(base_of(k, i), 8)
                dst[at, :] = src[at, :] * grid + add[k]

        each_tile(one)

    def spread_tile(i, values, bufs):
        vf, wf, syv, dyv, syw, dyw = bufs
        s = stiff[pl.ds(tile_at(0, i), 8), :]
        for k in range(3):
            at = pl.ds(base_of(k, i), 8)
            v = values[k]
            w = s * v
            vf[at, :] = v
            wf[at, :] = w
            for x, sy, dy in ((v, syv, dyv), (w, syw, dyw)):
                ahead, behind = turn(x, -1), turn(x, 1)
                sy[at, :] = ahead + behind
                dy[at, :] = ahead - behind

    def spread(ref):
        each_tile(lambda i: spread_tile(i, [ref[pl.ds(base_of(k, i), 8), :] for k in range(3)], set_a))

    def couple(u_ref, sy_ref, dy_ref, i):
        def at(ref, k, dz):
            return ref[pl.ds(base_of(k, i) + dz, 8), :]

        up = [at(u_ref, k, 1) for k in range(3)]
        um = [at(u_ref, k, -1) for k in range(3)]
        u = [at(u_ref, k, 0) for k in range(3)]
        s = [up[k] + um[k] for k in range(3)]
        yp = [at(sy_ref, k, 1) for k in range(3)]
        ym = [at(sy_ref, k, -1) for k in range(3)]
        sy = [at(sy_ref, k, 0) for k in range(3)]
        sys = [yp[k] + ym[k] for k in range(3)]
        t_x, t_z = up[0] - um[0], up[2] - um[2]
        ty_x, ty_z = yp[0] - ym[0], yp[2] - ym[2]
        dp = [at(dy_ref, k, 1) for k in range(3)]
        dm = [at(dy_ref, k, -1) for k in range(3)]
        dys_x, dys_y = dp[0] + dm[0], dp[1] + dm[1]
        dyt_y, dyt_z = dp[1] - dm[1], dp[2] - dm[2]
        dy_x, dy_y = at(dy_ref, 0, 0), at(dy_ref, 1, 0)
        e, th, c7 = 0.125, 1.0 / 18.0, 7.0 / 18.0
        still = [
            sy[0] + s[0] + 0.5 * sys[0],
            1.5 * sy[1] + s[1] + 0.625 * sys[1] + e * dyt_z,
            sy[2] + 1.5 * s[2] + 0.625 * sys[2] + e * dyt_y,
        ]
        even = [
            1.5 * u[0] + 0.625 * (sy[0] + s[0]) + c7 * sys[0],
            u[1] + 0.625 * sy[1] + 0.5 * s[1] + c7 * sys[1] + th * dyt_z,
            u[2] + 0.5 * sy[2] + 0.625 * s[2] + c7 * sys[2] + th * dyt_y,
        ]
        odd = [
            e * (dy_y + t_z) + th * (dys_y + ty_z),
            e * dy_x + th * dys_x,
            e * t_x + th * ty_x,
        ]
        return [
            still[k] + (turn(even[k] + odd[k], -STRIDE) + turn(even[k] - odd[k], STRIDE)) for k in range(3)
        ], u

    def image_tile(i, bufs):
        vf, wf, syv, dyv, syw, dyw = bufs
        here = pl.ds(tile_at(0, i), 8)
        lv, v = couple(vf, syv, dyv, i)
        lw, _ = couple(wf, syw, dyw, i)
        s = stiff[here, :]
        d = [dmat[pl.ds(tile_at(rows * f, i), 8), :] for f in range(6)]
        full = ((0, 3, 4), (3, 1, 5), (4, 5, 2))
        out = []
        for m in range(3):
            diag = d[full[m][0]] * v[0] + d[full[m][1]] * v[1] + d[full[m][2]] * v[2]
            out.append(diag - 0.5 * (s * lv[m] + lw[m]))
        return out, v

    def local_solve(ref, out):
        def first(i):
            spread_tile(
                i,
                [cdiag[pl.ds(tile_at(rows * k, i), 8), :] * ref[pl.ds(base_of(k, i), 8), :] for k in range(3)],
                set_a,
            )

        each_tile(first)
        bufs = [set_a, set_b]
        for sweep in range(SWEEPS - 1):

            def one(i, sweep=sweep):
                image, v = image_tile(i, bufs[sweep % 2])
                new = []
                for k in range(3):
                    c = cdiag[pl.ds(tile_at(rows * k, i), 8), :]
                    new.append(v[k] + c * (ref[pl.ds(base_of(k, i), 8), :] - image[k]))
                if sweep < SWEEPS - 2:
                    spread_tile(i, new, bufs[(sweep + 1) % 2])
                else:
                    for k in range(3):
                        out[pl.ds(base_of(k, i), 8), :] = new[k]

            each_tile(one, UNROLL)

    def setup_stiffness():
        mix_copy.wait()
        parts = thirds(field[sbase : sbase + srows, :])[::-1]
        for f in range(0, 11, 2):
            wide = 128 * min(2, 11 - f)
            got = add_all([dot(part, mix[:, 128 * f : 128 * f + wide], (1, 0)) for part in parts])
            for g in range(wide // 128):
                mixed[srows * (f + g) : srows * (f + g + 1), :] = got[:, 128 * g : 128 * g + 128]
        count = cz // 2 + 1

        def at(f, shift):
            return mixed[srows * f + shift : srows * f + shift + count, :]

        for parity in range(2):
            here = lambda f: at(f, parity)
            beyond = lambda f: at(f, 1 - parity)
            s_here = here(0)
            stiff[pl.ds(parity, count, stride=2), :] = s_here
            for m in range(6):
                if m < 4:
                    value = (here(1 + m) + here(5 + m) + beyond(5 + m)) * (1.0 / 144.0)
                    if m < 3:
                        value = value + (0.5 * WHOLE) * s_here
                else:
                    tilt = here(5 + m) - beyond(5 + m)
                    value = (tilt if parity == 1 else -tilt) * (1.0 / 144.0)
                dmat[pl.ds(rows * m + parity, count, stride=2), :] = value

        def one(i):
            for k in range(3):
                part = pl.ds(tile_at(rows * k, i), 8)
                d = dmat[part, :]
                live = d > 0.0
                cdiag[part, :] = jnp.where(live, RELAX / jnp.where(live, d, 1.0), 0.0)

        each_tile(one)

    def first_row():
        moments(field)
        return turn_by(row_to_lanes(), turned)

    greeters = nline - 1 + nplane - 1
    for has, _ in sides.values():
        greeters = greeters + jnp.where(has, 1, 0)
    pl.semaphore_wait(barrier, greeters)

    def forward(which):
        line_arrive(which)
        plane_start(which, g1[which])

    exchange(field, 0, 1, lambda: line_start(0, first_row()), lambda: forward(0))
    setup_stiffness()
    local_solve(field, pfield)
    mat_copy.wait()
    plane_arrive(0)
    coarse_solve(0)
    with_coarse(pfield, zfield)
    exchange(zfield, 1, 2)

    spread(zfield)

    def image_and_sums(dsts, first, second):
        def one(i, acc):
            image, v = image_tile(i, set_a)
            own = node[pl.ds(tile_at(0, i), 8), :] > 0.0
            acc = list(acc)
            for k in range(3):
                at = pl.ds(base_of(k, i), 8)
                mine = jnp.where(own, image[k], 0.0)
                for dst in dsts:
                    dst[at, :] = mine
                acc[0] = acc[0] + first[at, :] * v[k]
                acc[1] = acc[1] + v[k] * mine
                if second is not None:
                    acc[2] = acc[2] + second[at, :] * v[k]
            return tuple(acc)

        count = 2 if second is None else 3
        acc = tuple(jnp.zeros((8, 128), F32) for _ in range(count))
        acc = lax.fori_loop(0, tiles // 2, lambda n, acc: one(2 * n + 1, one(2 * n, acc)), acc)
        for i in range(tiles // 2 * 2, tiles):
            acc = one(i, acc)
        return [jnp.sum(a, axis=0, keepdims=True) for a in acc]

    sums = image_and_sums((qfield, field), rfield, None)
    def second_row():
        moments(qfield)
        rowm[MODES : MODES + 1, :] = sums[0]
        rowm[MODES + 1 : MODES + 2, :] = sums[1]
        return turn_by(row_to_lanes(), turned)

    exchange(field, 2, 1, lambda: line_start(1, second_row()), lambda: forward(1))
    local_solve(field, pfield)
    plane_arrive(1)
    coarse_solve(1)
    rho0 = lane_sum(1, MODES)
    curve0 = lane_sum(1, MODES + 1)
    alpha0 = rho0 / curve0
    with_coarse(pfield, field)
    exchange(field, 3, 2)

    def renew(i):
        for k in range(3):
            at = pl.ds(base_of(k, i), 8)
            field[at, :] = zfield[at, :] - alpha0 * field[at, :]
            rfield[at, :] = rfield[at, :] - alpha0 * qfield[at, :]

    each_tile(renew)
    spread(field)

    sums = image_and_sums((pfield,), rfield, qfield)
    rowm[0:MODES, :] = jnp.zeros((MODES, 128), F32)
    for at in range(3):
        rowm[MODES + at : MODES + at + 1, :] = sums[at]
    line_start(2, row_to_lanes())
    for at, ref in enumerate((zfield, field, rfield, pfield, qfield)):
        for k in range(3):
            first = LEAD + k * rows + 1
            outs[192 * at + 64 * k : 192 * at + 64 * k + 64, :] = gather_out(place[...], ref[first : first + cz, :])
    line_arrive(2)
    plane_start(2, jnp.broadcast_to(jnp.sum(g1[2], axis=0, keepdims=True), (nline, 128)))
    plane_arrive(2)
    last = add_all([g2[2, p, 0:8, :] for p in range(nplane)])[0:1, :]
    rho1, zaz, zq = [
        jnp.sum(jnp.where(lane[0:1, :] == MODES + at, last, 0.0), axis=1, keepdims=True) for at in range(3)
    ]
    beta = rho1 / rho0
    alpha1 = rho1 / (zaz + 2.0 * beta * zq + beta * beta * curve0)

    for i in range(24):
        z0, z1, r1, q1, q0 = [outs[192 * at + 8 * i : 192 * at + 8 * i + 8, :] for at in range(5)]
        sol_out[8 * i : 8 * i + 8, :] = alpha0 * z0 + alpha1 * (z1 + beta * z0)
        res_out[8 * i : 8 * i + 8, :] = r1 - alpha1 * (q1 + beta * q0)

    for which in range(4):
        left(which)
    for which in range(3):
        for step in range(1, nline):
            line_copy(which, step).wait_send()
        for step in range(1, nplane):
            plane_copy(which, step).wait_send()


def turn_by(x, shift):
    return pltpu.roll(x, shift, 1)


def solution(mesh):
    sizes = (mesh.shape["gx"], mesh.shape["gy"], mesh.shape["gz"])
    nline = ZH * sizes[1]
    nplane = (sizes[0] // ZH) * sizes[2]

    def body(right_side, phase_labels, phase_moduli, coarse_nodes, coarse_inverse):
        cz = right_side.shape[3]
        rows, srows, total = plan(cz)
        tall = pltpu.VMEM((LEAD + total, 128), F32)
        ydeep = max(total // 10, 8 * -(-3 * rows // 40))
        cdeep = 16
        xdeep = max(total // 10, 8 * -(-3 * rows // 48))
        xdeep = max(xdeep, 5 * cdeep)
        vmem = pl.BlockSpec(memory_space=pltpu.VMEM)
        away = pl.BlockSpec(memory_space=pl.ANY)
        consts = tables(cz)
        sol, res = pl.pallas_call(
            functools.partial(kernel, sizes, cz),
            out_shape=(jax.ShapeDtypeStruct((192, cz), F32),) * 2,
            in_specs=[
                away,
                away,
                pl.BlockSpec(memory_space=pltpu.SMEM),
                away,
                away,
            ]
            + [away] * len(consts),
            out_specs=(vmem, vmem),
            scratch_shapes=[
                pltpu.VMEM(coarse_inverse.shape, F32),
                pltpu.VMEM((192, cz), F32),
                pltpu.VMEM(phase_labels.shape, jnp.int32),
                pltpu.VMEM((64, cz), jnp.int32),
            ]
            + [pltpu.VMEM(c.shape, c.dtype) for c in consts]
            + [
                pltpu.VMEM((11 * srows + 8, 128), F32),
                tall,
                tall,
                tall,
                tall,
                tall,
                (tall,) * 6,
                (tall,) * 6,
                pltpu.VMEM((6 * rows, 128), F32),
                pltpu.VMEM((rows, 128), F32),
                pltpu.VMEM((3 * rows, 128), F32),
                pltpu.VMEM((rows, 128), F32),
                pltpu.VMEM((rows, 128), F32),
                pltpu.VMEM((16, cz // 2), F32),
                pltpu.VMEM((128, 128), F32),
                pltpu.VMEM((40, 128), F32),
                pltpu.VMEM((16 * sizes[0], 128), F32),
                pltpu.VMEM((4, 2, 8, 128), F32),
                pltpu.VMEM((4, 6, 8, 128), F32),
                pltpu.VMEM((4, 2, ydeep, 128), F32),
                pltpu.VMEM((4, 2, ydeep, 128), F32),
                pltpu.VMEM((4, 2, xdeep, 128), F32),
                pltpu.VMEM((4, 2, xdeep, 128), F32),
                pltpu.VMEM((4, 4, cdeep, 128), F32),
                pltpu.VMEM((4, 4, cdeep, 128), F32),
                pltpu.VMEM((4, 4, 8, 128), F32),
                pltpu.VMEM((4, 16, 128), F32),
                pltpu.VMEM((2, 8, 128), F32),
                pltpu.VMEM((5 * 192, cz), F32),
                pltpu.VMEM((3, 8, 128), F32),
                pltpu.VMEM((3, nline, 128), F32),
                pltpu.VMEM((3, nline, 128), F32),
                pltpu.VMEM((3, nplane, nline, 128), F32),
                pltpu.SemaphoreType.DMA((9,)),
                pltpu.SemaphoreType.DMA((4, 27)),
                pltpu.SemaphoreType.DMA((4, 27)),
                pltpu.SemaphoreType.DMA((3, nline)),
                pltpu.SemaphoreType.DMA((3, nline)),
                pltpu.SemaphoreType.DMA((3, nplane)),
                pltpu.SemaphoreType.DMA((3, nplane)),
            ],
            compiler_params=pltpu.CompilerParams(
                collective_id=0, has_side_effects=True, vmem_limit_bytes=67_000_000
            ),
            name="schwarz_cg",
        )(
            right_side.reshape(192, cz),
            phase_labels,
            phase_moduli,
            coarse_nodes.reshape(64, cz),
            coarse_inverse,
            *consts,
        )
        return sol.reshape(right_side.shape), res.reshape(right_side.shape)

    spec = P(None, "gx", "gy", "gz")
    cells = P("gx", "gy", "gz")
    return jax.shard_map(
        body,
        mesh=mesh,
        in_specs=(spec, cells, P(), cells, P(("gx", "gy", "gz"), None)),
        out_specs=(spec, spec),
        check_vma=False,
    )
```

```python
import functools

import jax
import jax.numpy as jnp
import numpy as np
from jax import lax
from jax.experimental import pallas as pl
from jax.experimental.pallas import tpu as pltpu
from jax.sharding import PartitionSpec as P

MESH = pl.DeviceIdType.MESH
HIGH = lax.Precision.HIGHEST
F32 = jnp.float32

RELAX = 0.6
UNROLL = 4
SWEEPS = 4
SIDE = 8
STRIDE = 11
LEAD = 8
ZH = 2
NODES = 6
NEIGHBOURS = [(x, y, z) for x in (-1, 0, 1) for y in (-1, 0, 1) for z in (-1, 0, 1) if (x, y, z) != (0, 0, 0)]
MODES = 36


def bond(d):
    return d[0] * d[0] + d[1] * d[1] + d[2] * d[2]


def coef(m, k, d):
    n = bond(d)
    if n == 0:
        return 0.0
    return (1.0 / n if m == k else 0.0) + 0.5 * d[m] * d[k] / (n * n)


def plan(cz):
    rows = -(-(cz + 3) // 8) * 8
    srows = -(-(cz // 2 + 2) // 8) * 8
    total = -(-(3 * rows + srows) // 80) * 80
    return rows, srows, total


def tables(cz):
    rows, srows, total = plan(cz)
    place = np.zeros((64, 128), np.float32)
    for i in range(SIDE):
        for j in range(SIDE):
            place[i * SIDE + j, STRIDE * (i + 1) + j + 1] = 1.0
    spot = {-1: 0, 0: 1, 1: 2, 2: 3, 3: 8, 4: 9}
    place_blocks = np.zeros((16, 128), np.float32)
    for i in range(4):
        for j in range(4):
            place_blocks[i * 4 + j, STRIDE * spot[i] + spot[j]] = 1.0

    def lane_of(x, y):
        return STRIDE * spot[x // 2] + spot[y // 2]

    pairs = ((0, 0), (1, 1), (2, 2), (0, 1), (0, 2), (1, 2))
    mix = np.zeros((128, 11 * 128))
    for x in range(-1, 9):
        for y in range(-1, 9):
            out = STRIDE * (x + 1) + y + 1
            mix[lane_of(x, y), out] += 1.0
            for at, (m, k) in enumerate(pairs):
                for a in (-1, 0, 1):
                    for b in (-1, 0, 1):
                        src = lane_of(x + a, y + b)
                        if at < 4:
                            mix[src, 128 * (1 + at) + out] += 72.0 * coef(m, k, (a, b, 0))
                        mix[src, 128 * (5 + at) + out] += 72.0 * coef(m, k, (a, b, 1))
    mix = np.round(mix)
    lane = np.arange(128)
    ints = np.zeros((32, 128), np.int32)
    ints[0:8] = np.where(lane < 110, lane // STRIDE, 99)
    ints[8:16] = np.where(lane < 110, lane % STRIDE, 99)
    ints[16:24] = np.where(lane < 126, lane // 21, 99)
    ints[24:32] = np.where(lane < 126, lane % 21 % STRIDE, 99)
    floats = np.zeros((16, 128), np.float32)
    floats[0:8] = (2.0 * (lane // STRIDE - 1) + 1.0) / SIDE - 1.0
    floats[8:16] = (2.0 * (lane % STRIDE - 1) + 1.0) / SIDE - 1.0
    half = lambda a: jnp.asarray(a, jnp.bfloat16)
    return half(place), half(place_blocks), half(mix), jnp.asarray(ints), jnp.asarray(floats)


WHOLE = sum(coef(0, 0, (a, b, c)) for a in (-1, 0, 1) for b in (-1, 0, 1) for c in (-1, 0, 1))


def thirds(x):
    high = x.astype(jnp.bfloat16)
    rest = x - high.astype(F32)
    middle = rest.astype(jnp.bfloat16)
    return high, middle, (rest - middle.astype(F32)).astype(jnp.bfloat16)


def turn(x, shift):
    shift = shift % 128
    return x if shift == 0 else pltpu.roll(x, shift, 1)


def add_all(items):
    items = list(items)
    while len(items) > 1:
        items = [
            items[i] + items[i + 1] if i + 1 < len(items) else items[i] for i in range(0, len(items), 2)
        ]
    return items[0]


def kernel(
    sizes,
    cz,
    rhs_hbm,
    labels_hbm,
    moduli,
    nodes_hbm,
    inverse,
    place_hbm,
    place_blocks_hbm,
    mix_hbm,
    ints_hbm,
    floats_hbm,
    sol_out,
    res_out,
    mat,
    rhs,
    labels,
    nodes_in,
    place,
    place_blocks,
    mix,
    ints,
    floats,
    mixed,
    field,
    zfield,
    qfield,
    rfield,
    pfield,
    set_a,
    set_b,
    dmat,
    stiff,
    cdiag,
    node,
    gridm,
    stage,
    rowm,
    ybuf,
    cvec,
    zsend,
    zrecv,
    ysend,
    yrecv,
    xsend,
    xrecv,
    csend,
    crecv,
    rsend,
    rrecv,
    zsum,
    outs,
    gmsg,
    g1,
    g1c,
    g2,
    load_sem,
    halo_ss,
    halo_rs,
    g1_ss,
    g1_rs,
    g2_ss,
    g2_rs,
):
    ngx, ngy, ngz = sizes
    rows, srows, total = plan(cz)
    tiles = rows // 8
    sbase = LEAD + 3 * rows
    gx, gy, gz = lax.axis_index("gx"), lax.axis_index("gy"), lax.axis_index("gz")
    zhi, yhi = lax.rem(gx, ZH), lax.div(gx, ZH)
    nline = ZH * ngy
    nplane = (ngx // ZH) * ngz
    slot1 = zhi * ngy + gy
    slot2 = yhi * ngz + gz

    def line_peer(step):
        other = lax.rem(slot1 + step, nline)
        return (yhi * ZH + lax.div(other, ngy), lax.rem(other, ngy), gz)

    def plane_peer(step):
        other = lax.rem(slot2 + step, nplane)
        return (lax.div(other, ngz) * ZH + zhi, gy, lax.rem(other, ngz))

    sides = {}
    for d in NEIGHBOURS:
        has = None
        for way, at, count in zip(d, (gx, gy, gz), sizes):
            if way != 0:
                one = at > 0 if way < 0 else at < count - 1
                has = one if has is None else has & one
        sides[d] = (has, (gx + d[0], gy + d[1], gz + d[2]))

    loads = [
        pltpu.make_async_copy(src, dst, load_sem.at[at])
        for at, (src, dst) in enumerate(
            (
                (rhs_hbm, rhs),
                (nodes_hbm, nodes_in),
                (labels_hbm, labels),
                (place_hbm, place),
                (place_blocks_hbm, place_blocks),
                (ints_hbm, ints),
                (floats_hbm, floats),
                (mix_hbm, mix),
                (inverse, mat),
            )
        )
    ]
    for load in loads:
        load.start()
    mat_copy, mix_copy = loads[-1], loads[-2]

    barrier = pltpu.get_barrier_semaphore()
    for has, device in [sides[d] for d in sorted(NEIGHBOURS, key=lambda d: -abs(d[0]))]:

        @pl.when(has)
        def _(device=device):
            pl.semaphore_signal(barrier, inc=1, device_id=device, device_id_type=MESH)

    for step in range(1, nline):
        pl.semaphore_signal(barrier, inc=1, device_id=line_peer(step), device_id_type=MESH)
    for step in range(1, nplane):
        pl.semaphore_signal(barrier, inc=1, device_id=plane_peer(step), device_id_type=MESH)


    lane = lax.broadcasted_iota(jnp.int32, (8, 128), 1)
    sub = lax.broadcasted_iota(jnp.int32, (8, 128), 0)

    def base_of(k, i):
        return tile_at(LEAD + k * rows, i)

    def tile_at(first, i):
        return first + 8 * i if isinstance(i, int) else pl.multiple_of(first + 8 * i, 8)

    def repeat(count, one, unroll):
        whole = count // unroll if count > 2 * unroll else 0

        def some(n, carry):
            for j in range(unroll):
                one(n * unroll + j)
            return carry

        if whole:
            lax.fori_loop(0, whole, some, 0)
        for i in range(whole * unroll, count):
            one(i)

    def each_tile(one, unroll=4):
        whole = tiles // unroll

        def some(n, carry):
            for j in range(unroll):
                one(n * unroll + j)
            return carry

        lax.fori_loop(0, whole, some, 0)
        for i in range(whole * unroll, tiles):
            one(i)

    def xi_z(i):
        along = (sub + (8 * i - 1)).astype(F32)
        return (2.0 * along + 1.0) / cz - 1.0

    def deep(axis, width):
        if width == 1:
            return total // 10
        return 8 * -(-3 * rows // (40 if axis == 1 else 48))

    def edge_chunks(width):
        return 6 if width == 1 else 5

    def edge_deep(width):
        return 8 * -(-deep(2, width) // (8 * edge_chunks(width)))

    def inbox(which, d):
        x, y, z = d
        width = 1 + which % 2
        if z != 0:
            if x == 0:
                return zrecv.at[which, 3 * (z > 0) + y + 1]
            at = 6 * (x > 0) + 3 * (z > 0) + y + 1
            return rrecv.at[which, at : at + 1]
        if x != 0 and y != 0:
            return crecv.at[which, 2 * (x > 0) + (y > 0), 0 : edge_deep(width)]
        if y != 0:
            return yrecv.at[which, int(y > 0), 0 : deep(1, width)]
        return xrecv.at[which, int(x > 0), 0 : deep(2, width)]

    def outbox(which, d):
        x, y, z = d
        width = 1 + which % 2
        if z != 0:
            if x == 0:
                return zsend.at[which, int(z > 0)]
            at = 2 * (x > 0) + (z > 0)
            return rsend.at[which, at, 0:1]
        if x != 0 and y != 0:
            return csend.at[which, 2 * (x > 0) + (y > 0), 0 : edge_deep(width)]
        if y != 0:
            return ysend.at[which, int(y > 0), 0 : deep(1, width)]
        return xsend.at[which, int(x > 0), 0 : deep(2, width)]

    for f in range(6):
        dmat[rows * f + cz + 2 : rows * (f + 1), :] = jnp.zeros((rows - cz - 2, 128), F32)
    stiff[cz + 2 : rows, :] = jnp.zeros((rows - cz - 2, 128), F32)
    for ref in (field, rfield):
        ref[...] = jnp.zeros(ref.shape, F32)
    zfield[sbase:, :] = jnp.zeros((LEAD + total - sbase, 128), F32)
    for ref in set_a + set_b:
        ref[0:LEAD, :] = jnp.zeros((LEAD, 128), F32)
        ref[LEAD + 3 * rows : LEAD + 3 * rows + 8, :] = jnp.zeros((8, 128), F32)
    node[...] = jnp.zeros(node.shape, F32)
    rowm[...] = jnp.zeros(rowm.shape, F32)
    for ref in (zsend, xsend):
        ref[...] = jnp.zeros(ref.shape, F32)
    for t in range(4):
        for e in range(2):
            end = deep(2, 1 + t % 2)
            xrecv[t, e, end:, :] = jnp.zeros((xrecv.shape[2] - end, 128), F32)
    cvec[...] = jnp.zeros(cvec.shape, F32)
    stage[...] = jnp.zeros(stage.shape, F32)
    for d in NEIGHBOURS:

        @pl.when(jnp.logical_not(sides[d][0]))
        def _(d=d):
            for t in range(4):
                ref = inbox(t, d)
                ref[...] = jnp.zeros(ref.shape, F32)

    for load in loads[:-2]:
        load.wait()
    lane_x, lane_y, lane_c = ints[0:8, :], ints[8:16, :], ints[16:24, :]
    lane_e = ints[24:32, :]
    xi_x, xi_y = floats[0:8, :], floats[8:16, :]

    def dot(a, b, dims):
        return lax.dot_general(a, b, ((dims[:1], dims[1:]), ((), ())), preferred_element_type=F32)

    def spread_in(x):
        return add_all([dot(part, place[...], (0, 0)) for part in thirds(x)[::-1]])

    def gather_out(select, x):
        return add_all([dot(select, part, (1, 1)) for part in thirds(x)[::-1]])

    for k in range(3):
        piece = spread_in(rhs[64 * k : 64 * k + 64, :])
        first = LEAD + k * rows + 1
        field[first : first + cz, :] = piece
        rfield[first : first + cz, :] = piece
    node[1 : 1 + cz, :] = dot((nodes_in[...].astype(F32) + 1.0).astype(jnp.bfloat16), place[...], (0, 0))
    for i in range(4):
        stage[4 * i : 4 * i + 4, :] = labels[i].astype(F32) + 1.0
    phases = dot(stage[...].astype(jnp.bfloat16), place_blocks[...], (0, 0))
    blocks = jnp.zeros(phases.shape, F32)
    for phase in range(moduli.shape[0]):
        blocks = jnp.where(phases == float(phase + 1), moduli[phase], blocks)
    field[sbase + 1 : sbase + 1 + cz // 2, :] = blocks

    bad_lane = (
        ((gx == 0) & (lane_x == 0))
        | ((gx == ngx - 1) & (lane_x == 9))
        | ((gy == 0) & (lane_y == 0))
        | ((gy == ngy - 1) & (lane_y == 9))
        | (lane_x > 9)
        | (lane_y > 9)
    )
    low = jnp.where(gz == 0, 1, 0)
    high = jnp.where(gz == ngz - 1, cz + 1, cz + 2)

    def grid_tile(i):
        r = sub + 8 * i
        gridm[pl.ds(tile_at(0, i), 8), :] = jnp.where(bad_lane | (r < low) | (r >= high), 0.0, 1.0)

    each_tile(grid_tile)

    def number(d):
        return 9 * (d[0] + 1) + 3 * (d[1] + 1) + d[2] + 1

    def opposite(d):
        return (-d[0], -d[1], -d[2])

    def halo(which, d):
        return pltpu.make_async_remote_copy(
            src_ref=outbox(which, d),
            dst_ref=inbox(which, opposite(d)),
            send_sem=halo_ss.at[which, number(d)],
            recv_sem=halo_rs.at[which, number(opposite(d))],
            device_id=sides[d][1],
            device_id_type=MESH,
        )

    def send(which, group):
        for d in group:

            @pl.when(sides[d][0])
            def _(d=d):
                halo(which, d).start()

    def arrive(which, group):
        for d in group:

            @pl.when(sides[d][0])
            def _(d=d):
                pltpu.make_async_remote_copy(
                    src_ref=outbox(which, d),
                    dst_ref=inbox(which, d),
                    send_sem=halo_ss.at[which, number(d)],
                    recv_sem=halo_rs.at[which, number(d)],
                    device_id=sides[d][1],
                    device_id_type=MESH,
                ).wait_recv()

    def left(which):
        for d in NEIGHBOURS:

            @pl.when(sides[d][0])
            def _(d=d):
                halo(which, d).wait_send()

    def z_rows(width):
        if width == 1:
            got = [(LEAD + k * rows, cz, k) for k in range(3)] + [(sbase, cz // 2, 3)]
            return [(r + n, r + 1, r, r + n + 1, at) for r, n, at in got]
        out = []
        for k in range(3):
            for layer in range(2):
                r = LEAD + k * rows + layer
                out.append((r + cz, r, r, r + cz, 2 * k + layer))
        return out

    def groups(axis, width, along=None):
        if axis == 1:
            along = lane_y if along is None else along
            if width == 1:
                return 10, [along == k for k in range(10)]
            return 5, [(along == 2 * k) | (along == 2 * k + 1) for k in range(5)]
        if width == 1:
            return 10, [lane_x == k for k in range(10)]
        return 6, [lane_c == k for k in range(6)]

    def move(axis, width, along=None):
        if axis == 1:
            along = lane_y if along is None else along
            if width == 1:
                return 1, (1, 8), (0, 9), (along == 0, along == 9)
            return 2, (0, 8), (0, 8), (along < 2, (along == 8) | (along == 9))
        if width == 1:
            return STRIDE, (STRIDE, 8 * STRIDE), (0, 9 * STRIDE), (lane_x == 0, lane_x == 9)
        return 21, (0, 88), (0, 88), (lane < 21, (lane >= 88) & (lane < 109))

    def pack(src, first, dsts, axis, width, chunks, depth, along=None):
        gap, froms, _, _ = move(axis, width)
        masks = groups(axis, width, along)[1]

        def one(t):
            low, high = jnp.zeros((8, 128), F32), jnp.zeros((8, 128), F32)
            for k in range(chunks):
                tile = src[pl.ds(tile_at(first + 8 * k * depth, t), 8), :]
                low = jnp.where(masks[k], turn(tile, gap * k - froms[0]), low)
                high = jnp.where(masks[k], turn(tile, gap * k - froms[1]), high)
            at = pl.ds(tile_at(0, t), 8)
            dsts[0][at, :] = low
            dsts[1][at, :] = high

        repeat(depth, one, 6)

    def unpack(dst, first, srcs, axis, width, chunks, depth, along=None):
        gap, _, tos, ends = move(axis, width, along)

        def one(t):
            at = pl.ds(tile_at(0, t), 8)
            low, high = srcs[0][at, :], srcs[1][at, :]
            for k in range(chunks):
                part = pl.ds(tile_at(first + 8 * k * depth, t), 8)
                tile = dst[part, :]
                tile = tile + jnp.where(ends[0], turn(low, tos[0] - gap * k), 0.0)
                tile = tile + jnp.where(ends[1], turn(high, tos[1] - gap * k), 0.0)
                dst[part, :] = tile

        repeat(depth, one, 6)

    far_rows = [(x, y, z) for x in (-1, 1) for z in (-1, 1) for y in (-1, 0, 1)]
    near_layers = [(0, y, z) for z in (-1, 1) for y in (-1, 0, 1)]
    edges = [(x, y, 0) for x in (-1, 1) for y in (-1, 1)]

    def exchange(ref, which, width, early=None, late=None):
        chunks = [None, groups(1, width)[0], groups(2, width)[0]]
        depth = [None, deep(1, width) // 8, deep(2, width) // 8]
        edge, edge_parts = edge_deep(width) // 8, edge_chunks(width)
        along = lane_y if width == 1 else lane_e
        gap, froms, tos, ends = move(2, width)
        layers = 4 if width == 1 else 6
        pack(ref, LEAD, [xsend.at[which, e] for e in range(2)], 2, width, chunks[2], depth[2])
        send(which, [(-1, 0, 0), (1, 0, 0)])
        for x in range(2):
            pack(
                xsend.at[which, x],
                0,
                [csend.at[which, 2 * x + y] for y in range(2)],
                1,
                width,
                edge_parts,
                edge,
                along,
            )
        send(which, edges)
        for up_from, down_from, _, _, at in z_rows(width):
            zsend[which, 0, at : at + 1, :] = ref[down_from : down_from + 1, :]
            zsend[which, 1, at : at + 1, :] = ref[up_from : up_from + 1, :]
        mine = [(sub == r) & (lane >= gap * r) & (lane < gap * r + gap) for r in range(layers)]
        for z in range(2):
            tile = zsend[which, z]
            for x in range(2):
                row = jnp.zeros((8, 128), F32)
                for r in range(layers):
                    row = jnp.where(mine[r], turn(tile, gap * r - froms[x]), row)
                rsend[which, 2 * x + z, 0:1, :] = jnp.sum(row, axis=0, keepdims=True)
        send(which, far_rows)
        pack(ref, LEAD, [ysend.at[which, e] for e in range(2)], 1, width, chunks[1], depth[1])
        send(which, [(0, -1, 0), (0, 1, 0)])
        send(which, near_layers)
        if early is not None:
            early()
        arrive(which, [(0, -1, 0), (0, 1, 0)])
        unpack(ref, LEAD, [yrecv.at[which, e] for e in range(2)], 1, width, chunks[1], depth[1])
        if late is not None:
            late()
        arrive(which, near_layers)
        arrive(which, far_rows)
        yends = move(1, width)[3]
        for z in range(2):
            tiles_y = []
            for y in range(3):
                tile = zrecv[which, 3 * z + y]
                for x in range(2):
                    at = 6 * x + 3 * z + y
                    row = jnp.broadcast_to(rrecv[which, at : at + 1, :], (8, 128))
                    for r in range(layers):
                        here = (sub == r) & ends[x]
                        tile = tile + jnp.where(here, turn(row, tos[x] - gap * r), 0.0)
                tiles_y.append(tile)
            zsum[z] = (
                tiles_y[1]
                + jnp.where(yends[0], turn(tiles_y[0], -8), 0.0)
                + jnp.where(yends[1], turn(tiles_y[2], 8), 0.0)
            )
        for _, _, low_to, high_to, at in z_rows(width):
            ref[low_to : low_to + 1, :] += zsum[0, at : at + 1, :]
            ref[high_to : high_to + 1, :] += zsum[1, at : at + 1, :]
        arrive(which, [(-1, 0, 0), (1, 0, 0)])
        arrive(which, edges)
        for x in range(2):
            unpack(
                xrecv.at[which, x],
                0,
                [crecv.at[which, 2 * x + y] for y in range(2)],
                1,
                width,
                edge_parts,
                edge,
                along,
            )
        unpack(ref, LEAD, [xrecv.at[which, e] for e in range(2)], 2, width, chunks[2], depth[2])

    def line_copy(which, step):
        return pltpu.make_async_remote_copy(
            src_ref=gmsg.at[which, pl.ds(0, 1)],
            dst_ref=g1.at[which, pl.ds(slot1, 1)],
            send_sem=g1_ss.at[which, step],
            recv_sem=g1_rs.at[which, slot1],
            device_id=line_peer(step),
            device_id_type=MESH,
        )

    def line_start(which, message):
        gmsg[which] = message
        g1[which, pl.ds(slot1, 1), :] = message[0:1, :]
        for step in range(1, nline):
            line_copy(which, step).start()

    def line_arrive(which):
        for step in range(1, nline):
            other = lax.rem(slot1 + step, nline)
            pltpu.make_async_remote_copy(
                src_ref=gmsg.at[which, pl.ds(0, 1)],
                dst_ref=g1.at[which, pl.ds(other, 1)],
                send_sem=g1_ss.at[which, step],
                recv_sem=g1_rs.at[which, other],
                device_id=line_peer(step),
                device_id_type=MESH,
            ).wait_recv()

    def plane_rows(which):
        return nline if which < 2 else 8

    def plane_copy(which, step):
        return pltpu.make_async_remote_copy(
            src_ref=g1c.at[which, 0 : plane_rows(which)],
            dst_ref=g2.at[which, slot2, 0 : plane_rows(which)],
            send_sem=g2_ss.at[which, step],
            recv_sem=g2_rs.at[which, slot2],
            device_id=plane_peer(step),
            device_id_type=MESH,
        )

    def plane_start(which, block):
        g1c[which] = block
        g2[which, pl.ds(slot2, 1)] = block[None]
        for step in range(1, nplane):
            plane_copy(which, step).start()

    def plane_arrive(which):
        for step in range(1, nplane):
            other = lax.rem(slot2 + step, nplane)
            pltpu.make_async_remote_copy(
                src_ref=g1c.at[which, 0 : plane_rows(which)],
                dst_ref=g2.at[which, other, 0 : plane_rows(which)],
                send_sem=g2_ss.at[which, step],
                recv_sem=g2_rs.at[which, other],
                device_id=plane_peer(step),
                device_id_type=MESH,
            ).wait_recv()

    def moments(ref):
        def one(i, acc):
            r = [ref[pl.ds(base_of(k, i), 8), :] for k in range(3)]
            own = node[pl.ds(tile_at(0, i), 8), :]
            z = xi_z(i)
            parts = r + [xi_y * r[2] - z * r[1], z * r[0] - xi_x * r[2], xi_x * r[1] - xi_y * r[0]]
            out = []
            for g in range(NODES):
                here = own == float(g + 1)
                for m in range(6):
                    out.append(acc[6 * g + m] + jnp.where(here, parts[m], 0.0))
            return tuple(out)

        acc = lax.fori_loop(0, tiles, one, tuple(jnp.zeros((8, 128), F32) for _ in range(MODES)))
        for at in range(MODES):
            rowm[at : at + 1, :] = jnp.sum(acc[at], axis=0, keepdims=True)

    def row_to_lanes():
        return gather_out(jnp.ones((8, 128), jnp.bfloat16), rowm[...])

    turned = lax.rem((gy * ngz + gz) * MODES, 128)

    def own_range(c):
        begin = (sub * ngz + c) * MODES - 128 * sub
        ahead = begin < 128
        first = (lane >= begin) & (lane < begin + MODES)
        second = (lane + 128 >= begin) & (lane + 128 < begin + MODES)
        return first, second

    def coarse_solve(which):
        ranges = [own_range(c) for c in range(ngz)]
        acc = [jnp.zeros((8, 128), F32) for _ in range(5)]
        for y in range(ngx // ZH):
            for h in range(ZH):
                a = y * ZH + h
                got = [g2[which, y * ngz + c, 8 * h : 8 * h + 8, :] for c in range(ngz)]
                main = add_all([jnp.where(ranges[c][0], got[c], 0.0) for c in range(ngz)])
                nxt = add_all([jnp.where(ranges[c][1], got[c], 0.0) for c in range(ngz)])
                cvec[16 * a + 8 : 16 * a + 9, :] = jnp.zeros((1, 128), F32)
                cvec[16 * a : 16 * a + 8, :] = main
                cvec[16 * a + 1 : 16 * a + 9, :] += nxt
        for a in range(ngx):
            for j in range(9):
                row = jnp.broadcast_to(cvec[16 * a + j : 16 * a + j + 1, :], (8, 128))
                col = 128 * (9 * a + j)
                for t in range(4):
                    acc[t] = acc[t] + mat[8 * t : 8 * t + 8, col : col + 128] * row
                acc[4] = acc[4] + jnp.concatenate([mat[32:36, col : col + 128]] * 2, axis=0) * row
        for t in range(5):
            ybuf[8 * t : 8 * t + 8, :] = jnp.broadcast_to(jnp.sum(acc[t], axis=1, keepdims=True), (8, 128))

    def lane_sum(which, at):
        parts = []
        for c in range(ngz):
            pos = lax.rem((sub * ngz + c) * MODES + at, 128)
            here = lane == pos
            for y in range(ngx // ZH):
                for h in range(ZH):
                    parts.append(jnp.where(here, g2[which, y * ngz + c, 8 * h : 8 * h + 8, :], 0.0))
        whole = jnp.sum(add_all(parts), axis=0, keepdims=True)
        return jnp.sum(whole, axis=1, keepdims=True)

    def with_coarse(src, dst):
        def one(i):
            own = node[pl.ds(tile_at(0, i), 8), :]
            grid = gridm[pl.ds(tile_at(0, i), 8), :]
            z = xi_z(i)
            modes = [jnp.zeros((8, 128), F32) for _ in range(6)]
            for g in range(NODES):
                here = own == float(g + 1)
                for m in range(6):
                    at = 6 * g + m
                    modes[m] = jnp.where(here, jnp.broadcast_to(ybuf[at : at + 1, :], (8, 128)), modes[m])
            t, w = modes[:3], modes[3:]
            add = [
                t[0] + (w[1] * z - w[2] * xi_y),
                t[1] + (w[2] * xi_x - w[0] * z),
                t[2] + (w[0] * xi_y - w[1] * xi_x),
            ]
            for k in range(3):
                at = pl.ds(base_of(k, i), 8)
                dst[at, :] = src[at, :] * grid + add[k]

        each_tile(one)

    def spread_tile(i, values, bufs):
        vf, wf, syv, dyv, syw, dyw = bufs
        s = stiff[pl.ds(tile_at(0, i), 8), :]
        for k in range(3):
            at = pl.ds(base_of(k, i), 8)
            v = values[k]
            w = s * v
            vf[at, :] = v
            wf[at, :] = w
            for x, sy, dy in ((v, syv, dyv), (w, syw, dyw)):
                ahead, behind = turn(x, -1), turn(x, 1)
                sy[at, :] = ahead + behind
                dy[at, :] = ahead - behind

    def spread(ref):
        each_tile(lambda i: spread_tile(i, [ref[pl.ds(base_of(k, i), 8), :] for k in range(3)], set_a), 8)

    def couple(u_ref, sy_ref, dy_ref, i):
        def at(ref, k, dz):
            return ref[pl.ds(base_of(k, i) + dz, 8), :]

        up = [at(u_ref, k, 1) for k in range(3)]
        um = [at(u_ref, k, -1) for k in range(3)]
        u = [at(u_ref, k, 0) for k in range(3)]
        s = [up[k] + um[k] for k in range(3)]
        yp = [at(sy_ref, k, 1) for k in range(3)]
        ym = [at(sy_ref, k, -1) for k in range(3)]
        sy = [at(sy_ref, k, 0) for k in range(3)]
        sys = [yp[k] + ym[k] for k in range(3)]
        t_x, t_z = up[0] - um[0], up[2] - um[2]
        ty_x, ty_z = yp[0] - ym[0], yp[2] - ym[2]
        dp = [at(dy_ref, k, 1) for k in range(3)]
        dm = [at(dy_ref, k, -1) for k in range(3)]
        dys_x, dys_y = dp[0] + dm[0], dp[1] + dm[1]
        dyt_y, dyt_z = dp[1] - dm[1], dp[2] - dm[2]
        dy_x, dy_y = at(dy_ref, 0, 0), at(dy_ref, 1, 0)
        e, th, c7 = 0.125, 1.0 / 18.0, 7.0 / 18.0
        still = [
            sy[0] + s[0] + 0.5 * sys[0],
            1.5 * sy[1] + s[1] + 0.625 * sys[1] + e * dyt_z,
            sy[2] + 1.5 * s[2] + 0.625 * sys[2] + e * dyt_y,
        ]
        even = [
            1.5 * u[0] + 0.625 * (sy[0] + s[0]) + c7 * sys[0],
            u[1] + 0.625 * sy[1] + 0.5 * s[1] + c7 * sys[1] + th * dyt_z,
            u[2] + 0.5 * sy[2] + 0.625 * s[2] + c7 * sys[2] + th * dyt_y,
        ]
        odd = [
            e * (dy_y + t_z) + th * (dys_y + ty_z),
            e * dy_x + th * dys_x,
            e * t_x + th * ty_x,
        ]
        return [
            still[k] + (turn(even[k] + odd[k], -STRIDE) + turn(even[k] - odd[k], STRIDE)) for k in range(3)
        ], u

    def image_tile(i, bufs):
        vf, wf, syv, dyv, syw, dyw = bufs
        here = pl.ds(tile_at(0, i), 8)
        lv, v = couple(vf, syv, dyv, i)
        lw, _ = couple(wf, syw, dyw, i)
        s = stiff[here, :]
        d = [dmat[pl.ds(tile_at(rows * f, i), 8), :] for f in range(6)]
        full = ((0, 3, 4), (3, 1, 5), (4, 5, 2))
        out = []
        for m in range(3):
            diag = d[full[m][0]] * v[0] + d[full[m][1]] * v[1] + d[full[m][2]] * v[2]
            out.append(diag - 0.5 * (s * lv[m] + lw[m]))
        return out, v

    def local_solve(ref, out):
        def first(i):
            spread_tile(
                i,
                [cdiag[pl.ds(tile_at(rows * k, i), 8), :] * ref[pl.ds(base_of(k, i), 8), :] for k in range(3)],
                set_a,
            )

        each_tile(first, 8)
        bufs = [set_a, set_b]
        for sweep in range(SWEEPS - 1):

            def one(i, sweep=sweep):
                image, v = image_tile(i, bufs[sweep % 2])
                new = []
                for k in range(3):
                    c = cdiag[pl.ds(tile_at(rows * k, i), 8), :]
                    new.append(v[k] + c * (ref[pl.ds(base_of(k, i), 8), :] - image[k]))
                if sweep < SWEEPS - 2:
                    spread_tile(i, new, bufs[(sweep + 1) % 2])
                else:
                    for k in range(3):
                        out[pl.ds(base_of(k, i), 8), :] = new[k]

            each_tile(one, UNROLL)

    def setup_stiffness():
        mix_copy.wait()
        parts = thirds(field[sbase : sbase + srows, :])[::-1]
        for f in range(0, 11, 2):
            wide = 128 * min(2, 11 - f)
            got = add_all([dot(part, mix[:, 128 * f : 128 * f + wide], (1, 0)) for part in parts])
            for g in range(wide // 128):
                mixed[srows * (f + g) : srows * (f + g + 1), :] = got[:, 128 * g : 128 * g + 128]
        count = cz // 2 + 1

        def at(f, shift):
            return mixed[srows * f + shift : srows * f + shift + count, :]

        for parity in range(2):
            here = lambda f: at(f, parity)
            beyond = lambda f: at(f, 1 - parity)
            s_here = here(0)
            stiff[pl.ds(parity, count, stride=2), :] = s_here
            for m in range(6):
                if m < 4:
                    value = (here(1 + m) + here(5 + m) + beyond(5 + m)) * (1.0 / 144.0)
                    if m < 3:
                        value = value + (0.5 * WHOLE) * s_here
                else:
                    tilt = here(5 + m) - beyond(5 + m)
                    value = (tilt if parity == 1 else -tilt) * (1.0 / 144.0)
                dmat[pl.ds(rows * m + parity, count, stride=2), :] = value

        def one(i):
            for k in range(3):
                part = pl.ds(tile_at(rows * k, i), 8)
                d = dmat[part, :]
                live = d > 0.0
                cdiag[part, :] = jnp.where(live, RELAX / jnp.where(live, d, 1.0), 0.0)

        each_tile(one)

    def first_row():
        moments(field)
        return turn_by(row_to_lanes(), turned)

    greeters = nline - 1 + nplane - 1
    for has, _ in sides.values():
        greeters = greeters + jnp.where(has, 1, 0)
    pl.semaphore_wait(barrier, greeters)

    def forward(which):
        line_arrive(which)
        plane_start(which, g1[which])

    exchange(field, 0, 1, lambda: line_start(0, first_row()), lambda: forward(0))
    setup_stiffness()
    local_solve(field, pfield)
    mat_copy.wait()
    plane_arrive(0)
    coarse_solve(0)
    with_coarse(pfield, zfield)
    exchange(zfield, 1, 2)

    spread(zfield)

    def image_and_sums(dsts, first, second):
        def one(i, acc):
            image, v = image_tile(i, set_a)
            own = node[pl.ds(tile_at(0, i), 8), :] > 0.0
            acc = list(acc)
            for k in range(3):
                at = pl.ds(base_of(k, i), 8)
                mine = jnp.where(own, image[k], 0.0)
                for dst in dsts:
                    dst[at, :] = mine
                acc[0] = acc[0] + first[at, :] * v[k]
                acc[1] = acc[1] + v[k] * mine
                if second is not None:
                    acc[2] = acc[2] + second[at, :] * v[k]
            return tuple(acc)

        count = 2 if second is None else 3
        acc = tuple(jnp.zeros((8, 128), F32) for _ in range(count))
        acc = lax.fori_loop(0, tiles // 2, lambda n, acc: one(2 * n + 1, one(2 * n, acc)), acc)
        for i in range(tiles // 2 * 2, tiles):
            acc = one(i, acc)
        return [jnp.sum(a, axis=0, keepdims=True) for a in acc]

    sums = image_and_sums((qfield, field), rfield, None)
    def second_row():
        moments(qfield)
        rowm[MODES : MODES + 1, :] = sums[0]
        rowm[MODES + 1 : MODES + 2, :] = sums[1]
        return turn_by(row_to_lanes(), turned)

    exchange(field, 2, 1, lambda: line_start(1, second_row()), lambda: forward(1))
    local_solve(field, pfield)
    plane_arrive(1)
    coarse_solve(1)
    rho0 = lane_sum(1, MODES)
    curve0 = lane_sum(1, MODES + 1)
    alpha0 = rho0 / curve0
    with_coarse(pfield, field)
    exchange(field, 3, 2)

    def renew(i):
        for k in range(3):
            at = pl.ds(base_of(k, i), 8)
            field[at, :] = zfield[at, :] - alpha0 * field[at, :]
            rfield[at, :] = rfield[at, :] - alpha0 * qfield[at, :]

    each_tile(renew)
    spread(field)

    sums = image_and_sums((pfield,), rfield, qfield)
    rowm[0:MODES, :] = jnp.zeros((MODES, 128), F32)
    for at in range(3):
        rowm[MODES + at : MODES + at + 1, :] = sums[at]
    line_start(2, row_to_lanes())
    for at, ref in enumerate((zfield, field, rfield, pfield, qfield)):
        for k in range(3):
            first = LEAD + k * rows + 1
            outs[192 * at + 64 * k : 192 * at + 64 * k + 64, :] = gather_out(place[...], ref[first : first + cz, :])
    line_arrive(2)
    plane_start(2, jnp.broadcast_to(jnp.sum(g1[2], axis=0, keepdims=True), (nline, 128)))
    plane_arrive(2)
    last = add_all([g2[2, p, 0:8, :] for p in range(nplane)])[0:1, :]
    rho1, zaz, zq = [
        jnp.sum(jnp.where(lane[0:1, :] == MODES + at, last, 0.0), axis=1, keepdims=True) for at in range(3)
    ]
    beta = rho1 / rho0
    alpha1 = rho1 / (zaz + 2.0 * beta * zq + beta * beta * curve0)

    for i in range(24):
        z0, z1, r1, q1, q0 = [outs[192 * at + 8 * i : 192 * at + 8 * i + 8, :] for at in range(5)]
        sol_out[8 * i : 8 * i + 8, :] = alpha0 * z0 + alpha1 * (z1 + beta * z0)
        res_out[8 * i : 8 * i + 8, :] = r1 - alpha1 * (q1 + beta * q0)

    for which in range(4):
        left(which)
    for which in range(3):
        for step in range(1, nline):
            line_copy(which, step).wait_send()
        for step in range(1, nplane):
            plane_copy(which, step).wait_send()


def turn_by(x, shift):
    return pltpu.roll(x, shift, 1)


def solution(mesh):
    sizes = (mesh.shape["gx"], mesh.shape["gy"], mesh.shape["gz"])
    nline = ZH * sizes[1]
    nplane = (sizes[0] // ZH) * sizes[2]

    def body(right_side, phase_labels, phase_moduli, coarse_nodes, coarse_inverse):
        cz = right_side.shape[3]
        rows, srows, total = plan(cz)
        tall = pltpu.VMEM((LEAD + total, 128), F32)
        ydeep = max(total // 10, 8 * -(-3 * rows // 40))
        cdeep = 16
        xdeep = max(total // 10, 8 * -(-3 * rows // 48))
        xdeep = max(xdeep, 5 * cdeep)
        vmem = pl.BlockSpec(memory_space=pltpu.VMEM)
        away = pl.BlockSpec(memory_space=pl.ANY)
        consts = tables(cz)
        sol, res = pl.pallas_call(
            functools.partial(kernel, sizes, cz),
            out_shape=(jax.ShapeDtypeStruct((192, cz), F32),) * 2,
            in_specs=[
                away,
                away,
                pl.BlockSpec(memory_space=pltpu.SMEM),
                away,
                away,
            ]
            + [away] * len(consts),
            out_specs=(vmem, vmem),
            scratch_shapes=[
                pltpu.VMEM(coarse_inverse.shape, F32),
                pltpu.VMEM((192, cz), F32),
                pltpu.VMEM(phase_labels.shape, jnp.int32),
                pltpu.VMEM((64, cz), jnp.int32),
            ]
            + [pltpu.VMEM(c.shape, c.dtype) for c in consts]
            + [
                pltpu.VMEM((11 * srows + 8, 128), F32),
                tall,
                tall,
                tall,
                tall,
                tall,
                (tall,) * 6,
                (tall,) * 6,
                pltpu.VMEM((6 * rows, 128), F32),
                pltpu.VMEM((rows, 128), F32),
                pltpu.VMEM((3 * rows, 128), F32),
                pltpu.VMEM((rows, 128), F32),
                pltpu.VMEM((rows, 128), F32),
                pltpu.VMEM((16, cz // 2), F32),
                pltpu.VMEM((128, 128), F32),
                pltpu.VMEM((40, 128), F32),
                pltpu.VMEM((16 * sizes[0], 128), F32),
                pltpu.VMEM((4, 2, 8, 128), F32),
                pltpu.VMEM((4, 6, 8, 128), F32),
                pltpu.VMEM((4, 2, ydeep, 128), F32),
                pltpu.VMEM((4, 2, ydeep, 128), F32),
                pltpu.VMEM((4, 2, xdeep, 128), F32),
                pltpu.VMEM((4, 2, xdeep, 128), F32),
                pltpu.VMEM((4, 4, cdeep, 128), F32),
                pltpu.VMEM((4, 4, cdeep, 128), F32),
                pltpu.VMEM((4, 4, 8, 128), F32),
                pltpu.VMEM((4, 16, 128), F32),
                pltpu.VMEM((2, 8, 128), F32),
                pltpu.VMEM((5 * 192, cz), F32),
                pltpu.VMEM((3, 8, 128), F32),
                pltpu.VMEM((3, nline, 128), F32),
                pltpu.VMEM((3, nline, 128), F32),
                pltpu.VMEM((3, nplane, nline, 128), F32),
                pltpu.SemaphoreType.DMA((9,)),
                pltpu.SemaphoreType.DMA((4, 27)),
                pltpu.SemaphoreType.DMA((4, 27)),
                pltpu.SemaphoreType.DMA((3, nline)),
                pltpu.SemaphoreType.DMA((3, nline)),
                pltpu.SemaphoreType.DMA((3, nplane)),
                pltpu.SemaphoreType.DMA((3, nplane)),
            ],
            compiler_params=pltpu.CompilerParams(
                collective_id=0, has_side_effects=True, vmem_limit_bytes=67_000_000
            ),
            name="schwarz_cg",
        )(
            right_side.reshape(192, cz),
            phase_labels,
            phase_moduli,
            coarse_nodes.reshape(64, cz),
            coarse_inverse,
            *consts,
        )
        return sol.reshape(right_side.shape), res.reshape(right_side.shape)

    spec = P(None, "gx", "gy", "gz")
    cells = P("gx", "gy", "gz")
    return jax.shard_map(
        body,
        mesh=mesh,
        in_specs=(spec, cells, P(), cells, P(("gx", "gy", "gz"), None)),
        out_specs=(spec, spec),
        check_vma=False,
    )
```
